128 devices in a mesh: lat: 8 (over x_lo, z), lon: 16 (over x_hi, y, core).
Axes of the slice: x: 4 (x_hi: 2, x_lo: 2; x = x_hi * 2 + x_lo), y: 4, z: 4, core: 2. Of those that a mesh axis runs over, the one named last changes fastest.
Arguments:
- features: bfloat16 [32, 1024, 2048], P(None, 'lat', 'lon'), may hold values from -6 to 6
- cotangent: bfloat16 [32, 1024, 2048], P(None, 'lat', 'lon'), may hold values from -6 to 6
- sea_mask: int32 [1024, 2048], P('lat', 'lon'), may hold values 0 or 1
- weights: bfloat16 [5, 32, 32], replicated, may hold values from -1 to 1
Outputs:
- feature_grad: bfloat16 [32, 1024, 2048], P(None, 'lat', 'lon')
- weight_grad: float32 [5, 32, 32], replicated
The draws below stay inside these ranges and needn't reach their ends.
Inputs may be any that keep to these rules, and one draw needn't show every extreme that they name: `sea_mask`: 1 marks a sea cell, 0 a land cell.
All inputs are finite; a program needn't handle non-finite values. No bound on the sum of `sea_mask` on one device may be relied on, other than what follows from the above.
Results may differ from the reference program's by a relative error of at most 0.0069.
Values sent between devices are 32-bit elements; how exact they have to be, the bound alone decides.
A program may use at most 128 MiB of HBM per device.

```python
import math
import jax
import jax.numpy as jnp

C = 32
K = 4
NLAT = 1024
NLON = 2048


def wave_field(key, lat_freq, lon_freq, spread):
    scale_key, phase_key = jax.random.split(key)
    amplitudes = jax.random.uniform(scale_key, (C, 1, 1), jnp.float32, 1.0 - spread, 1.0 + spread)
    phases = jax.random.uniform(phase_key, (C, 1, 1), jnp.float32, 0.0, 2.0 * math.pi)
    row_index = jnp.arange(NLAT, dtype=jnp.int32).reshape(1, NLAT, 1)
    column_index = jnp.arange(NLON, dtype=jnp.int32).reshape(1, 1, NLON)
    row_turns = (lat_freq * row_index % NLAT).astype(jnp.float32) / NLAT
    column_turns = (lon_freq * column_index % NLON).astype(jnp.float32) / NLON
    return amplitudes * jnp.sin(2.0 * math.pi * (row_turns + column_turns) + phases)


def draw_features(key, part):
    wave_key, noise_key = jax.random.split(jax.random.fold_in(key, 11))
    lat_freq = NLAT // 128 + 1
    lon_freq = NLON // 256 + 1
    smooth = 1.2 * wave_field(wave_key, lat_freq, lon_freq, 0.4)
    rough_part = 0.6 * jax.random.normal(noise_key, (C, NLAT, NLON), jnp.float32)
    return jnp.clip(smooth + rough_part, -6.0, 6.0).astype(jnp.bfloat16)


def draw_cotangent(key, part):
    wave_key, noise_key = jax.random.split(jax.random.fold_in(key, 23))
    lat_freq = NLAT // 128 + 1
    lon_freq = 2 * (NLON // 256 + 1)
    smooth = 2.5 * wave_field(wave_key, lat_freq, lon_freq, 0.4)
    rough_part = 0.5 * jax.random.normal(noise_key, (C, NLAT, NLON), jnp.float32)
    return jnp.clip(smooth + rough_part, -6.0, 6.0).astype(jnp.bfloat16)


def draw_weights(key, part):
    weight_key = jax.random.fold_in(key, 37)
    orders = jnp.arange(K + 1, dtype=jnp.float32) + 2.0
    total_square = float(sum(((order_k + 2) ** 2 for order_k in range(K + 1))))
    factor = orders * math.sqrt((K + 1) / total_square)
    deviation = factor.reshape(K + 1, 1, 1) / math.sqrt(C * (K + 1))
    baseline = jnp.clip(jax.random.normal(weight_key, (K + 1, C, C), jnp.float32), -4.0, 4.0)
    return (baseline * deviation).astype(jnp.bfloat16)


def with_ends(array, key, smallest, high):
    index_at = [jax.random.randint(jax.random.fold_in(key, axis), (), 0, length) for axis, length in enumerate(array.shape)]
    main_axis = array.shape.index(max(array.shape))
    next_to = index_at[:main_axis] + [(index_at[main_axis] + 1) % array.shape[main_axis]] + index_at[main_axis + 1:]
    return array.at[tuple(index_at)].set(smallest).at[tuple(next_to)].set(high)


def setup_inputs(seed: int = 0) -> dict:
    keys = jax.random.split(jax.random.key(seed), 5)
    features = draw_features(jax.random.fold_in(keys[4], 71), 0)
    cotangent = draw_cotangent(jax.random.fold_in(keys[4], 71), 0)
    sea_mask = with_ends((jax.random.randint(keys[2], (NLAT, NLON), 0, 5) < 4).astype(jnp.int32), jax.random.fold_in(keys[2], 1), 0, 1)
    weights = draw_weights(jax.random.fold_in(keys[4], 71), 0)
    return {"features": features, "cotangent": cotangent, "sea_mask": sea_mask, "weights": weights}


NEIGHBOURS = ((0, -1), (0, 1), (-1, 0), (1, 0), (-1, 1), (1, -1))

def neigh_sum(padded, outer_pad, inner_pad):
    row_count = padded.shape[-2] - 2 * (outer_pad - inner_pad)
    col_count = padded.shape[-1] - 2 * (outer_pad - inner_pad)
    base = outer_pad - inner_pad
    summed = None
    for step_row, step_col in NEIGHBOURS:
        shifted = padded[..., base + step_row:base + step_row + row_count, base + step_col:base + step_col + col_count]
        summed = shifted if summed is None else summed + shifted
    return summed

def surround(cells_in):
    wrapped = jnp.concatenate([cells_in[..., -1:], cells_in, cells_in[..., :1]], axis=-1)
    widths = [(0, 0)] * (cells_in.ndim - 2) + [(1, 1), (0, 0)]
    return jnp.pad(wrapped, widths)

def reference(features, cotangent, sea_mask, weights):
    sea_cells = sea_mask.astype(jnp.float32)
    degree = neigh_sum(surround(sea_cells), 1, 0)
    weighting = sea_cells / jnp.sqrt(jnp.maximum(degree, 1.0))
    weights_f = weights.astype(jnp.float32)

    def laplace(cells_in):
        return -weighting * neigh_sum(surround(weighting * cells_in), 1, 0)

    def series(initial, visitor, carried):
        carried = visitor(carried, 0, initial)
        previous = initial
        current = laplace(initial)
        carried = visitor(carried, 1, current)
        for index_k in range(2, K + 1):
            advanced = 2.0 * laplace(current) - previous
            carried = visitor(carried, index_k, advanced)
            previous, current = (current, advanced)
        return carried
    initial = sea_cells * features.astype(jnp.float32)

    def forward_visit(carried, index_k, term):
        rounded = term.astype(jnp.bfloat16).astype(jnp.float32)
        return carried + jnp.einsum('cd,cij->dij', weights_f[index_k], rounded)
    mixed = series(initial, forward_visit, jnp.zeros(features.shape, jnp.float32))
    activated = jnp.tanh(mixed)
    grad_mix = (cotangent.astype(jnp.float32) * (1.0 - activated * activated)).astype(jnp.bfloat16)
    grad_f = grad_mix.astype(jnp.float32)

    def weight_visit(carried, index_k, term):
        rounded = term.astype(jnp.bfloat16).astype(jnp.float32)
        return carried + (jnp.einsum('cij,dij->cd', rounded, grad_f),)
    weight_terms = jnp.stack(series(initial, weight_visit, ()))
    weight_grad = weight_terms * (1.0 / math.sqrt(NLAT * NLON))

    def project(index_k):
        return jnp.einsum('cd,dij->cij', weights_f[index_k], grad_f)
    upper_one = project(K)
    upper_two = jnp.zeros(features.shape, jnp.float32)
    for index_k in range(K - 1, 0, -1):
        fresh = project(index_k) + 2.0 * laplace(upper_one) - upper_two
        upper_two, upper_one = (upper_one, fresh)
    result = project(0) + laplace(upper_one) - upper_two
    feature_grad = (sea_cells * result).astype(jnp.bfloat16)
    return (feature_grad, weight_grad)
```

```python
import functools
import math

import jax
import jax.numpy as jnp
from jax import lax
from jax.experimental import pallas as pl
from jax.experimental.pallas import tpu as pltpu
from jax.sharding import PartitionSpec as P

K = 4
C = 32
B = 128
RG = 4
R = B // RG
H = 4
RE = R + 2 * H
CE = B + 16
CP = CE + 16
O = 16
F32 = jnp.float32
BF16 = jnp.bfloat16
NT = (((1,), (1,)), ((), ()))


def kernel(
    n_lat, n_lon,
    feat_hbm, cot_hbm, mask_hbm, w_hbm,
    out_hbm, wg_ref,
    feat_v, cot_v, mask_v, w_v, xf, cf, out_v,
    ya, yb, coef, scale, terms, gcat,
    mb, sm, vm, snat, wf, wb, eye, sel,
    pack, lrow, lcol, own, ar1, ar2,
    in_sem, out_sem, mask_send, mask_recv, halo_send, halo_recv,
    ar1_send, ar1_recv, ar2_send, ar2_recv,
):
    lat = lax.axis_index("lat")
    lon = lax.axis_index("lon")
    north, south = lax.rem(lat + n_lat - 1, n_lat), lax.rem(lat + 1, n_lat)
    west, east = lax.rem(lon + n_lon - 1, n_lon), lax.rem(lon + 1, n_lon)

    feat_in = pltpu.make_async_copy(feat_hbm, feat_v, in_sem.at[0])
    cot_in = pltpu.make_async_copy(cot_hbm, cot_v, in_sem.at[1])
    mask_in = pltpu.make_async_copy(mask_hbm, mask_v, in_sem.at[2])
    w_in = pltpu.make_async_copy(w_hbm, w_v, in_sem.at[3])
    mask_in.start()
    feat_in.start()
    w_in.start()
    cot_in.start()

    barrier = pltpu.get_barrier_semaphore()

    def greet(i, j):
        pl.semaphore_signal(
            barrier, inc=1, device_id=(i, j), device_id_type=pl.DeviceIdType.MESH
        )

    for i in (north, south):
        for j in (west, east):
            greet(i, j)

    def greet_lon(off, _):
        greet(lat, lax.rem(lon + off, n_lon))
        return 0

    def greet_lat(off, _):
        greet(lax.rem(lat + off, n_lat), lon)
        return 0

    lax.fori_loop(1, n_lon, greet_lon, 0)
    lax.fori_loop(1, n_lat, greet_lat, 0)

    row_i = lax.broadcasted_iota(jnp.int32, (B, B), 0)
    col_i = lax.broadcasted_iota(jnp.int32, (B, B), 1)
    eye[...] = (row_i == col_i).astype(F32).astype(BF16)
    sel_r = lax.broadcasted_iota(jnp.int32, (CE, 2 * B), 0)
    sel_c = lax.broadcasted_iota(jnp.int32, (CE, 2 * B), 1)
    inside = (sel_r >= 8) & (sel_r < 8 + B) & (sel_c == sel_r - 8)
    left = (sel_r < 8) & (sel_c == 2 * B - 8 + sel_r)
    right = (sel_r >= 8 + B) & (sel_c == sel_r - 8)
    sel[...] = (inside | left | right).astype(F32).astype(BF16)

    mask_in.wait()
    mb[1, 8 : 8 + B, :] = mask_v[...].astype(F32)
    pl.semaphore_wait(barrier, 4 + (n_lon - 1) + (n_lat - 1))

    def remote(src, dst, send, recv, i, j):
        return pltpu.make_async_remote_copy(
            src_ref=src, dst_ref=dst, send_sem=send, recv_sem=recv,
            device_id=(i, j), device_id_type=pl.DeviceIdType.MESH,
        )

    mid, top, bottom = pl.ds(8, B), pl.ds(8, 8), pl.ds(B, 8)
    above, below = pl.ds(0, 8), pl.ds(8 + B, 8)
    mask_plan = (
        (mid, 0, mid, lat, east),
        (mid, 2, mid, lat, west),
        (bottom, 1, above, south, lon),
        (top, 1, below, north, lon),
        (bottom, 0, above, south, east),
        (bottom, 2, above, south, west),
        (top, 0, below, north, east),
        (top, 2, below, north, west),
    )
    mask_copies = [
        remote(mb.at[1, src], mb.at[slot, dst], mask_send.at[n], mask_recv.at[n], i, j)
        for n, (src, slot, dst, i, j) in enumerate(mask_plan)
    ]
    for copy in mask_copies:
        copy.start()

    lane = lax.broadcasted_iota(jnp.int32, (B, B), 1)

    def halo_copies(phase, y):
        plan = (
            (pack.at[phase, 0], lrow.at[phase, 0, mid], south, lon),
            (pack.at[phase, 1], lrow.at[phase, 1, mid], north, lon),
            (pack.at[phase, 0, pl.ds(B - 8, 8)], lrow.at[phase, 0, above], south, east),
            (pack.at[phase, 0, pl.ds(0, 8)], lrow.at[phase, 0, below], south, west),
            (pack.at[phase, 1, pl.ds(B - 8, 8)], lrow.at[phase, 1, above], north, east),
            (pack.at[phase, 1, pl.ds(0, 8)], lrow.at[phase, 1, below], north, west),
            (y.at[pl.ds(H, R), pl.ds(O + B - 8, 8)], lcol.at[phase, 0], lat, east),
            (y.at[pl.ds(H, R), pl.ds(O, 8)], lcol.at[phase, 1], lat, west),
        )
        return [
            remote(src, dst, halo_send.at[phase, n], halo_recv.at[phase, n], i, j)
            for n, (src, dst, i, j) in enumerate(plan)
        ]

    def pack_rows(phase, y):
        last, first = None, None
        for i in range(H):
            a = pltpu.roll(y[H + R - H + i, O : O + B, :], (32 * i + 32) % 128, 1)
            b = pltpu.roll(y[H + i, O : O + B, :], (32 * i) % 128, 1)
            here = (lane >= 32 * i) & (lane < 32 * i + 32)
            last = a if last is None else jnp.where(here, a, last)
            first = b if first is None else jnp.where(here, b, first)
        pack[phase, 0] = last
        pack[phase, 1] = first

    feat_in.wait()

    def widen(src, dst):
        def body(c, _):
            dst[pl.ds(pl.multiple_of(c * B, B), B), :] = src[c].astype(F32)
            return 0

        lax.fori_loop(0, C, body, 0)

    def rows_of(flat, r):
        return jnp.concatenate(
            [flat[pl.ds(R * g + r, C, stride=B), :] for g in range(RG)], axis=0
        )

    widen(feat_v, xf)

    def turn(r):
        x = rows_of(xf, r).astype(BF16)
        yb[H + r, O : O + B, :] = lax.dot_general(
            eye[...], x, NT, preferred_element_type=F32
        )

    def turn_edge(i, _):
        turn(i + (R - 2 * H) * (i // H))
        return 0

    def turn_inner(i, _):
        turn(i)
        return 0

    lax.fori_loop(0, 2 * H, turn_edge, 0)
    first_halo = halo_copies(0, yb)
    pack_rows(0, yb)
    for copy in first_halo[:6]:
        copy.start()
    lax.fori_loop(H, R - H, turn_inner, 0)
    for copy in first_halo[6:]:
        copy.start()

    w_in.wait()
    block = (row_i // C) == (col_i // C)
    for k in range(K + 1):
        one = w_v[k].astype(F32)
        wide = jnp.concatenate([one] * RG, axis=1)
        full = jnp.where(block, jnp.concatenate([wide] * RG, axis=0), 0.0)
        wb[:, k * B : (k + 1) * B] = full.astype(BF16)
        wf[:, k * B : (k + 1) * B] = full.T.astype(BF16)

    for copy in mask_copies:
        copy.wait()
    north_ok = (lat > 0).astype(F32)
    south_ok = (lat < n_lat - 1).astype(F32)
    lane_e = lax.broadcasted_iota(jnp.int32, (CE, B), 1)
    row_e = lax.broadcasted_iota(jnp.int32, (CE, B), 0)
    ok = jnp.where(row_e < 8, north_ok, jnp.where(row_e >= 8 + B, south_ok, 1.0))
    sm[...] = jnp.zeros_like(sm)
    sm[0, 8 : 8 + CE, :] = mb[1] * ok
    sm[1, 8 : 8 + CE, :] = jnp.where(lane_e < 64, mb[2], mb[0]) * ok

    def ring(main, side, shift, edge):
        m, s = pltpu.roll(main, shift, 1), pltpu.roll(side, shift, 1)
        at = lane_e == edge
        return jnp.where(at, s, m), jnp.where(at, m, s)

    here = [sm[t, 8 : 8 + CE, :] for t in range(2)]
    up = [sm[t, 7 : 7 + CE, :] for t in range(2)]
    down = [sm[t, 9 : 9 + CE, :] for t in range(2)]
    from_left = ring(here[0] + down[0], here[1] + down[1], 1, 0)
    from_right = ring(here[0] + up[0], here[1] + up[1], B - 1, B - 1)
    for t in range(2):
        degree = from_left[t] + from_right[t] + up[t] + down[t]
        vm[:, t * B : (t + 1) * B] = here[t] * jnp.maximum(degree, 1.0)
        if t == 0:
            snat[...] = jnp.sqrt(jnp.maximum(degree, 1.0)[8 : 8 + B])

    def spread(r, _):
        rows = jnp.concatenate(
            [
                jnp.broadcast_to(vm[pl.ds(8 - H + R * g + r, 1), :], (C, 2 * B))
                for g in range(RG)
            ],
            axis=0,
        )
        v = lax.dot_general(sel[...], rows.astype(BF16), NT, preferred_element_type=F32)
        m = jnp.maximum(v, 1.0)
        rs = lax.rsqrt(m)
        coef[r] = jnp.where(v > 0.5, -2.0 * rs * rs, 0.0)
        scale[r] = m * rs
        return 0

    lax.fori_loop(0, RE, spread, 0)

    def assemble(phase, y, ok_north, ok_south):
        def sides(r, _):
            y[H + r, O - 8 : O, :] = lcol[phase, 0, r]
            y[H + r, O + B : O + B + 8, :] = lcol[phase, 1, r]
            return 0

        lax.fori_loop(0, R, sides, 0)
        for i in range(H):
            own_up = pltpu.roll(y[R + i, O - 8 : O + B + 8, :], 32, 1)
            far_up = pltpu.roll(lrow[phase, 0], (B - 32 * i) % B, 1) * ok_north
            y[i, O - 8 : O + B + 8, :] = jnp.where(lane_e < 32, far_up, own_up)
            own_down = pltpu.roll(y[H + i, O - 8 : O + B + 8, :], B - 32, 1)
            far_down = pltpu.roll(lrow[phase, 1], (96 - 32 * i) % B, 1) * ok_south
            y[H + R + i, O - 8 : O + B + 8, :] = jnp.where(
                lane_e >= 96, far_down, own_down
            )

    def keep(k, r, value):
        terms[pl.ds(pl.multiple_of(r * B, B), B), k * B : (k + 1) * B] = value.astype(BF16)

    def step(src, dst, k, scaled):
        reach = K - k
        first, count = (O - 8, CE) if reach else (O, B)
        skip = O - first

        def sums(r):
            mid_ = src[r, first : first + count, :]
            low = src[r, first - 1 : first - 1 + count, :]
            high = src[r, first + 1 : first + 1 + count, :]
            return mid_ + high, low + high, mid_ + low

        def advance(r, carried):
            e0, e1, f1 = carried
            e2, f2, h2 = sums(r + 1)
            a = coef[r, first - O + 8 : first - O + 8 + count, :]
            total = a * (e0 + f1 + h2)
            if k == 1:
                value = 0.5 * total
            else:
                value = total - dst[r, first : first + count, :]
            dst[r, first : first + count, :] = value
            return (e1, e2, f2), value

        def outer(r, carried):
            return advance(r, carried)[0]

        def inner(r, carried):
            carried, value = advance(r, carried)
            value = value[skip : skip + B]
            if scaled:
                value = value * scale[r, 8 : 8 + B, :]
            keep(k, r - H, value)
            return carried

        low = H - reach
        e0 = sums(low - 1)[0]
        e1, f1, _ = sums(low)
        carried = (e0, e1, f1)
        if reach:
            carried = lax.fori_loop(low, H, outer, carried)
        carried = lax.fori_loop(H, H + R, inner, carried)
        if reach:
            lax.fori_loop(H + R, H + R + reach, outer, carried)

    for copy in first_halo:
        copy.wait()
    assemble(0, yb, 1.0, 1.0)

    def start_row(r, _):
        x = yb[r, O - 8 : O + B + 8, :]
        ya[r, O - 8 : O + B + 8, :] = (-0.5 * coef[r] * scale[r]) * x
        return 0

    lax.fori_loop(0, RE, start_row, 0)

    def keep_first(r, _):
        keep(0, r, ya[H + r, O : O + B, :] * scale[H + r, 8 : 8 + B, :])
        return 0

    lax.fori_loop(0, R, keep_first, 0)
    step(ya, yb, 1, True)
    step(yb, ya, 2, True)
    step(ya, yb, 3, True)
    step(yb, ya, 4, True)

    cot_in.wait()
    widen(cot_v, cf)

    def mix(r):
        t = terms[pl.ds(pl.multiple_of(r * B, B), B), :]
        mixed = lax.dot_general(wf[...], t, NT, preferred_element_type=F32)
        act = jnp.tanh(mixed)
        grad = (rows_of(cf, r) * (1.0 - act * act)).astype(BF16)
        gcat[:, pl.ds(pl.multiple_of(r * B, B), B)] = grad
        turned = lax.dot_general(eye[...], grad, NT, preferred_element_type=F32)
        w = -0.5 * coef[H + r, 8 : 8 + B, :] * scale[H + r, 8 : 8 + B, :]
        ya[H + r, O : O + B, :] = w * turned

    def mix_edge(i, _):
        mix(i + (R - 2 * H) * (i // H))
        return 0

    def mix_inner(i, _):
        mix(i)
        return 0

    lax.fori_loop(0, 2 * H, mix_edge, 0)
    second_halo = halo_copies(1, ya)
    pack_rows(1, ya)
    for copy in second_halo[:6]:
        copy.start()
    lax.fori_loop(H, R - H, mix_inner, 0)
    for copy in second_halo[6:]:
        copy.start()

    chunk = 8 * B
    acc = None
    for n in range(R * B // chunk):
        part = jnp.dot(
            gcat[:, n * chunk : (n + 1) * chunk],
            terms[n * chunk : (n + 1) * chunk, :],
            preferred_element_type=F32,
        )
        acc = part if acc is None else acc + part
    lane_c = lax.broadcasted_iota(jnp.int32, (C, B), 1) // C
    folded = []
    for k in range(K + 1):
        tot = None
        for g in range(RG):
            piece = acc[g * C : (g + 1) * C, k * B : (k + 1) * B]
            tot = piece if tot is None else jnp.where(lane_c == g, piece, tot)
        tot = tot + pltpu.roll(tot, 64, 1)
        tot = tot + pltpu.roll(tot, 32, 1)
        folded.append(tot)
    head = folded[0]
    for k in range(1, K):
        head = jnp.where(lane_c == k, folded[k], head)
    tail = folded[K][0:8]
    for g in range(1, RG):
        tail = jnp.where(lane_c[0:8] == g, folded[K][8 * g : 8 * g + 8], tail)
    grid_cells = n_lat * n_lon * B * B
    own[0, 0:C, :] = head * (1.0 / math.sqrt(grid_cells))
    own[0, C : C + 8, :] = tail * (1.0 / math.sqrt(grid_cells))

    def lon_copy(off):
        return remote(
            own.at[0], ar1.at[lon], ar1_send.at[off], ar1_recv.at[lon],
            lat, lax.rem(lon + off, n_lon),
        )

    def lon_wait(off):
        q = lax.rem(lon + n_lon - off, n_lon)
        return remote(own.at[0], ar1.at[q], ar1_send.at[off], ar1_recv.at[q], lat, q)

    def lat_copy(off):
        return remote(
            own.at[1], ar2.at[lat], ar2_send.at[off], ar2_recv.at[lat],
            lax.rem(lat + off, n_lat), lon,
        )

    def lat_wait(off):
        q = lax.rem(lat + n_lat - off, n_lat)
        return remote(own.at[1], ar2.at[q], ar2_send.at[off], ar2_recv.at[q], q, lon)

    def run(count, act):
        def body(off, _):
            act(off)
            return 0

        lax.fori_loop(1, count, body, 0)

    run(n_lon, lambda off: lon_copy(off).start())
    ar1[lon] = own[0]

    for copy in second_halo:
        copy.wait()
    assemble(1, ya, north_ok, south_ok)

    def keep_grad(r, _):
        keep(0, r, ya[H + r, O : O + B, :])
        return 0

    lax.fori_loop(0, R, keep_grad, 0)
    step(ya, yb, 1, False)
    step(yb, ya, 2, False)

    run(n_lon, lambda off: lon_wait(off).wait())
    total = ar1[0]
    for q in range(1, n_lon):
        total = total + ar1[q]
    own[1] = total
    run(n_lat, lambda off: lat_copy(off).start())
    ar2[lat] = total

    step(ya, yb, 3, False)
    step(yb, ya, 4, False)

    def finish(r, _):
        t = terms[pl.ds(pl.multiple_of(r * B, B), B), :]
        res = lax.dot_general(wb[...], t, NT, preferred_element_type=F32)
        for g in range(RG):
            s = jnp.broadcast_to(snat[pl.ds(R * g + r, 1), :], (C, B))
            xf[pl.ds(R * g + r, C, stride=B), :] = res[g * C : (g + 1) * C] * s
        return 0

    lax.fori_loop(0, R, finish, 0)

    def narrow(c, _):
        out_v[c] = xf[pl.ds(pl.multiple_of(c * B, B), B), :].astype(BF16)
        return 0

    lax.fori_loop(0, C, narrow, 0)
    out_copy = pltpu.make_async_copy(out_v, out_hbm, out_sem)
    out_copy.start()

    run(n_lat, lambda off: lat_wait(off).wait())
    total = ar2[0]
    for q in range(1, n_lat):
        total = total + ar2[q]
    flat = total[0:C].T
    for k in range(K):
        wg_ref[k] = flat[k * C : (k + 1) * C, :]
    last = total[C : C + 8]
    last = jnp.concatenate(
        [last if g == 0 else pltpu.roll(last, B - C * g, 1) for g in range(RG)], axis=0
    )
    wg_ref[K] = last.T[0:C, :]
    out_copy.wait()


def solution(mesh):
    n_lat, n_lon = mesh.shape["lat"], mesh.shape["lon"]
    hbm = pl.BlockSpec(memory_space=pl.ANY)
    sem = pltpu.SemaphoreType.DMA

    def local(features, cotangent, sea_mask, weights):
        return pl.pallas_call(
            functools.partial(kernel, n_lat, n_lon),
            out_shape=(
                jax.ShapeDtypeStruct((C, B, B), BF16),
                jax.ShapeDtypeStruct((K + 1, C, C), F32),
            ),
            in_specs=[hbm] * 4,
            out_specs=(hbm, pl.BlockSpec(memory_space=pltpu.VMEM)),
            scratch_shapes=[
                pltpu.VMEM((C, B, B), BF16),
                pltpu.VMEM((C, B, B), BF16),
                pltpu.VMEM((B, B), jnp.int32),
                pltpu.VMEM((K + 1, C, C), BF16),
                pltpu.VMEM((C * B, B), F32),
                pltpu.VMEM((C * B, B), F32),
                pltpu.VMEM((C, B, B), BF16),
                pltpu.VMEM((RE, CP, B), F32),
                pltpu.VMEM((RE, CP, B), F32),
                pltpu.VMEM((RE, CE, B), F32),
                pltpu.VMEM((RE, CE, B), F32),
                pltpu.VMEM((R * B, (K + 1) * B), BF16),
                pltpu.VMEM((B, R * B), BF16),
                pltpu.VMEM((3, CE, B), F32),
                pltpu.VMEM((2, CP, B), F32),
                pltpu.VMEM((CE, 2 * B), F32),
                pltpu.VMEM((B, B), F32),
                pltpu.VMEM((B, (K + 1) * B), BF16),
                pltpu.VMEM((B, (K + 1) * B), BF16),
                pltpu.VMEM((B, B), BF16),
                pltpu.VMEM((CE, 2 * B), BF16),
                pltpu.VMEM((2, 2, B, B), F32),
                pltpu.VMEM((2, 2, CE, B), F32),
                pltpu.VMEM((2, 2, R, 8, B), F32),
                pltpu.VMEM((2, C + 8, B), F32),
                pltpu.VMEM((n_lon, C + 8, B), F32),
                pltpu.VMEM((n_lat, C + 8, B), F32),
                sem((4,)), sem(()), sem((8,)), sem((8,)), sem((2, 8)), sem((2, 8)),
                sem((n_lon,)), sem((n_lon,)), sem((n_lat,)), sem((n_lat,)),
            ],
            compiler_params=pltpu.CompilerParams(
                collective_id=0, has_side_effects=True, vmem_limit_bytes=56 << 20
            ),
        )(features, cotangent, sea_mask, weights)

    placed = (P(None, "lat", "lon"), P(None, "lat", "lon"), P("lat", "lon"), P())
    return jax.shard_map(
        local, mesh=mesh, in_specs=placed, out_specs=(P(None, "lat", "lon"), P()), check_vma=False
    )
```

```python
import functools
import math

import jax
import jax.numpy as jnp
from jax import lax
from jax.experimental import pallas as pl
from jax.experimental.pallas import tpu as pltpu
from jax.sharding import PartitionSpec as P

K = 4
C = 32
B = 128
RG = 4
R = B // RG
H = 4
RE = R + 2 * H
CE = B + 16
CP = CE + 16
O = 16
F32 = jnp.float32
BF16 = jnp.bfloat16
NT = (((1,), (1,)), ((), ()))


def kernel(
    n_lat, n_lon,
    feat_hbm, cot_hbm, mask_hbm, w_hbm,
    out_hbm, wg_ref,
    feat_v, cot_v, mask_v, w_v, xf, cf, out_v,
    ya, yb, coef, scale, terms, gcat,
    mb, sm, vm, snat, wf, wb, sel,
    pack, lrow, lcol, own, ar1, ar2,
    in_sem, out_sem, mask_send, mask_recv, halo_send, halo_recv,
    ar1_send, ar1_recv, ar2_send, ar2_recv,
):
    lat = lax.axis_index("lat")
    lon = lax.axis_index("lon")
    north, south = lax.rem(lat + n_lat - 1, n_lat), lax.rem(lat + 1, n_lat)
    west, east = lax.rem(lon + n_lon - 1, n_lon), lax.rem(lon + 1, n_lon)

    feat_in = pltpu.make_async_copy(feat_hbm, feat_v, in_sem.at[0])
    cot_in = pltpu.make_async_copy(cot_hbm, cot_v, in_sem.at[1])
    mask_in = pltpu.make_async_copy(mask_hbm, mask_v, in_sem.at[2])
    w_in = pltpu.make_async_copy(w_hbm, w_v, in_sem.at[3])
    mask_in.start()
    feat_in.start()
    w_in.start()
    cot_in.start()

    barrier = pltpu.get_barrier_semaphore()

    def greet(i, j):
        pl.semaphore_signal(
            barrier, inc=1, device_id=(i, j), device_id_type=pl.DeviceIdType.MESH
        )

    for i in (north, south):
        for j in (west, east):
            greet(i, j)

    def greet_lon(off, _):
        greet(lat, lax.rem(lon + off, n_lon))
        return 0

    def greet_lat(off, _):
        greet(lax.rem(lat + off, n_lat), lon)
        return 0

    lax.fori_loop(1, n_lon, greet_lon, 0)
    lax.fori_loop(1, n_lat, greet_lat, 0)

    row_i = lax.broadcasted_iota(jnp.int32, (B, B), 0)
    col_i = lax.broadcasted_iota(jnp.int32, (B, B), 1)
    sel_r = lax.broadcasted_iota(jnp.int32, (CE, 2 * B), 0)
    sel_c = lax.broadcasted_iota(jnp.int32, (CE, 2 * B), 1)
    inside = (sel_r >= 8) & (sel_r < 8 + B) & (sel_c == sel_r - 8)
    left = (sel_r < 8) & (sel_c == 2 * B - 8 + sel_r)
    right = (sel_r >= 8 + B) & (sel_c == sel_r - 8)
    sel[...] = (inside | left | right).astype(F32).astype(BF16)

    mask_in.wait()
    mb[1, 8 : 8 + B, :] = mask_v[...].astype(F32)
    pl.semaphore_wait(barrier, 4 + (n_lon - 1) + (n_lat - 1))

    def remote(src, dst, send, recv, i, j):
        return pltpu.make_async_remote_copy(
            src_ref=src, dst_ref=dst, send_sem=send, recv_sem=recv,
            device_id=(i, j), device_id_type=pl.DeviceIdType.MESH,
        )

    mid, top, bottom = pl.ds(8, B), pl.ds(8, 8), pl.ds(B, 8)
    above, below = pl.ds(0, 8), pl.ds(8 + B, 8)
    mask_plan = (
        (mid, 0, mid, lat, east),
        (mid, 2, mid, lat, west),
        (bottom, 1, above, south, lon),
        (top, 1, below, north, lon),
        (bottom, 0, above, south, east),
        (bottom, 2, above, south, west),
        (top, 0, below, north, east),
        (top, 2, below, north, west),
    )
    mask_copies = [
        remote(mb.at[1, src], mb.at[slot, dst], mask_send.at[n], mask_recv.at[n], i, j)
        for n, (src, slot, dst, i, j) in enumerate(mask_plan)
    ]
    for copy in mask_copies:
        copy.start()

    lane = lax.broadcasted_iota(jnp.int32, (B, B), 1)

    def halo_copies(phase, y):
        plan = (
            (pack.at[phase, 0], lrow.at[phase, 0, mid], south, lon),
            (pack.at[phase, 1], lrow.at[phase, 1, mid], north, lon),
            (pack.at[phase, 0, pl.ds(B - 8, 8)], lrow.at[phase, 0, above], south, east),
            (pack.at[phase, 0, pl.ds(0, 8)], lrow.at[phase, 0, below], south, west),
            (pack.at[phase, 1, pl.ds(B - 8, 8)], lrow.at[phase, 1, above], north, east),
            (pack.at[phase, 1, pl.ds(0, 8)], lrow.at[phase, 1, below], north, west),
            (y.at[pl.ds(H, R), pl.ds(O + B - 8, 8)], lcol.at[phase, 0], lat, east),
            (y.at[pl.ds(H, R), pl.ds(O, 8)], lcol.at[phase, 1], lat, west),
        )
        return [
            remote(src, dst, halo_send.at[phase, n], halo_recv.at[phase, n], i, j)
            for n, (src, dst, i, j) in enumerate(plan)
        ]

    def pack_rows(phase, y):
        last, first = None, None
        for i in range(H):
            a = pltpu.roll(y[H + R - H + i, O : O + B, :], (32 * i + 32) % 128, 1)
            b = pltpu.roll(y[H + i, O : O + B, :], (32 * i) % 128, 1)
            here = (lane >= 32 * i) & (lane < 32 * i + 32)
            last = a if last is None else jnp.where(here, a, last)
            first = b if first is None else jnp.where(here, b, first)
        pack[phase, 0] = last
        pack[phase, 1] = first

    feat_in.wait()

    def widen(src, dst):
        def body(c, _):
            dst[pl.ds(pl.multiple_of(c * B, B), B), :] = src[c].astype(F32)
            return 0

        lax.fori_loop(0, C, body, 0, unroll=4)

    def rows_of(flat, r):
        return jnp.concatenate(
            [flat[pl.ds(R * g + r, C, stride=B), :] for g in range(RG)], axis=0
        )

    widen(feat_v, xf)

    def turn(r):
        yb[H + r, O : O + B, :] = rows_of(xf, r).T

    def turn_edge(i, _):
        turn(i + (R - 2 * H) * (i // H))
        return 0

    def turn_inner(i, _):
        turn(i)
        return 0

    lax.fori_loop(0, 2 * H, turn_edge, 0, unroll=8)
    first_halo = halo_copies(0, yb)
    pack_rows(0, yb)
    for copy in first_halo[:6]:
        copy.start()
    lax.fori_loop(H, R - H, turn_inner, 0, unroll=8)
    for copy in first_halo[6:]:
        copy.start()

    w_in.wait()
    block = (row_i // C) == (col_i // C)
    for k in range(K + 1):
        one = w_v[k].astype(F32)
        wide = jnp.concatenate([one] * RG, axis=1)
        full = jnp.where(block, jnp.concatenate([wide] * RG, axis=0), 0.0)
        wb[:, k * B : (k + 1) * B] = full.astype(BF16)
        wf[:, k * B : (k + 1) * B] = full.T.astype(BF16)

    for copy in mask_copies:
        copy.wait()
    north_ok = (lat > 0).astype(F32)
    south_ok = (lat < n_lat - 1).astype(F32)
    lane_e = lax.broadcasted_iota(jnp.int32, (CE, B), 1)
    row_e = lax.broadcasted_iota(jnp.int32, (CE, B), 0)
    ok = jnp.where(row_e < 8, north_ok, jnp.where(row_e >= 8 + B, south_ok, 1.0))
    sm[...] = jnp.zeros_like(sm)
    sm[0, 8 : 8 + CE, :] = mb[1] * ok
    sm[1, 8 : 8 + CE, :] = jnp.where(lane_e < 64, mb[2], mb[0]) * ok

    def ring(main, side, shift, edge):
        m, s = pltpu.roll(main, shift, 1), pltpu.roll(side, shift, 1)
        at = lane_e == edge
        return jnp.where(at, s, m), jnp.where(at, m, s)

    here = [sm[t, 8 : 8 + CE, :] for t in range(2)]
    up = [sm[t, 7 : 7 + CE, :] for t in range(2)]
    down = [sm[t, 9 : 9 + CE, :] for t in range(2)]
    from_left = ring(here[0] + down[0], here[1] + down[1], 1, 0)
    from_right = ring(here[0] + up[0], here[1] + up[1], B - 1, B - 1)
    for t in range(2):
        degree = from_left[t] + from_right[t] + up[t] + down[t]
        vm[:, t * B : (t + 1) * B] = here[t] * jnp.maximum(degree, 1.0)
        if t == 0:
            snat[...] = jnp.sqrt(jnp.maximum(degree, 1.0)[8 : 8 + B])

    def spread(p, _):
        rows = jnp.concatenate(
            [
                jnp.broadcast_to(vm[pl.ds(8 - H + R * g + 2 * p + j, 1), :], (C, 2 * B))
                for j in range(2)
                for g in range(RG)
            ],
            axis=0,
        )
        v = lax.dot_general(sel[...], rows.astype(BF16), NT, preferred_element_type=F32)
        m = jnp.maximum(v, 1.0)
        rs = lax.rsqrt(m)
        a, s = jnp.where(v > 0.5, -2.0 * rs * rs, 0.0), m * rs
        for j in range(2):
            coef[2 * p + j] = a[:, j * B : (j + 1) * B]
            scale[2 * p + j] = s[:, j * B : (j + 1) * B]
        return 0

    lax.fori_loop(0, RE // 2, spread, 0, unroll=4)

    def assemble(phase, y, ok_north, ok_south):
        def sides(r, _):
            y[H + r, O - 8 : O, :] = lcol[phase, 0, r]
            y[H + r, O + B : O + B + 8, :] = lcol[phase, 1, r]
            return 0

        lax.fori_loop(0, R, sides, 0, unroll=4)
        for i in range(H):
            own_up = pltpu.roll(y[R + i, O - 8 : O + B + 8, :], 32, 1)
            far_up = pltpu.roll(lrow[phase, 0], (B - 32 * i) % B, 1) * ok_north
            y[i, O - 8 : O + B + 8, :] = jnp.where(lane_e < 32, far_up, own_up)
            own_down = pltpu.roll(y[H + i, O - 8 : O + B + 8, :], B - 32, 1)
            far_down = pltpu.roll(lrow[phase, 1], (96 - 32 * i) % B, 1) * ok_south
            y[H + R + i, O - 8 : O + B + 8, :] = jnp.where(
                lane_e >= 96, far_down, own_down
            )

    def keep(k, r, value):
        terms[pl.ds(pl.multiple_of(r * B, B), B), k * B : (k + 1) * B] = value.astype(BF16)

    def step(src, dst, k, scaled):
        reach = K - k
        first, count = (O - 8, CE) if reach else (O, B)
        size = 48 if reach else 64
        for at in range(0, count, size):
            step_block(src, dst, k, scaled, first + at, size)

    def step_block(src, dst, k, scaled, first, size):
        reach = K - k
        lo, hi = max(first, O), min(first + size, O + B)

        def sums(r):
            mid_ = src[r, first : first + size, :]
            low = src[r, first - 1 : first - 1 + size, :]
            high = src[r, first + 1 : first + 1 + size, :]
            return mid_ + high, low + high, mid_ + low

        def advance(r, carried):
            e0, e1, f1 = carried
            e2, f2, h2 = sums(r + 1)
            a = coef[r, first - O + 8 : first - O + 8 + size, :]
            total = a * (e0 + f1 + h2)
            if k == 1:
                value = 0.5 * total
            else:
                value = total - dst[r, first : first + size, :]
            dst[r, first : first + size, :] = value
            return (e1, e2, f2), value

        def outer(r, carried):
            return advance(r, carried)[0]

        def inner(r, carried):
            carried, value = advance(r, carried)
            value = value[lo - first : hi - first]
            if scaled:
                value = value * scale[r, lo - O + 8 : hi - O + 8, :]
            at = pl.multiple_of((r - H) * B + lo - O, 8)
            terms[pl.ds(at, hi - lo), k * B : (k + 1) * B] = value.astype(BF16)
            return carried

        low = H - reach
        e0 = sums(low - 1)[0]
        e1, f1, _ = sums(low)
        carried = (e0, e1, f1)
        if reach:
            carried = lax.fori_loop(low, H, outer, carried, unroll=reach)
        carried = lax.fori_loop(H, H + R, inner, carried, unroll=8)
        if reach:
            lax.fori_loop(H + R, H + R + reach, outer, carried, unroll=reach)

    for copy in first_halo:
        copy.wait()
    assemble(0, yb, 1.0, 1.0)

    def start_row(r, _):
        x = yb[r, O - 8 : O + B + 8, :]
        ya[r, O - 8 : O + B + 8, :] = (-0.5 * coef[r] * scale[r]) * x
        return 0

    lax.fori_loop(0, RE, start_row, 0, unroll=4)

    def keep_first(r, _):
        keep(0, r, ya[H + r, O : O + B, :] * scale[H + r, 8 : 8 + B, :])
        return 0

    lax.fori_loop(0, R, keep_first, 0, unroll=4)
    step(ya, yb, 1, True)
    step(yb, ya, 2, True)
    step(ya, yb, 3, True)
    step(yb, ya, 4, True)

    cot_in.wait()
    widen(cot_v, cf)

    def mix(p):
        at = pl.ds(pl.multiple_of(2 * p * B, 2 * B), 2 * B)
        mixed = lax.dot_general(wf[...], terms[at, :], NT, preferred_element_type=F32)
        act = jnp.tanh(mixed)
        cot = jnp.concatenate([rows_of(cf, 2 * p), rows_of(cf, 2 * p + 1)], axis=1)
        gcat[:, at] = (cot * (1.0 - act * act)).astype(BF16)

    def turn_grad(r):
        grad = gcat[:, pl.ds(pl.multiple_of(r * B, B), B)].astype(F32)
        w = -0.5 * coef[H + r, 8 : 8 + B, :] * scale[H + r, 8 : 8 + B, :]
        ya[H + r, O : O + B, :] = w * grad.T

    def mix_edge(i, _):
        mix(i + (R // 2 - H) * (i // (H // 2)))
        return 0

    def mix_inner(i, _):
        mix(i)
        return 0

    def grad_edge(i, _):
        turn_grad(i + (R - 2 * H) * (i // H))
        return 0

    def grad_inner(i, _):
        turn_grad(i)
        return 0

    lax.fori_loop(0, H, mix_edge, 0, unroll=H)
    lax.fori_loop(0, 2 * H, grad_edge, 0, unroll=8)
    second_halo = halo_copies(1, ya)
    pack_rows(1, ya)
    for copy in second_halo[:6]:
        copy.start()
    lax.fori_loop(H // 2, R // 2 - H // 2, mix_inner, 0, unroll=4)
    lax.fori_loop(H, R - H, grad_inner, 0, unroll=8)
    for copy in second_halo[6:]:
        copy.start()

    chunk = 8 * B
    acc = None
    for n in range(R * B // chunk):
        part = jnp.dot(
            gcat[:, n * chunk : (n + 1) * chunk],
            terms[n * chunk : (n + 1) * chunk, :],
            preferred_element_type=F32,
        )
        acc = part if acc is None else acc + part
    lane_c = lax.broadcasted_iota(jnp.int32, (C, B), 1) // C
    folded = []
    for k in range(K + 1):
        tot = None
        for g in range(RG):
            piece = acc[g * C : (g + 1) * C, k * B : (k + 1) * B]
            tot = piece if tot is None else jnp.where(lane_c == g, piece, tot)
        tot = tot + pltpu.roll(tot, 64, 1)
        tot = tot + pltpu.roll(tot, 32, 1)
        folded.append(tot)
    head = folded[0]
    for k in range(1, K):
        head = jnp.where(lane_c == k, folded[k], head)
    tail = folded[K][0:8]
    for g in range(1, RG):
        tail = jnp.where(lane_c[0:8] == g, folded[K][8 * g : 8 * g + 8], tail)
    grid_cells = n_lat * n_lon * B * B
    own[0, 0:C, :] = head * (1.0 / math.sqrt(grid_cells))
    own[0, C : C + 8, :] = tail * (1.0 / math.sqrt(grid_cells))

    def lon_copy(off):
        return remote(
            own.at[0], ar1.at[lon], ar1_send.at[off], ar1_recv.at[lon],
            lat, lax.rem(lon + off, n_lon),
        )

    def lon_wait(off):
        q = lax.rem(lon + n_lon - off, n_lon)
        return remote(own.at[0], ar1.at[q], ar1_send.at[off], ar1_recv.at[q], lat, q)

    def lat_copy(off):
        return remote(
            own.at[1], ar2.at[lat], ar2_send.at[off], ar2_recv.at[lat],
            lax.rem(lat + off, n_lat), lon,
        )

    def lat_wait(off):
        q = lax.rem(lat + n_lat - off, n_lat)
        return remote(own.at[1], ar2.at[q], ar2_send.at[off], ar2_recv.at[q], q, lon)

    def run(count, act):
        def body(off, _):
            act(off)
            return 0

        lax.fori_loop(1, count, body, 0)

    run(n_lon, lambda off: lon_copy(off).start())
    ar1[lon] = own[0]

    for copy in second_halo:
        copy.wait()
    assemble(1, ya, north_ok, south_ok)

    def keep_grad(r, _):
        keep(0, r, ya[H + r, O : O + B, :])
        return 0

    lax.fori_loop(0, R, keep_grad, 0, unroll=4)
    step(ya, yb, 1, False)
    step(yb, ya, 2, False)

    run(n_lon, lambda off: lon_wait(off).wait())
    total = ar1[0]
    for q in range(1, n_lon):
        total = total + ar1[q]
    own[1] = total
    run(n_lat, lambda off: lat_copy(off).start())
    ar2[lat] = total

    step(ya, yb, 3, False)
    step(yb, ya, 4, False)

    def finish(p, _):
        t = terms[pl.ds(pl.multiple_of(2 * p * B, 2 * B), 2 * B), :]
        res = lax.dot_general(wb[...], t, NT, preferred_element_type=F32)
        for j in range(2):
            for g in range(RG):
                row = R * g + 2 * p + j
                s = jnp.broadcast_to(snat[pl.ds(row, 1), :], (C, B))
                part = res[g * C : (g + 1) * C, j * B : (j + 1) * B]
                xf[pl.ds(row, C, stride=B), :] = part * s
        return 0

    lax.fori_loop(0, R // 2, finish, 0, unroll=4)

    def narrow(c, _):
        out_v[c] = xf[pl.ds(pl.multiple_of(c * B, B), B), :].astype(BF16)
        return 0

    lax.fori_loop(0, C, narrow, 0, unroll=4)
    out_copy = pltpu.make_async_copy(out_v, out_hbm, out_sem)
    out_copy.start()

    run(n_lat, lambda off: lat_wait(off).wait())
    total = ar2[0]
    for q in range(1, n_lat):
        total = total + ar2[q]
    flat = total[0:C].T
    for k in range(K):
        wg_ref[k] = flat[k * C : (k + 1) * C, :]
    last = total[C : C + 8]
    last = jnp.concatenate(
        [last if g == 0 else pltpu.roll(last, B - C * g, 1) for g in range(RG)], axis=0
    )
    wg_ref[K] = last.T[0:C, :]
    out_copy.wait()


def solution(mesh):
    n_lat, n_lon = mesh.shape["lat"], mesh.shape["lon"]
    hbm = pl.BlockSpec(memory_space=pl.ANY)
    sem = pltpu.SemaphoreType.DMA

    def local(features, cotangent, sea_mask, weights):
        return pl.pallas_call(
            functools.partial(kernel, n_lat, n_lon),
            out_shape=(
                jax.ShapeDtypeStruct((C, B, B), BF16),
                jax.ShapeDtypeStruct((K + 1, C, C), F32),
            ),
            in_specs=[hbm] * 4,
            out_specs=(hbm, pl.BlockSpec(memory_space=pltpu.VMEM)),
            scratch_shapes=[
                pltpu.VMEM((C, B, B), BF16),
                pltpu.VMEM((C, B, B), BF16),
                pltpu.VMEM((B, B), jnp.int32),
                pltpu.VMEM((K + 1, C, C), BF16),
                pltpu.VMEM((C * B, B), F32),
                pltpu.VMEM((C * B, B), F32),
                pltpu.VMEM((C, B, B), BF16),
                pltpu.VMEM((RE, CP, B), F32),
                pltpu.VMEM((RE, CP, B), F32),
                pltpu.VMEM((RE, CE, B), F32),
                pltpu.VMEM((RE, CE, B), F32),
                pltpu.VMEM((R * B, (K + 1) * B), BF16),
                pltpu.VMEM((B, R * B), BF16),
                pltpu.VMEM((3, CE, B), F32),
                pltpu.VMEM((2, CP, B), F32),
                pltpu.VMEM((CE, 2 * B), F32),
                pltpu.VMEM((B, B), F32),
                pltpu.VMEM((B, (K + 1) * B), BF16),
                pltpu.VMEM((B, (K + 1) * B), BF16),
                pltpu.VMEM((CE, 2 * B), BF16),
                pltpu.VMEM((2, 2, B, B), F32),
                pltpu.VMEM((2, 2, CE, B), F32),
                pltpu.VMEM((2, 2, R, 8, B), F32),
                pltpu.VMEM((2, C + 8, B), F32),
                pltpu.VMEM((n_lon, C + 8, B), F32),
                pltpu.VMEM((n_lat, C + 8, B), F32),
                sem((4,)), sem(()), sem((8,)), sem((8,)), sem((2, 8)), sem((2, 8)),
                sem((n_lon,)), sem((n_lon,)), sem((n_lat,)), sem((n_lat,)),
            ],
            compiler_params=pltpu.CompilerParams(
                collective_id=0, has_side_effects=True, vmem_limit_bytes=56 << 20
            ),
        )(features, cotangent, sea_mask, weights)

    placed = (P(None, "lat", "lon"), P(None, "lat", "lon"), P("lat", "lon"), P())
    return jax.shard_map(
        local, mesh=mesh, in_specs=placed, out_specs=(P(None, "lat", "lon"), P()), check_vma=False
    )
```

```python
import functools
import math

import jax
import jax.numpy as jnp
from jax import lax
from jax.experimental import pallas as pl
from jax.experimental.pallas import tpu as pltpu
from jax.sharding import PartitionSpec as P

K = 4
C = 32
B = 128
RG = 4
R = B // RG
H = 4
RE = R + 2 * H
CE = B + 16
CP = CE + 16
O = 16
F32 = jnp.float32
BF16 = jnp.bfloat16
NT = (((1,), (1,)), ((), ()))


def kernel(
    n_lat, n_lon,
    feat_hbm, cot_hbm, mask_hbm, w_hbm,
    out_hbm, wg_ref,
    feat_v, cot_v, mask_v, w_v, xf, cf, out_v,
    ya, yb, coef, scale, terms, gcat,
    mtx, mrx, sm, vm, snat, wf, wb, sel,
    pack, cpack, lrow, lcol, own, ar1, ar2,
    in_sem, out_sem, mask_send, mask_recv, halo_send, halo_recv,
    ar1_send, ar1_recv, ar2_send, ar2_recv,
):
    lat = lax.axis_index("lat")
    lon = lax.axis_index("lon")
    north, south = lax.rem(lat + n_lat - 1, n_lat), lax.rem(lat + 1, n_lat)
    west, east = lax.rem(lon + n_lon - 1, n_lon), lax.rem(lon + 1, n_lon)

    feat_in = pltpu.make_async_copy(feat_hbm, feat_v, in_sem.at[0])
    cot_in = pltpu.make_async_copy(cot_hbm, cot_v, in_sem.at[1])
    mask_in = pltpu.make_async_copy(mask_hbm, mask_v, in_sem.at[2])
    w_in = pltpu.make_async_copy(w_hbm, w_v, in_sem.at[3])
    mask_in.start()
    feat_in.start()
    w_in.start()
    cot_in.start()

    barrier = pltpu.get_barrier_semaphore()

    def greet(i, j):
        pl.semaphore_signal(
            barrier, inc=1, device_id=(i, j), device_id_type=pl.DeviceIdType.MESH
        )

    for i in (north, south):
        for j in (west, east):
            greet(i, j)

    def greet_lon(off, _):
        greet(lat, lax.rem(lon + off, n_lon))
        return 0

    def greet_lat(off, _):
        greet(lax.rem(lat + off, n_lat), lon)
        return 0

    lax.fori_loop(1, n_lon, greet_lon, 0)
    lax.fori_loop(1, n_lat, greet_lat, 0)

    row_i = lax.broadcasted_iota(jnp.int32, (B, B), 0)
    col_i = lax.broadcasted_iota(jnp.int32, (B, B), 1)
    sel_r = lax.broadcasted_iota(jnp.int32, (CE, 2 * B), 0)
    sel_c = lax.broadcasted_iota(jnp.int32, (CE, 2 * B), 1)
    inside = (sel_r >= 8) & (sel_r < 8 + B) & (sel_c == sel_r - 8)
    left = (sel_r < 8) & (sel_c == 2 * B - 8 + sel_r)
    right = (sel_r >= 8 + B) & (sel_c == sel_r - 8)
    sel[...] = (inside | left | right).astype(F32).astype(BF16)

    mask_in.wait()
    flags = mask_v[...].astype(F32)
    turned_flags = flags.T
    mtx[0] = flags[B - 8 :]
    mtx[1] = flags[:8]
    mtx[2] = turned_flags[B - 8 :]
    mtx[3] = turned_flags[:8]
    pl.semaphore_wait(barrier, 4 + (n_lon - 1) + (n_lat - 1))

    def remote(src, dst, send, recv, i, j):
        return pltpu.make_async_remote_copy(
            src_ref=src, dst_ref=dst, send_sem=send, recv_sem=recv,
            device_id=(i, j), device_id_type=pl.DeviceIdType.MESH,
        )

    mid = pl.ds(8, B)
    above, below = pl.ds(0, 8), pl.ds(8 + B, 8)
    mask_plan = (
        (2, 0, lat, east),
        (3, 1, lat, west),
        (0, 2, south, lon),
        (1, 3, north, lon),
        (0, 4, south, east),
        (0, 5, south, west),
        (1, 6, north, east),
        (1, 7, north, west),
    )
    mask_copies = [
        remote(mtx.at[src], mrx.at[n], mask_send.at[n], mask_recv.at[n], i, j)
        for src, n, i, j in mask_plan
    ]
    for copy in mask_copies:
        copy.start()

    lane = lax.broadcasted_iota(jnp.int32, (B, B), 1)

    def halo_copies(phase):
        plan = (
            (pack.at[phase, 0], lrow.at[phase, 0, mid], south, lon),
            (pack.at[phase, 1], lrow.at[phase, 1, mid], north, lon),
            (pack.at[phase, 0, pl.ds(B - 8, 8)], lrow.at[phase, 0, above], south, east),
            (pack.at[phase, 0, pl.ds(0, 8)], lrow.at[phase, 0, below], south, west),
            (pack.at[phase, 1, pl.ds(B - 8, 8)], lrow.at[phase, 1, above], north, east),
            (pack.at[phase, 1, pl.ds(0, 8)], lrow.at[phase, 1, below], north, west),
        ) + tuple(
            (cpack.at[phase, side, at], lcol.at[phase, side, at], lat, (east, west)[side])
            for at in (pl.ds(0, 2), pl.ds(14, 2), pl.ds(2, 4), pl.ds(6, 4), pl.ds(10, 4))
            for side in range(2)
        )
        return [
            remote(src, dst, halo_send.at[phase, n], halo_recv.at[phase, n], i, j)
            for n, (src, dst, i, j) in enumerate(plan)
        ]

    def pack_rows(phase, y):
        last, first = None, None
        for i in range(H):
            a = pltpu.roll(y[H + R - H + i, O : O + B, :], (32 * i + 32) % 128, 1)
            b = pltpu.roll(y[H + i, O : O + B, :], (32 * i) % 128, 1)
            here = (lane >= 32 * i) & (lane < 32 * i + 32)
            last = a if last is None else jnp.where(here, a, last)
            first = b if first is None else jnp.where(here, b, first)
        pack[phase, 0] = last
        pack[phase, 1] = first

    half = lax.broadcasted_iota(jnp.int32, (8, B), 0) < 4

    def pack_columns(phase, y, p):
        a, b = y[H + 2 * p, O + B - 8 : O + B, :], y[H + 2 * p + 1, O + B - 8 : O + B, :]
        cpack[phase, 0, p] = jnp.where(half, pltpu.roll(a, 4, 0), b)
        a, b = y[H + 2 * p, O : O + 8, :], y[H + 2 * p + 1, O : O + 8, :]
        cpack[phase, 1, p] = jnp.where(half, a, pltpu.roll(b, 4, 0))

    def send_chunks(phase, y, copies, turn_rows):
        turn_rows(0, H)
        turn_rows(R - H, H)
        for p in (0, 1, 14, 15):
            pack_columns(phase, y, p)
        pack_rows(phase, y)
        for copy in copies[:10]:
            copy.start()
        for n in range(3):
            turn_rows(H + 8 * n, 8)
            for p in range(2 + 4 * n, 6 + 4 * n):
                pack_columns(phase, y, p)
            for copy in copies[10 + 2 * n : 12 + 2 * n]:
                copy.start()

    feat_in.wait()

    def widen(src, dst):
        def body(c, _):
            dst[pl.ds(pl.multiple_of(c * B, B), B), :] = src[c].astype(F32)
            return 0

        lax.fori_loop(0, C, body, 0, unroll=4)

    def rows_of(flat, r):
        return jnp.concatenate(
            [flat[pl.ds(R * g + r, C, stride=B), :] for g in range(RG)], axis=0
        )

    widen(feat_v, xf)

    def turn(r):
        yb[H + r, O : O + B, :] = rows_of(xf, r).T

    def turn_rows(first, count):
        for r in range(first, first + count):
            turn(r)

    first_halo = halo_copies(0)
    send_chunks(0, yb, first_halo, turn_rows)

    w_in.wait()
    block = (row_i // C) == (col_i // C)
    for k in range(K + 1):
        one = w_v[k].astype(F32)
        wide = jnp.concatenate([one] * RG, axis=1)
        full = jnp.where(block, jnp.concatenate([wide] * RG, axis=0), 0.0)
        wb[:, k * B : (k + 1) * B] = full.astype(BF16)
        wf[:, k * B : (k + 1) * B] = full.T.astype(BF16)

    for copy in mask_copies:
        copy.wait()
    north_ok = (lat > 0).astype(F32)
    south_ok = (lat < n_lat - 1).astype(F32)
    lane_e = lax.broadcasted_iota(jnp.int32, (CE, B), 1)
    sm[:, 0:8, :] = jnp.zeros((2, 8, B), F32)
    sm[:, 8 + CE :, :] = jnp.zeros((2, 8, B), F32)
    sm[0, 8:16, :] = mrx[2] * north_ok
    sm[0, 16 : 16 + B, :] = mask_v[...].astype(F32)
    sm[0, 16 + B : 24 + B, :] = mrx[3] * south_ok
    low_lanes = lane_e[0:8] < 64
    sm[1, 8:16, :] = jnp.where(low_lanes, mrx[5], mrx[4]) * north_ok
    sm[1, 16 : 16 + B, :] = jnp.concatenate(
        [mrx[1], jnp.zeros((B - 16, B), F32), mrx[0]], axis=0
    ).T
    sm[1, 16 + B : 24 + B, :] = jnp.where(low_lanes, mrx[7], mrx[6]) * south_ok

    def ring(main, side, shift, edge):
        m, s = pltpu.roll(main, shift, 1), pltpu.roll(side, shift, 1)
        at = lane_e == edge
        return jnp.where(at, s, m), jnp.where(at, m, s)

    here = [sm[t, 8 : 8 + CE, :] for t in range(2)]
    up = [sm[t, 7 : 7 + CE, :] for t in range(2)]
    down = [sm[t, 9 : 9 + CE, :] for t in range(2)]
    from_left = ring(here[0] + down[0], here[1] + down[1], 1, 0)
    from_right = ring(here[0] + up[0], here[1] + up[1], B - 1, B - 1)
    for t in range(2):
        degree = from_left[t] + from_right[t] + up[t] + down[t]
        vm[:, t * B : (t + 1) * B] = here[t] * jnp.maximum(degree, 1.0)
        if t == 0:
            snat[...] = jnp.sqrt(jnp.maximum(degree, 1.0)[8 : 8 + B])

    def spread(p, _):
        rows = jnp.concatenate(
            [
                jnp.broadcast_to(vm[pl.ds(8 - H + R * g + 2 * p + j, 1), :], (C, 2 * B))
                for j in range(2)
                for g in range(RG)
            ],
            axis=0,
        )
        v = lax.dot_general(sel[...], rows.astype(BF16), NT, preferred_element_type=F32)
        m = jnp.maximum(v, 1.0)
        rs = lax.rsqrt(m)
        a, s = jnp.where(v > 0.5, -2.0 * rs * rs, 0.0), m * rs
        for j in range(2):
            coef[2 * p + j] = a[:, j * B : (j + 1) * B]
            scale[2 * p + j] = s[:, j * B : (j + 1) * B]
        return 0

    lax.fori_loop(0, RE // 2, spread, 0, unroll=4)

    def assemble(phase, y, ok_north, ok_south):
        for p in range(R // 2):
            a, b = lcol[phase, 0, p], lcol[phase, 1, p]
            y[H + 2 * p, O - 8 : O, :] = pltpu.roll(a, 4, 0)
            y[H + 2 * p + 1, O - 8 : O, :] = a
            y[H + 2 * p, O + B : O + B + 8, :] = b
            y[H + 2 * p + 1, O + B : O + B + 8, :] = pltpu.roll(b, 4, 0)
        for i in range(H):
            own_up = pltpu.roll(y[R + i, O - 8 : O + B + 8, :], 32, 1)
            far_up = pltpu.roll(lrow[phase, 0], (B - 32 * i) % B, 1) * ok_north
            y[i, O - 8 : O + B + 8, :] = jnp.where(lane_e < 32, far_up, own_up)
            own_down = pltpu.roll(y[H + i, O - 8 : O + B + 8, :], B - 32, 1)
            far_down = pltpu.roll(lrow[phase, 1], (96 - 32 * i) % B, 1) * ok_south
            y[H + R + i, O - 8 : O + B + 8, :] = jnp.where(
                lane_e >= 96, far_down, own_down
            )

    def keep(k, r, value):
        terms[pl.ds(pl.multiple_of(r * B, B), B), k * B : (k + 1) * B] = value.astype(BF16)

    def step(src, dst, k, scaled):
        reach = K - k
        first, count = (O - 8, CE) if reach else (O, B)
        size = 48 if reach else 64
        for at in range(0, count, size):
            step_block(src, dst, k, scaled, first + at, size)

    def step_block(src, dst, k, scaled, first, size):
        reach = K - k
        lo, hi = max(first, O), min(first + size, O + B)

        def sums(r):
            mid_ = src[r, first : first + size, :]
            low = src[r, first - 1 : first - 1 + size, :]
            high = src[r, first + 1 : first + 1 + size, :]
            return mid_ + high, low + high, mid_ + low

        def advance(r, carried):
            e0, e1, f1 = carried
            e2, f2, h2 = sums(r + 1)
            a = coef[r, first - O + 8 : first - O + 8 + size, :]
            total = a * (e0 + f1 + h2)
            if k == 1:
                value = 0.5 * total
            else:
                value = total - dst[r, first : first + size, :]
            dst[r, first : first + size, :] = value
            return (e1, e2, f2), value

        def outer(r, carried):
            return advance(r, carried)[0]

        def inner(r, carried):
            carried, value = advance(r, carried)
            value = value[lo - first : hi - first]
            if scaled:
                value = value * scale[r, lo - O + 8 : hi - O + 8, :]
            at = pl.multiple_of((r - H) * B + lo - O, 8)
            terms[pl.ds(at, hi - lo), k * B : (k + 1) * B] = value.astype(BF16)
            return carried

        low = H - reach
        e0 = sums(low - 1)[0]
        e1, f1, _ = sums(low)
        carried = (e0, e1, f1)
        if reach:
            carried = lax.fori_loop(low, H, outer, carried, unroll=reach)
        carried = lax.fori_loop(H, H + R, inner, carried, unroll=8)
        if reach:
            lax.fori_loop(H + R, H + R + reach, outer, carried, unroll=reach)

    for copy in first_halo:
        copy.wait()
    assemble(0, yb, 1.0, 1.0)

    def start_row(r, _):
        x = yb[r, O - 8 : O + B + 8, :]
        ya[r, O - 8 : O + B + 8, :] = (-0.5 * coef[r] * scale[r]) * x
        return 0

    lax.fori_loop(0, RE, start_row, 0, unroll=4)

    def keep_first(r, _):
        keep(0, r, ya[H + r, O : O + B, :] * scale[H + r, 8 : 8 + B, :])
        return 0

    lax.fori_loop(0, R, keep_first, 0, unroll=4)
    step(ya, yb, 1, True)
    step(yb, ya, 2, True)
    step(ya, yb, 3, True)
    step(yb, ya, 4, True)

    cot_in.wait()
    widen(cot_v, cf)

    def mix(p):
        at = pl.ds(pl.multiple_of(2 * p * B, 2 * B), 2 * B)
        mixed = lax.dot_general(wf[...], terms[at, :], NT, preferred_element_type=F32)
        act = jnp.tanh(mixed)
        cot = jnp.concatenate([rows_of(cf, 2 * p), rows_of(cf, 2 * p + 1)], axis=1)
        gcat[:, at] = (cot * (1.0 - act * act)).astype(BF16)

    def turn_grad(r):
        grad = gcat[:, pl.ds(pl.multiple_of(r * B, B), B)].astype(F32)
        w = -0.5 * coef[H + r, 8 : 8 + B, :] * scale[H + r, 8 : 8 + B, :]
        ya[H + r, O : O + B, :] = w * grad.T

    def grad_rows(first, count):
        for p in range(first // 2, (first + count) // 2):
            mix(p)
        for r in range(first, first + count):
            turn_grad(r)

    second_halo = halo_copies(1)
    send_chunks(1, ya, second_halo, grad_rows)

    chunk = 8 * B
    acc = None
    for n in range(R * B // chunk):
        part = jnp.dot(
            gcat[:, n * chunk : (n + 1) * chunk],
            terms[n * chunk : (n + 1) * chunk, :],
            preferred_element_type=F32,
        )
        acc = part if acc is None else acc + part
    lane_c = lax.broadcasted_iota(jnp.int32, (C, B), 1) // C
    folded = []
    for k in range(K + 1):
        tot = None
        for g in range(RG):
            piece = acc[g * C : (g + 1) * C, k * B : (k + 1) * B]
            tot = piece if tot is None else jnp.where(lane_c == g, piece, tot)
        tot = tot + pltpu.roll(tot, 64, 1)
        tot = tot + pltpu.roll(tot, 32, 1)
        folded.append(tot)
    head = folded[0]
    for k in range(1, K):
        head = jnp.where(lane_c == k, folded[k], head)
    tail = folded[K][0:8]
    for g in range(1, RG):
        tail = jnp.where(lane_c[0:8] == g, folded[K][8 * g : 8 * g + 8], tail)
    grid_cells = n_lat * n_lon * B * B
    own[0, 0:C, :] = head * (1.0 / math.sqrt(grid_cells))
    own[0, C : C + 8, :] = tail * (1.0 / math.sqrt(grid_cells))

    def lon_copy(off):
        return remote(
            own.at[0], ar1.at[lon], ar1_send.at[off], ar1_recv.at[lon],
            lat, lax.rem(lon + off, n_lon),
        )

    def lon_wait(off):
        q = lax.rem(lon + n_lon - off, n_lon)
        return remote(own.at[0], ar1.at[q], ar1_send.at[off], ar1_recv.at[q], lat, q)

    def lat_copy(off):
        return remote(
            own.at[1], ar2.at[lat], ar2_send.at[off], ar2_recv.at[lat],
            lax.rem(lat + off, n_lat), lon,
        )

    def lat_wait(off):
        q = lax.rem(lat + n_lat - off, n_lat)
        return remote(own.at[1], ar2.at[q], ar2_send.at[off], ar2_recv.at[q], q, lon)

    def run(count, act):
        def body(off, _):
            act(off)
            return 0

        lax.fori_loop(1, count, body, 0)

    run(n_lon, lambda off: lon_copy(off).start())
    ar1[lon] = own[0]

    for copy in second_halo:
        copy.wait()
    assemble(1, ya, north_ok, south_ok)

    def keep_grad(r, _):
        keep(0, r, ya[H + r, O : O + B, :])
        return 0

    lax.fori_loop(0, R, keep_grad, 0, unroll=4)
    step(ya, yb, 1, False)
    step(yb, ya, 2, False)

    run(n_lon, lambda off: lon_wait(off).wait())
    total = ar1[0]
    for q in range(1, n_lon):
        total = total + ar1[q]
    own[1] = total
    run(n_lat, lambda off: lat_copy(off).start())
    ar2[lat] = total

    step(ya, yb, 3, False)
    step(yb, ya, 4, False)

    def finish(p, _):
        t = terms[pl.ds(pl.multiple_of(2 * p * B, 2 * B), 2 * B), :]
        res = lax.dot_general(wb[...], t, NT, preferred_element_type=F32)
        for j in range(2):
            for g in range(RG):
                row = R * g + 2 * p + j
                s = jnp.broadcast_to(snat[pl.ds(row, 1), :], (C, B))
                part = res[g * C : (g + 1) * C, j * B : (j + 1) * B]
                xf[pl.ds(row, C, stride=B), :] = part * s
        return 0

    lax.fori_loop(0, R // 2, finish, 0, unroll=4)

    def narrow(c, _):
        out_v[c] = xf[pl.ds(pl.multiple_of(c * B, B), B), :].astype(BF16)
        return 0

    lax.fori_loop(0, C, narrow, 0, unroll=4)
    out_copy = pltpu.make_async_copy(out_v, out_hbm, out_sem)
    out_copy.start()

    run(n_lat, lambda off: lat_wait(off).wait())
    total = ar2[0]
    for q in range(1, n_lat):
        total = total + ar2[q]
    flat = total[0:C].T
    for k in range(K):
        wg_ref[k] = flat[k * C : (k + 1) * C, :]
    last = total[C : C + 8]
    last = jnp.concatenate(
        [last if g == 0 else pltpu.roll(last, B - C * g, 1) for g in range(RG)], axis=0
    )
    wg_ref[K] = last.T[0:C, :]
    out_copy.wait()


def solution(mesh):
    n_lat, n_lon = mesh.shape["lat"], mesh.shape["lon"]
    hbm = pl.BlockSpec(memory_space=pl.ANY)
    sem = pltpu.SemaphoreType.DMA

    def local(features, cotangent, sea_mask, weights):
        return pl.pallas_call(
            functools.partial(kernel, n_lat, n_lon),
            out_shape=(
                jax.ShapeDtypeStruct((C, B, B), BF16),
                jax.ShapeDtypeStruct((K + 1, C, C), F32),
            ),
            in_specs=[hbm] * 4,
            out_specs=(hbm, pl.BlockSpec(memory_space=pltpu.VMEM)),
            scratch_shapes=[
                pltpu.VMEM((C, B, B), BF16),
                pltpu.VMEM((C, B, B), BF16),
                pltpu.VMEM((B, B), jnp.int32),
                pltpu.VMEM((K + 1, C, C), BF16),
                pltpu.VMEM((C * B, B), F32),
                pltpu.VMEM((C * B, B), F32),
                pltpu.VMEM((C, B, B), BF16),
                pltpu.VMEM((RE, CP, B), F32),
                pltpu.VMEM((RE, CP, B), F32),
                pltpu.VMEM((RE, CE, B), F32),
                pltpu.VMEM((RE, CE, B), F32),
                pltpu.VMEM((R * B, (K + 1) * B), BF16),
                pltpu.VMEM((B, R * B), BF16),
                pltpu.VMEM((4, 8, B), F32),
                pltpu.VMEM((8, 8, B), F32),
                pltpu.VMEM((2, CP, B), F32),
                pltpu.VMEM((CE, 2 * B), F32),
                pltpu.VMEM((B, B), F32),
                pltpu.VMEM((B, (K + 1) * B), BF16),
                pltpu.VMEM((B, (K + 1) * B), BF16),
                pltpu.VMEM((CE, 2 * B), BF16),
                pltpu.VMEM((2, 2, B, B), F32),
                pltpu.VMEM((2, 2, R // 2, 8, B), F32),
                pltpu.VMEM((2, 2, CE, B), F32),
                pltpu.VMEM((2, 2, R // 2, 8, B), F32),
                pltpu.VMEM((2, C + 8, B), F32),
                pltpu.VMEM((n_lon, C + 8, B), F32),
                pltpu.VMEM((n_lat, C + 8, B), F32),
                sem((4,)), sem(()), sem((8,)), sem((8,)), sem((2, 16)), sem((2, 16)),
                sem((n_lon,)), sem((n_lon,)), sem((n_lat,)), sem((n_lat,)),
            ],
            compiler_params=pltpu.CompilerParams(
                collective_id=0, has_side_effects=True, vmem_limit_bytes=56 << 20
            ),
        )(features, cotangent, sea_mask, weights)

    placed = (P(None, "lat", "lon"), P(None, "lat", "lon"), P("lat", "lon"), P())
    return jax.shard_map(
        local, mesh=mesh, in_specs=placed, out_specs=(P(None, "lat", "lon"), P()), check_vma=False
    )
```

```python
import functools
import math

import jax
import jax.numpy as jnp
from jax import lax
from jax.experimental import pallas as pl
from jax.experimental.pallas import tpu as pltpu
from jax.sharding import PartitionSpec as P

K = 4
C = 32
B = 128
RG = 4
R = B // RG
H = 4
RE = R + 2 * H
CE = B + 16
CP = CE + 16
O = 16
F32 = jnp.float32
BF16 = jnp.bfloat16
NT = (((1,), (1,)), ((), ()))


def kernel(
    n_lat, n_lon,
    feat_hbm, cot_hbm, mask_hbm, w_hbm,
    terms, snat, wb, sum_ref,
    feat_v, cot_v, mask_v, w_v, xf, cf,
    ya, yb, coef, scale, gcat,
    mtx, mrx, sm, vm, wf, sel,
    pack, cpack, lrow, lcol, own, ar1, ar2,
    in_sem, mask_send, mask_recv, halo_send, halo_recv,
    ar1_send, ar1_recv, ar2_send, ar2_recv,
):
    lat = lax.axis_index("lat")
    lon = lax.axis_index("lon")
    north, south = lax.rem(lat + n_lat - 1, n_lat), lax.rem(lat + 1, n_lat)
    west, east = lax.rem(lon + n_lon - 1, n_lon), lax.rem(lon + 1, n_lon)

    feat_in = pltpu.make_async_copy(feat_hbm, feat_v, in_sem.at[0])
    cot_in = pltpu.make_async_copy(cot_hbm, cot_v, in_sem.at[1])
    mask_in = pltpu.make_async_copy(mask_hbm, mask_v, in_sem.at[2])
    w_in = pltpu.make_async_copy(w_hbm, w_v, in_sem.at[3])
    mask_in.start()
    feat_in.start()
    w_in.start()
    cot_in.start()

    barrier = pltpu.get_barrier_semaphore()

    def greet(i, j):
        pl.semaphore_signal(
            barrier, inc=1, device_id=(i, j), device_id_type=pl.DeviceIdType.MESH
        )

    for i in (north, south):
        for j in (west, east):
            greet(i, j)

    def greet_lon(off, _):
        greet(lat, lax.rem(lon + off, n_lon))
        return 0

    def greet_lat(off, _):
        greet(lax.rem(lat + off, n_lat), lon)
        return 0

    lax.fori_loop(1, n_lon, greet_lon, 0)
    lax.fori_loop(1, n_lat, greet_lat, 0)

    row_i = lax.broadcasted_iota(jnp.int32, (B, B), 0)
    col_i = lax.broadcasted_iota(jnp.int32, (B, B), 1)
    sel_r = lax.broadcasted_iota(jnp.int32, (CE, 2 * B), 0)
    sel_c = lax.broadcasted_iota(jnp.int32, (CE, 2 * B), 1)
    inside = (sel_r >= 8) & (sel_r < 8 + B) & (sel_c == sel_r - 8)
    left = (sel_r < 8) & (sel_c == 2 * B - 8 + sel_r)
    right = (sel_r >= 8 + B) & (sel_c == sel_r - 8)
    sel[...] = (inside | left | right).astype(F32).astype(BF16)

    mask_in.wait()
    flags = mask_v[...].astype(F32)
    turned_flags = flags.T
    mtx[0] = flags[B - 8 :]
    mtx[1] = flags[:8]
    mtx[2] = turned_flags[B - 8 :]
    mtx[3] = turned_flags[:8]
    pl.semaphore_wait(barrier, 4 + (n_lon - 1) + (n_lat - 1))

    def remote(src, dst, send, recv, i, j):
        return pltpu.make_async_remote_copy(
            src_ref=src, dst_ref=dst, send_sem=send, recv_sem=recv,
            device_id=(i, j), device_id_type=pl.DeviceIdType.MESH,
        )

    mid = pl.ds(8, B)
    above, below = pl.ds(0, 8), pl.ds(8 + B, 8)
    mask_plan = (
        (2, 0, lat, east),
        (3, 1, lat, west),
        (0, 2, south, lon),
        (1, 3, north, lon),
        (0, 4, south, east),
        (0, 5, south, west),
        (1, 6, north, east),
        (1, 7, north, west),
    )
    mask_copies = [
        remote(mtx.at[src], mrx.at[n], mask_send.at[n], mask_recv.at[n], i, j)
        for src, n, i, j in mask_plan
    ]
    for copy in mask_copies:
        copy.start()

    lane = lax.broadcasted_iota(jnp.int32, (B, B), 1)

    def halo_copies(phase):
        plan = (
            (pack.at[phase, 0], lrow.at[phase, 0, mid], south, lon),
            (pack.at[phase, 1], lrow.at[phase, 1, mid], north, lon),
            (pack.at[phase, 0, pl.ds(B - 8, 8)], lrow.at[phase, 0, above], south, east),
            (pack.at[phase, 0, pl.ds(0, 8)], lrow.at[phase, 0, below], south, west),
            (pack.at[phase, 1, pl.ds(B - 8, 8)], lrow.at[phase, 1, above], north, east),
            (pack.at[phase, 1, pl.ds(0, 8)], lrow.at[phase, 1, below], north, west),
        ) + tuple(
            (cpack.at[phase, side, at], lcol.at[phase, side, at], lat, (east, west)[side])
            for at in (pl.ds(0, 2), pl.ds(14, 2), pl.ds(2, 4), pl.ds(6, 4), pl.ds(10, 4))
            for side in range(2)
        )
        return [
            remote(src, dst, halo_send.at[phase, n], halo_recv.at[phase, n], i, j)
            for n, (src, dst, i, j) in enumerate(plan)
        ]

    def pack_rows(phase, y):
        last, first = None, None
        for i in range(H):
            a = pltpu.roll(y[H + R - H + i, O : O + B, :], (32 * i + 32) % 128, 1)
            b = pltpu.roll(y[H + i, O : O + B, :], (32 * i) % 128, 1)
            here = (lane >= 32 * i) & (lane < 32 * i + 32)
            last = a if last is None else jnp.where(here, a, last)
            first = b if first is None else jnp.where(here, b, first)
        pack[phase, 0] = last
        pack[phase, 1] = first

    half = lax.broadcasted_iota(jnp.int32, (8, B), 0) < 4

    def pack_columns(phase, y, p):
        a, b = y[H + 2 * p, O + B - 8 : O + B, :], y[H + 2 * p + 1, O + B - 8 : O + B, :]
        cpack[phase, 0, p] = jnp.where(half, pltpu.roll(a, 4, 0), b)
        a, b = y[H + 2 * p, O : O + 8, :], y[H + 2 * p + 1, O : O + 8, :]
        cpack[phase, 1, p] = jnp.where(half, a, pltpu.roll(b, 4, 0))

    def send_chunks(phase, y, copies, turn_rows):
        turn_rows(0, H)
        turn_rows(R - H, H)
        for p in (0, 1, 14, 15):
            pack_columns(phase, y, p)
        pack_rows(phase, y)
        for copy in copies[:10]:
            copy.start()
        for n in range(3):
            turn_rows(H + 8 * n, 8)
            for p in range(2 + 4 * n, 6 + 4 * n):
                pack_columns(phase, y, p)
            for copy in copies[10 + 2 * n : 12 + 2 * n]:
                copy.start()

    feat_in.wait()

    def widen(src, dst):
        def body(c, _):
            dst[pl.ds(pl.multiple_of(c * B, B), B), :] = src[c].astype(F32)
            return 0

        lax.fori_loop(0, C, body, 0, unroll=4)

    def rows_of(flat, r):
        return jnp.concatenate(
            [flat[pl.ds(R * g + r, C, stride=B), :] for g in range(RG)], axis=0
        )

    widen(feat_v, xf)

    def turn(r):
        yb[H + r, O : O + B, :] = rows_of(xf, r).T

    def turn_rows(first, count):
        for r in range(first, first + count):
            turn(r)

    first_halo = halo_copies(0)
    send_chunks(0, yb, first_halo, turn_rows)

    w_in.wait()
    block = (row_i // C) == (col_i // C)
    for k in range(K + 1):
        one = w_v[k].astype(F32)
        wide = jnp.concatenate([one] * RG, axis=1)
        full = jnp.where(block, jnp.concatenate([wide] * RG, axis=0), 0.0)
        wb[:, k * B : (k + 1) * B] = full.astype(BF16)
        wf[:, k * B : (k + 1) * B] = full.T.astype(BF16)

    for copy in mask_copies:
        copy.wait()
    north_ok = (lat > 0).astype(F32)
    south_ok = (lat < n_lat - 1).astype(F32)
    lane_e = lax.broadcasted_iota(jnp.int32, (CE, B), 1)
    sm[:, 0:8, :] = jnp.zeros((2, 8, B), F32)
    sm[:, 8 + CE :, :] = jnp.zeros((2, 8, B), F32)
    sm[0, 8:16, :] = mrx[2] * north_ok
    sm[0, 16 : 16 + B, :] = mask_v[...].astype(F32)
    sm[0, 16 + B : 24 + B, :] = mrx[3] * south_ok
    low_lanes = lane_e[0:8] < 64
    sm[1, 8:16, :] = jnp.where(low_lanes, mrx[5], mrx[4]) * north_ok
    sm[1, 16 : 16 + B, :] = jnp.concatenate(
        [mrx[1], jnp.zeros((B - 16, B), F32), mrx[0]], axis=0
    ).T
    sm[1, 16 + B : 24 + B, :] = jnp.where(low_lanes, mrx[7], mrx[6]) * south_ok

    def ring(main, side, shift, edge):
        m, s = pltpu.roll(main, shift, 1), pltpu.roll(side, shift, 1)
        at = lane_e == edge
        return jnp.where(at, s, m), jnp.where(at, m, s)

    here = [sm[t, 8 : 8 + CE, :] for t in range(2)]
    up = [sm[t, 7 : 7 + CE, :] for t in range(2)]
    down = [sm[t, 9 : 9 + CE, :] for t in range(2)]
    from_left = ring(here[0] + down[0], here[1] + down[1], 1, 0)
    from_right = ring(here[0] + up[0], here[1] + up[1], B - 1, B - 1)
    for t in range(2):
        degree = from_left[t] + from_right[t] + up[t] + down[t]
        vm[:, t * B : (t + 1) * B] = here[t] * jnp.maximum(degree, 1.0)
        if t == 0:
            snat[...] = jnp.sqrt(jnp.maximum(degree, 1.0)[8 : 8 + B])

    def spread(p, _):
        rows = jnp.concatenate(
            [
                jnp.broadcast_to(vm[pl.ds(8 - H + R * g + 2 * p + j, 1), :], (C, 2 * B))
                for j in range(2)
                for g in range(RG)
            ],
            axis=0,
        )
        v = lax.dot_general(sel[...], rows.astype(BF16), NT, preferred_element_type=F32)
        m = jnp.maximum(v, 1.0)
        rs = lax.rsqrt(m)
        a, s = jnp.where(v > 0.5, -2.0 * rs * rs, 0.0), m * rs
        for j in range(2):
            coef[2 * p + j] = a[:, j * B : (j + 1) * B]
            scale[2 * p + j] = s[:, j * B : (j + 1) * B]
        return 0

    lax.fori_loop(0, RE // 2, spread, 0, unroll=4)

    def assemble(phase, y, ok_north, ok_south):
        for p in range(R // 2):
            a, b = lcol[phase, 0, p], lcol[phase, 1, p]
            y[H + 2 * p, O - 8 : O, :] = pltpu.roll(a, 4, 0)
            y[H + 2 * p + 1, O - 8 : O, :] = a
            y[H + 2 * p, O + B : O + B + 8, :] = b
            y[H + 2 * p + 1, O + B : O + B + 8, :] = pltpu.roll(b, 4, 0)
        for i in range(H):
            own_up = pltpu.roll(y[R + i, O - 8 : O + B + 8, :], 32, 1)
            far_up = pltpu.roll(lrow[phase, 0], (B - 32 * i) % B, 1) * ok_north
            y[i, O - 8 : O + B + 8, :] = jnp.where(lane_e < 32, far_up, own_up)
            own_down = pltpu.roll(y[H + i, O - 8 : O + B + 8, :], B - 32, 1)
            far_down = pltpu.roll(lrow[phase, 1], (96 - 32 * i) % B, 1) * ok_south
            y[H + R + i, O - 8 : O + B + 8, :] = jnp.where(
                lane_e >= 96, far_down, own_down
            )

    def keep(k, r, value):
        terms[pl.ds(pl.multiple_of(r * B, B), B), k * B : (k + 1) * B] = value.astype(BF16)

    def step(src, dst, k, scaled):
        reach = K - k
        first, count = (O - 8, CE) if reach else (O, B)
        size = 48 if reach else 64
        for at in range(0, count, size):
            step_block(src, dst, k, scaled, first + at, size)

    def step_block(src, dst, k, scaled, first, size):
        reach = K - k
        lo, hi = max(first, O), min(first + size, O + B)

        def sums(r):
            mid_ = src[r, first : first + size, :]
            low = src[r, first - 1 : first - 1 + size, :]
            high = src[r, first + 1 : first + 1 + size, :]
            return mid_ + high, low + high, mid_ + low

        def advance(r, carried):
            e0, e1, f1 = carried
            e2, f2, h2 = sums(r + 1)
            a = coef[r, first - O + 8 : first - O + 8 + size, :]
            total = a * (e0 + f1 + h2)
            if k == 1:
                value = 0.5 * total
            else:
                value = total - dst[r, first : first + size, :]
            dst[r, first : first + size, :] = value
            return (e1, e2, f2), value

        def outer(r, carried):
            return advance(r, carried)[0]

        def inner(r, carried):
            carried, value = advance(r, carried)
            value = value[lo - first : hi - first]
            if scaled:
                value = value * scale[r, lo - O + 8 : hi - O + 8, :]
            at = pl.multiple_of((r - H) * B + lo - O, 8)
            terms[pl.ds(at, hi - lo), k * B : (k + 1) * B] = value.astype(BF16)
            return carried

        low = H - reach
        e0 = sums(low - 1)[0]
        e1, f1, _ = sums(low)
        carried = (e0, e1, f1)
        if reach:
            carried = lax.fori_loop(low, H, outer, carried, unroll=reach)
        carried = lax.fori_loop(H, H + R, inner, carried, unroll=8)
        if reach:
            lax.fori_loop(H + R, H + R + reach, outer, carried, unroll=reach)

    for copy in first_halo:
        copy.wait()
    assemble(0, yb, 1.0, 1.0)

    def start_row(r, _):
        x = yb[r, O - 8 : O + B + 8, :]
        ya[r, O - 8 : O + B + 8, :] = (-0.5 * coef[r] * scale[r]) * x
        return 0

    lax.fori_loop(0, RE, start_row, 0, unroll=4)

    def keep_first(r, _):
        keep(0, r, ya[H + r, O : O + B, :] * scale[H + r, 8 : 8 + B, :])
        return 0

    lax.fori_loop(0, R, keep_first, 0, unroll=4)
    step(ya, yb, 1, True)
    step(yb, ya, 2, True)
    step(ya, yb, 3, True)
    step(yb, ya, 4, True)

    cot_in.wait()
    widen(cot_v, cf)

    def mix(p):
        at = pl.ds(pl.multiple_of(2 * p * B, 2 * B), 2 * B)
        mixed = lax.dot_general(wf[...], terms[at, :], NT, preferred_element_type=F32)
        act = jnp.tanh(mixed)
        cot = jnp.concatenate([rows_of(cf, 2 * p), rows_of(cf, 2 * p + 1)], axis=1)
        gcat[:, at] = (cot * (1.0 - act * act)).astype(BF16)

    def turn_grad(r):
        grad = gcat[:, pl.ds(pl.multiple_of(r * B, B), B)].astype(F32)
        w = -0.5 * coef[H + r, 8 : 8 + B, :] * scale[H + r, 8 : 8 + B, :]
        ya[H + r, O : O + B, :] = w * grad.T

    def grad_rows(first, count):
        for p in range(first // 2, (first + count) // 2):
            mix(p)
        for r in range(first, first + count):
            turn_grad(r)

    second_halo = halo_copies(1)
    send_chunks(1, ya, second_halo, grad_rows)

    chunk = 8 * B
    acc = None
    for n in range(R * B // chunk):
        part = jnp.dot(
            gcat[:, n * chunk : (n + 1) * chunk],
            terms[n * chunk : (n + 1) * chunk, :],
            preferred_element_type=F32,
        )
        acc = part if acc is None else acc + part
    lane_c = lax.broadcasted_iota(jnp.int32, (C, B), 1) // C
    folded = []
    for k in range(K + 1):
        tot = None
        for g in range(RG):
            piece = acc[g * C : (g + 1) * C, k * B : (k + 1) * B]
            tot = piece if tot is None else jnp.where(lane_c == g, piece, tot)
        tot = tot + pltpu.roll(tot, 64, 1)
        tot = tot + pltpu.roll(tot, 32, 1)
        folded.append(tot)
    head = folded[0]
    for k in range(1, K):
        head = jnp.where(lane_c == k, folded[k], head)
    tail = folded[K][0:8]
    for g in range(1, RG):
        tail = jnp.where(lane_c[0:8] == g, folded[K][8 * g : 8 * g + 8], tail)
    grid_cells = n_lat * n_lon * B * B
    own[0, 0:C, :] = head * (1.0 / math.sqrt(grid_cells))
    own[0, C : C + 8, :] = tail * (1.0 / math.sqrt(grid_cells))

    def lon_copy(off):
        return remote(
            own.at[0], ar1.at[lon], ar1_send.at[off], ar1_recv.at[lon],
            lat, lax.rem(lon + off, n_lon),
        )

    def lon_wait(off):
        q = lax.rem(lon + n_lon - off, n_lon)
        return remote(own.at[0], ar1.at[q], ar1_send.at[off], ar1_recv.at[q], lat, q)

    def lat_copy(off):
        return remote(
            own.at[1], ar2.at[lat], ar2_send.at[off], ar2_recv.at[lat],
            lax.rem(lat + off, n_lat), lon,
        )

    def lat_wait(off):
        q = lax.rem(lat + n_lat - off, n_lat)
        return remote(own.at[1], ar2.at[q], ar2_send.at[off], ar2_recv.at[q], q, lon)

    def run(count, act):
        def body(off, _):
            act(off)
            return 0

        lax.fori_loop(1, count, body, 0)

    run(n_lon, lambda off: lon_copy(off).start())
    ar1[lon] = own[0]

    for copy in second_halo:
        copy.wait()
    assemble(1, ya, north_ok, south_ok)

    def keep_grad(r, _):
        keep(0, r, ya[H + r, O : O + B, :])
        return 0

    lax.fori_loop(0, R, keep_grad, 0, unroll=4)
    step(ya, yb, 1, False)

    run(n_lon, lambda off: lon_wait(off).wait())
    total = ar1[0]
    for q in range(1, n_lon):
        total = total + ar1[q]
    own[1] = total
    run(n_lat, lambda off: lat_copy(off).start())
    ar2[lat] = total

    step(yb, ya, 2, False)
    step(ya, yb, 3, False)
    step(yb, ya, 4, False)

    run(n_lat, lambda off: lat_wait(off).wait())
    total = ar2[0]
    for q in range(1, n_lat):
        total = total + ar2[q]
    sum_ref[...] = total


def close(terms, snat, wb, sum_ref, out_hbm, wg_ref, xf, out_v, out_sem):
    def finish(p, _):
        t = terms[pl.ds(pl.multiple_of(2 * p * B, 2 * B), 2 * B), :]
        res = lax.dot_general(wb[...], t, NT, preferred_element_type=F32)
        for j in range(2):
            for g in range(RG):
                row = R * g + 2 * p + j
                s = jnp.broadcast_to(snat[pl.ds(row, 1), :], (C, B))
                part = res[g * C : (g + 1) * C, j * B : (j + 1) * B]
                xf[pl.ds(row, C, stride=B), :] = part * s
        return 0

    lax.fori_loop(0, R // 2, finish, 0, unroll=4)

    part = C // 4
    copies = [
        pltpu.make_async_copy(
            out_v.at[pl.ds(n * part, part)], out_hbm.at[pl.ds(n * part, part)], out_sem.at[n]
        )
        for n in range(4)
    ]
    for n in range(4):
        for c in range(n * part, (n + 1) * part):
            out_v[c] = xf[c * B : (c + 1) * B, :].astype(BF16)
        copies[n].start()
    total = sum_ref[...]
    flat = total[0:C].T
    for k in range(K):
        wg_ref[k] = flat[k * C : (k + 1) * C, :]
    last = total[C : C + 8]
    last = jnp.concatenate(
        [last if g == 0 else pltpu.roll(last, B - C * g, 1) for g in range(RG)], axis=0
    )
    wg_ref[K] = last.T[0:C, :]
    for copy in copies:
        copy.wait()


def solution(mesh):
    n_lat, n_lon = mesh.shape["lat"], mesh.shape["lon"]
    hbm = pl.BlockSpec(memory_space=pltpu.HBM)
    sem = pltpu.SemaphoreType.DMA

    def local(features, cotangent, sea_mask, weights):
        vmem = pl.BlockSpec(memory_space=pltpu.VMEM)
        carried = (
            pltpu.VMEM((R * B, (K + 1) * B), BF16),
            pltpu.VMEM((B, B), F32),
            pltpu.VMEM((B, (K + 1) * B), BF16),
            pltpu.VMEM((C + 8, B), F32),
        )
        carried = pl.pallas_call(
            functools.partial(kernel, n_lat, n_lon),
            out_shape=carried,
            in_specs=[hbm] * 4,
            out_specs=(vmem,) * 4,
            scratch_shapes=[
                pltpu.VMEM((C, B, B), BF16),
                pltpu.VMEM((C, B, B), BF16),
                pltpu.VMEM((B, B), jnp.int32),
                pltpu.VMEM((K + 1, C, C), BF16),
                pltpu.VMEM((C * B, B), F32),
                pltpu.VMEM((C * B, B), F32),
                pltpu.VMEM((RE, CP, B), F32),
                pltpu.VMEM((RE, CP, B), F32),
                pltpu.VMEM((RE, CE, B), F32),
                pltpu.VMEM((RE, CE, B), F32),
                pltpu.VMEM((B, R * B), BF16),
                pltpu.VMEM((4, 8, B), F32),
                pltpu.VMEM((8, 8, B), F32),
                pltpu.VMEM((2, CP, B), F32),
                pltpu.VMEM((CE, 2 * B), F32),
                pltpu.VMEM((B, (K + 1) * B), BF16),
                pltpu.VMEM((CE, 2 * B), BF16),
                pltpu.VMEM((2, 2, B, B), F32),
                pltpu.VMEM((2, 2, R // 2, 8, B), F32),
                pltpu.VMEM((2, 2, CE, B), F32),
                pltpu.VMEM((2, 2, R // 2, 8, B), F32),
                pltpu.VMEM((2, C + 8, B), F32),
                pltpu.VMEM((n_lon, C + 8, B), F32),
                pltpu.VMEM((n_lat, C + 8, B), F32),
                sem((4,)), sem((8,)), sem((8,)), sem((2, 16)), sem((2, 16)),
                sem((n_lon,)), sem((n_lon,)), sem((n_lat,)), sem((n_lat,)),
            ],
            compiler_params=pltpu.CompilerParams(
                collective_id=0, has_side_effects=True, vmem_limit_bytes=40 << 20
            ),
        )(features, cotangent, sea_mask, weights)
        return pl.pallas_call(
            close,
            out_shape=(
                jax.ShapeDtypeStruct((C, B, B), BF16),
                jax.ShapeDtypeStruct((K + 1, C, C), F32),
            ),
            in_specs=[vmem] * 4,
            out_specs=(hbm, vmem),
            scratch_shapes=[pltpu.VMEM((C * B, B), F32), pltpu.VMEM((C, B, B), BF16), sem((4,))],
            compiler_params=pltpu.CompilerParams(vmem_limit_bytes=16 << 20),
        )(*carried)

    placed = (P(None, "lat", "lon"), P(None, "lat", "lon"), P("lat", "lon"), P())
    return jax.shard_map(
        local, mesh=mesh, in_specs=placed, out_specs=(P(None, "lat", "lon"), P()), check_vma=False
    )
```

```python
import functools
import math

import jax
import jax.numpy as jnp
from jax import lax
from jax.experimental import pallas as pl
from jax.experimental.pallas import tpu as pltpu
from jax.sharding import PartitionSpec as P

K = 4
C = 32
B = 128
RG = 4
R = B // RG
H = 4
RE = R + 2 * H
CE = B + 16
CP = CE + 16
O = 16
F32 = jnp.float32
BF16 = jnp.bfloat16
NT = (((1,), (1,)), ((), ()))


def kernel(
    n_lat, n_lon,
    feat_hbm, cot_hbm, mask_hbm, w_hbm,
    terms, snat, wb, sum_ref,
    feat_v, cot_v, mask_v, w_v, xf, cf,
    ya, yb, coef, scale, gcat,
    mtx, mrx, sm, vm, wf, sel,
    pack, cpack, lrow, lcol, own, ar1, ar2,
    in_sem, mask_send, mask_recv, halo_send, halo_recv,
    ar1_send, ar1_recv, ar2_send, ar2_recv,
):
    lat = lax.axis_index("lat")
    lon = lax.axis_index("lon")
    north, south = lax.rem(lat + n_lat - 1, n_lat), lax.rem(lat + 1, n_lat)
    west, east = lax.rem(lon + n_lon - 1, n_lon), lax.rem(lon + 1, n_lon)

    feat_in = pltpu.make_async_copy(feat_hbm, feat_v, in_sem.at[0])
    cot_in = pltpu.make_async_copy(cot_hbm, cot_v, in_sem.at[1])
    mask_in = pltpu.make_async_copy(mask_hbm, mask_v, in_sem.at[2])
    w_in = pltpu.make_async_copy(w_hbm, w_v, in_sem.at[3])
    mask_in.start()
    feat_in.start()
    w_in.start()
    cot_in.start()

    barrier = pltpu.get_barrier_semaphore()

    def greet(i, j):
        pl.semaphore_signal(
            barrier, inc=1, device_id=(i, j), device_id_type=pl.DeviceIdType.MESH
        )

    for i in (north, south):
        for j in (west, east):
            greet(i, j)

    def greet_lon(off, _):
        greet(lat, lax.rem(lon + off, n_lon))
        return 0

    def greet_lat(off, _):
        greet(lax.rem(lat + off, n_lat), lon)
        return 0

    lax.fori_loop(1, n_lon, greet_lon, 0)
    lax.fori_loop(1, n_lat, greet_lat, 0)

    row_i = lax.broadcasted_iota(jnp.int32, (B, B), 0)
    col_i = lax.broadcasted_iota(jnp.int32, (B, B), 1)
    sel_r = lax.broadcasted_iota(jnp.int32, (CE, 2 * B), 0)
    sel_c = lax.broadcasted_iota(jnp.int32, (CE, 2 * B), 1)
    inside = (sel_r >= 8) & (sel_r < 8 + B) & (sel_c == sel_r - 8)
    left = (sel_r < 8) & (sel_c == 2 * B - 8 + sel_r)
    right = (sel_r >= 8 + B) & (sel_c == sel_r - 8)
    sel[...] = (inside | left | right).astype(F32).astype(BF16)

    mask_in.wait()
    flags = mask_v[...].astype(F32)
    turned_flags = flags.T
    mtx[0] = flags[B - 8 :]
    mtx[1] = flags[:8]
    mtx[2] = turned_flags[B - 8 :]
    mtx[3] = turned_flags[:8]
    pl.semaphore_wait(barrier, 4 + (n_lon - 1) + (n_lat - 1))

    def remote(src, dst, send, recv, i, j):
        return pltpu.make_async_remote_copy(
            src_ref=src, dst_ref=dst, send_sem=send, recv_sem=recv,
            device_id=(i, j), device_id_type=pl.DeviceIdType.MESH,
        )

    mid = pl.ds(8, B)
    above, below = pl.ds(0, 8), pl.ds(8 + B, 8)
    mask_plan = (
        (2, 0, lat, east),
        (3, 1, lat, west),
        (0, 2, south, lon),
        (1, 3, north, lon),
        (0, 4, south, east),
        (0, 5, south, west),
        (1, 6, north, east),
        (1, 7, north, west),
    )
    mask_copies = [
        remote(mtx.at[src], mrx.at[n], mask_send.at[n], mask_recv.at[n], i, j)
        for src, n, i, j in mask_plan
    ]
    for copy in mask_copies:
        copy.start()

    lane = lax.broadcasted_iota(jnp.int32, (B, B), 1)

    def halo_copies(phase):
        plan = (
            (pack.at[phase, 0], lrow.at[phase, 0, mid], south, lon),
            (pack.at[phase, 1], lrow.at[phase, 1, mid], north, lon),
            (pack.at[phase, 0, pl.ds(B - 8, 8)], lrow.at[phase, 0, above], south, east),
            (pack.at[phase, 0, pl.ds(0, 8)], lrow.at[phase, 0, below], south, west),
            (pack.at[phase, 1, pl.ds(B - 8, 8)], lrow.at[phase, 1, above], north, east),
            (pack.at[phase, 1, pl.ds(0, 8)], lrow.at[phase, 1, below], north, west),
        ) + tuple(
            (cpack.at[phase, side, at], lcol.at[phase, side, at], lat, (east, west)[side])
            for at in (pl.ds(0, 2), pl.ds(14, 2), pl.ds(2, 4), pl.ds(6, 4), pl.ds(10, 4))
            for side in range(2)
        )
        return [
            remote(src, dst, halo_send.at[phase, n], halo_recv.at[phase, n], i, j)
            for n, (src, dst, i, j) in enumerate(plan)
        ]

    def pack_rows(phase, y):
        last, first = None, None
        for i in range(H):
            a = pltpu.roll(y[H + R - H + i, O : O + B, :], (32 * i + 32) % 128, 1)
            b = pltpu.roll(y[H + i, O : O + B, :], (32 * i) % 128, 1)
            here = (lane >= 32 * i) & (lane < 32 * i + 32)
            last = a if last is None else jnp.where(here, a, last)
            first = b if first is None else jnp.where(here, b, first)
        pack[phase, 0] = last
        pack[phase, 1] = first

    half = lax.broadcasted_iota(jnp.int32, (8, B), 0) < 4

    def pack_columns(phase, y, p):
        a, b = y[H + 2 * p, O + B - 8 : O + B, :], y[H + 2 * p + 1, O + B - 8 : O + B, :]
        cpack[phase, 0, p] = jnp.where(half, pltpu.roll(a, 4, 0), b)
        a, b = y[H + 2 * p, O : O + 8, :], y[H + 2 * p + 1, O : O + 8, :]
        cpack[phase, 1, p] = jnp.where(half, a, pltpu.roll(b, 4, 0))

    def send_chunks(phase, y, copies, turn_rows):
        turn_rows(0, H)
        turn_rows(R - H, H)
        for p in (0, 1, 14, 15):
            pack_columns(phase, y, p)
        pack_rows(phase, y)
        for copy in copies[:10]:
            copy.start()
        for n in range(3):
            turn_rows(H + 8 * n, 8)
            for p in range(2 + 4 * n, 6 + 4 * n):
                pack_columns(phase, y, p)
            for copy in copies[10 + 2 * n : 12 + 2 * n]:
                copy.start()

    feat_in.wait()

    def widen(src, dst):
        def body(c, _):
            dst[pl.ds(pl.multiple_of(c * B, B), B), :] = src[c].astype(F32)
            return 0

        lax.fori_loop(0, C, body, 0, unroll=4)

    def rows_of(flat, r):
        return jnp.concatenate(
            [flat[pl.ds(R * g + r, C, stride=B), :] for g in range(RG)], axis=0
        )

    widen(feat_v, xf)

    def turn(r):
        yb[H + r, O : O + B, :] = rows_of(xf, r).T

    def turn_rows(first, count):
        for r in range(first, first + count):
            turn(r)

    first_halo = halo_copies(0)
    send_chunks(0, yb, first_halo, turn_rows)

    w_in.wait()
    block = (row_i // C) == (col_i // C)
    for k in range(K + 1):
        one = w_v[k].astype(F32)
        wide = jnp.concatenate([one] * RG, axis=1)
        full = jnp.where(block, jnp.concatenate([wide] * RG, axis=0), 0.0)
        wb[:, k * B : (k + 1) * B] = full.astype(BF16)
        wf[:, k * B : (k + 1) * B] = full.T.astype(BF16)

    for copy in mask_copies:
        copy.wait()
    north_ok = (lat > 0).astype(F32)
    south_ok = (lat < n_lat - 1).astype(F32)
    lane_e = lax.broadcasted_iota(jnp.int32, (CE, B), 1)
    sm[:, 0:8, :] = jnp.zeros((2, 8, B), F32)
    sm[:, 8 + CE :, :] = jnp.zeros((2, 8, B), F32)
    sm[0, 8:16, :] = mrx[2] * north_ok
    sm[0, 16 : 16 + B, :] = mask_v[...].astype(F32)
    sm[0, 16 + B : 24 + B, :] = mrx[3] * south_ok
    low_lanes = lane_e[0:8] < 64
    sm[1, 8:16, :] = jnp.where(low_lanes, mrx[5], mrx[4]) * north_ok
    sm[1, 16 : 16 + B, :] = jnp.concatenate(
        [mrx[1], jnp.zeros((B - 16, B), F32), mrx[0]], axis=0
    ).T
    sm[1, 16 + B : 24 + B, :] = jnp.where(low_lanes, mrx[7], mrx[6]) * south_ok

    def ring(main, side, shift, edge):
        m, s = pltpu.roll(main, shift, 1), pltpu.roll(side, shift, 1)
        at = lane_e == edge
        return jnp.where(at, s, m), jnp.where(at, m, s)

    here = [sm[t, 8 : 8 + CE, :] for t in range(2)]
    up = [sm[t, 7 : 7 + CE, :] for t in range(2)]
    down = [sm[t, 9 : 9 + CE, :] for t in range(2)]
    from_left = ring(here[0] + down[0], here[1] + down[1], 1, 0)
    from_right = ring(here[0] + up[0], here[1] + up[1], B - 1, B - 1)
    for t in range(2):
        degree = from_left[t] + from_right[t] + up[t] + down[t]
        vm[:, t * B : (t + 1) * B] = here[t] * jnp.maximum(degree, 1.0)
        if t == 0:
            snat[...] = jnp.sqrt(jnp.maximum(degree, 1.0)[8 : 8 + B])

    def spread(p, _):
        rows = jnp.concatenate(
            [
                jnp.broadcast_to(vm[pl.ds(8 - H + R * g + 2 * p + j, 1), :], (C, 2 * B))
                for j in range(2)
                for g in range(RG)
            ],
            axis=0,
        )
        v = lax.dot_general(sel[...], rows.astype(BF16), NT, preferred_element_type=F32)
        m = jnp.maximum(v, 1.0)
        rs = lax.rsqrt(m)
        a, s = jnp.where(v > 0.5, -2.0 * rs * rs, 0.0), m * rs
        for j in range(2):
            coef[2 * p + j] = a[:, j * B : (j + 1) * B]
            scale[2 * p + j] = s[:, j * B : (j + 1) * B]
        return 0

    lax.fori_loop(0, RE // 2, spread, 0, unroll=4)

    def assemble(phase, y, ok_north, ok_south):
        for p in range(R // 2):
            a, b = lcol[phase, 0, p], lcol[phase, 1, p]
            y[H + 2 * p, O - 8 : O, :] = pltpu.roll(a, 4, 0)
            y[H + 2 * p + 1, O - 8 : O, :] = a
            y[H + 2 * p, O + B : O + B + 8, :] = b
            y[H + 2 * p + 1, O + B : O + B + 8, :] = pltpu.roll(b, 4, 0)
        for i in range(H):
            own_up = pltpu.roll(y[R + i, O - 8 : O + B + 8, :], 32, 1)
            far_up = pltpu.roll(lrow[phase, 0], (B - 32 * i) % B, 1) * ok_north
            y[i, O - 8 : O + B + 8, :] = jnp.where(lane_e < 32, far_up, own_up)
            own_down = pltpu.roll(y[H + i, O - 8 : O + B + 8, :], B - 32, 1)
            far_down = pltpu.roll(lrow[phase, 1], (96 - 32 * i) % B, 1) * ok_south
            y[H + R + i, O - 8 : O + B + 8, :] = jnp.where(
                lane_e >= 96, far_down, own_down
            )

    def keep(k, r, value):
        terms[pl.ds(pl.multiple_of(r * B, B), B), k * B : (k + 1) * B] = value.astype(BF16)

    def step(src, dst, k, scaled):
        reach = K - k
        first, count = (O - 8, CE) if reach else (O, B)
        size = 48 if reach else 64
        for at in range(0, count, size):
            step_block(src, dst, k, scaled, first + at, size)

    def step_block(src, dst, k, scaled, first, size):
        reach = K - k
        lo, hi = max(first, O), min(first + size, O + B)

        def sums(r):
            mid_ = src[r, first : first + size, :]
            low = src[r, first - 1 : first - 1 + size, :]
            high = src[r, first + 1 : first + 1 + size, :]
            return mid_ + high, low + high, mid_ + low

        def advance(r, carried):
            e0, e1, f1 = carried
            e2, f2, h2 = sums(r + 1)
            a = coef[r, first - O + 8 : first - O + 8 + size, :]
            total = a * (e0 + f1 + h2)
            if k == 1:
                value = 0.5 * total
            else:
                value = total - dst[r, first : first + size, :]
            dst[r, first : first + size, :] = value
            return (e1, e2, f2), value

        def outer(r, carried):
            return advance(r, carried)[0]

        def inner(r, carried):
            carried, value = advance(r, carried)
            value = value[lo - first : hi - first]
            if scaled:
                value = value * scale[r, lo - O + 8 : hi - O + 8, :]
            at = pl.multiple_of((r - H) * B + lo - O, 8)
            terms[pl.ds(at, hi - lo), k * B : (k + 1) * B] = value.astype(BF16)
            return carried

        low = H - reach
        e0 = sums(low - 1)[0]
        e1, f1, _ = sums(low)
        carried = (e0, e1, f1)
        if reach:
            carried = lax.fori_loop(low, H, outer, carried, unroll=reach)
        carried = lax.fori_loop(H, H + R, inner, carried, unroll=8)
        if reach:
            lax.fori_loop(H + R, H + R + reach, outer, carried, unroll=reach)

    for copy in first_halo:
        copy.wait()
    assemble(0, yb, 1.0, 1.0)

    def start_row(r, _):
        x = yb[r, O - 8 : O + B + 8, :]
        ya[r, O - 8 : O + B + 8, :] = (-0.5 * coef[r] * scale[r]) * x
        return 0

    lax.fori_loop(0, RE, start_row, 0, unroll=4)

    def keep_first(r, _):
        keep(0, r, ya[H + r, O : O + B, :] * scale[H + r, 8 : 8 + B, :])
        return 0

    lax.fori_loop(0, R, keep_first, 0, unroll=4)
    step(ya, yb, 1, True)
    step(yb, ya, 2, True)
    step(ya, yb, 3, True)
    step(yb, ya, 4, True)

    cot_in.wait()
    widen(cot_v, cf)

    def mix(p):
        at = pl.ds(pl.multiple_of(2 * p * B, 2 * B), 2 * B)
        mixed = lax.dot_general(wf[...], terms[at, :], NT, preferred_element_type=F32)
        act = jnp.tanh(mixed)
        cot = jnp.concatenate([rows_of(cf, 2 * p), rows_of(cf, 2 * p + 1)], axis=1)
        gcat[:, at] = (cot * (1.0 - act * act)).astype(BF16)

    def turn_grad(r):
        grad = gcat[:, pl.ds(pl.multiple_of(r * B, B), B)].astype(F32)
        w = -0.5 * coef[H + r, 8 : 8 + B, :] * scale[H + r, 8 : 8 + B, :]
        ya[H + r, O : O + B, :] = w * grad.T

    def grad_rows(first, count):
        for p in range(first // 2, (first + count) // 2):
            mix(p)
        for r in range(first, first + count):
            turn_grad(r)

    second_halo = halo_copies(1)
    send_chunks(1, ya, second_halo, grad_rows)

    chunk = 8 * B
    acc = None
    for n in range(R * B // chunk):
        part = jnp.dot(
            gcat[:, n * chunk : (n + 1) * chunk],
            terms[n * chunk : (n + 1) * chunk, :],
            preferred_element_type=F32,
        )
        acc = part if acc is None else acc + part
    lane_c = lax.broadcasted_iota(jnp.int32, (C, B), 1) // C
    folded = []
    for k in range(K + 1):
        tot = None
        for g in range(RG):
            piece = acc[g * C : (g + 1) * C, k * B : (k + 1) * B]
            tot = piece if tot is None else jnp.where(lane_c == g, piece, tot)
        tot = tot + pltpu.roll(tot, 64, 1)
        tot = tot + pltpu.roll(tot, 32, 1)
        folded.append(tot)
    head = folded[0]
    for k in range(1, K):
        head = jnp.where(lane_c == k, folded[k], head)
    tail = folded[K][0:8]
    for g in range(1, RG):
        tail = jnp.where(lane_c[0:8] == g, folded[K][8 * g : 8 * g + 8], tail)
    grid_cells = n_lat * n_lon * B * B
    own[0, 0:C, :] = head * (1.0 / math.sqrt(grid_cells))
    own[0, C : C + 8, :] = tail * (1.0 / math.sqrt(grid_cells))

    def lon_copy(off):
        return remote(
            own.at[0], ar1.at[lon], ar1_send.at[off], ar1_recv.at[lon],
            lat, lax.rem(lon + off, n_lon),
        )

    def lon_wait(off):
        q = lax.rem(lon + n_lon - off, n_lon)
        return remote(own.at[0], ar1.at[q], ar1_send.at[off], ar1_recv.at[q], lat, q)

    def lat_copy(off):
        return remote(
            own.at[1], ar2.at[lat], ar2_send.at[off], ar2_recv.at[lat],
            lax.rem(lat + off, n_lat), lon,
        )

    def lat_wait(off):
        q = lax.rem(lat + n_lat - off, n_lat)
        return remote(own.at[1], ar2.at[q], ar2_send.at[off], ar2_recv.at[q], q, lon)

    def run(count, act):
        def body(off, _):
            act(off)
            return 0

        lax.fori_loop(1, count, body, 0)

    run(n_lon, lambda off: lon_copy(off).start())
    ar1[lon] = own[0]

    for copy in second_halo:
        copy.wait()
    assemble(1, ya, north_ok, south_ok)

    def keep_grad(r, _):
        keep(0, r, ya[H + r, O : O + B, :])
        return 0

    lax.fori_loop(0, R, keep_grad, 0, unroll=4)
    step(ya, yb, 1, False)

    run(n_lon, lambda off: lon_wait(off).wait())
    total = ar1[0]
    for q in range(1, n_lon):
        total = total + ar1[q]
    own[1] = total
    run(n_lat, lambda off: lat_copy(off).start())
    ar2[lat] = total

    step(yb, ya, 2, False)
    step(ya, yb, 3, False)
    step(yb, ya, 4, False)

    run(n_lat, lambda off: lat_wait(off).wait())
    total = ar2[0]
    for q in range(1, n_lat):
        total = total + ar2[q]
    sum_ref[...] = total


def close(terms, snat, wb, sum_ref, out_hbm, wg_ref, xf, out_v, out_sem):
    def finish(p, _):
        t = terms[pl.ds(pl.multiple_of(2 * p * B, 2 * B), 2 * B), :]
        res = lax.dot_general(wb[...], t, NT, preferred_element_type=F32)
        for j in range(2):
            for g in range(RG):
                row = R * g + 2 * p + j
                s = jnp.broadcast_to(snat[pl.ds(row, 1), :], (C, B))
                part = res[g * C : (g + 1) * C, j * B : (j + 1) * B]
                xf[pl.ds(row, C, stride=B), :] = part * s
        return 0

    lax.fori_loop(0, R // 2, finish, 0, unroll=4)

    part = C // 4
    copies = [
        pltpu.make_async_copy(
            out_v.at[pl.ds(n * part, part)], out_hbm.at[pl.ds(n * part, part)], out_sem.at[n]
        )
        for n in range(4)
    ]
    for n in range(4):
        for c in range(n * part, (n + 1) * part):
            out_v[c] = xf[c * B : (c + 1) * B, :].astype(BF16)
        copies[n].start()
    total = sum_ref[...]
    flat = total[0:C].T
    for k in range(K):
        wg_ref[k] = flat[k * C : (k + 1) * C, :]
    last = total[C : C + 8]
    last = jnp.concatenate(
        [last if g == 0 else pltpu.roll(last, B - C * g, 1) for g in range(RG)], axis=0
    )
    wg_ref[K] = last.T[0:C, :]
    for copy in copies:
        copy.wait()


def solution(mesh):
    n_lat, n_lon = mesh.shape["lat"], mesh.shape["lon"]
    hbm = pl.BlockSpec(memory_space=pltpu.HBM)
    sem = pltpu.SemaphoreType.DMA

    def local(features, cotangent, sea_mask, weights):
        vmem = pl.BlockSpec(memory_space=pltpu.VMEM)
        carried = (
            pltpu.VMEM((R * B, (K + 1) * B), BF16),
            pltpu.VMEM((B, B), F32),
            pltpu.VMEM((B, (K + 1) * B), BF16),
            pltpu.VMEM((C + 8, B), F32),
        )
        carried = pl.pallas_call(
            functools.partial(kernel, n_lat, n_lon),
            out_shape=carried,
            in_specs=[hbm] * 4,
            out_specs=(vmem,) * 4,
            scratch_shapes=[
                pltpu.VMEM((C, B, B), BF16),
                pltpu.VMEM((C, B, B), BF16),
                pltpu.VMEM((B, B), jnp.int32),
                pltpu.VMEM((K + 1, C, C), BF16),
                pltpu.VMEM((C * B, B), F32),
                pltpu.VMEM((C * B, B), F32),
                pltpu.VMEM((RE, CP, B), F32),
                pltpu.VMEM((RE, CP, B), F32),
                pltpu.VMEM((RE, CE, B), F32),
                pltpu.VMEM((RE, CE, B), F32),
                pltpu.VMEM((B, R * B), BF16),
                pltpu.VMEM((4, 8, B), F32),
                pltpu.VMEM((8, 8, B), F32),
                pltpu.VMEM((2, CP, B), F32),
                pltpu.VMEM((CE, 2 * B), F32),
                pltpu.VMEM((B, (K + 1) * B), BF16),
                pltpu.VMEM((CE, 2 * B), BF16),
                pltpu.VMEM((2, 2, B, B), F32),
                pltpu.VMEM((2, 2, R // 2, 8, B), F32),
                pltpu.VMEM((2, 2, CE, B), F32),
                pltpu.VMEM((2, 2, R // 2, 8, B), F32),
                pltpu.VMEM((2, C + 8, B), F32),
                pltpu.VMEM((n_lon, C + 8, B), F32),
                pltpu.VMEM((n_lat, C + 8, B), F32),
                sem((4,)), sem((8,)), sem((8,)), sem((2, 16)), sem((2, 16)),
                sem((n_lon,)), sem((n_lon,)), sem((n_lat,)), sem((n_lat,)),
            ],
            compiler_params=pltpu.CompilerParams(
                collective_id=0, has_side_effects=True, vmem_limit_bytes=58 << 20
            ),
        )(features, cotangent, sea_mask, weights)
        return pl.pallas_call(
            close,
            out_shape=(
                jax.ShapeDtypeStruct((C, B, B), BF16),
                jax.ShapeDtypeStruct((K + 1, C, C), F32),
            ),
            in_specs=[vmem] * 4,
            out_specs=(hbm, vmem),
            scratch_shapes=[pltpu.VMEM((C * B, B), F32), pltpu.VMEM((C, B, B), BF16), sem((4,))],
            compiler_params=pltpu.CompilerParams(vmem_limit_bytes=16 << 20),
        )(*carried)

    placed = (P(None, "lat", "lon"), P(None, "lat", "lon"), P("lat", "lon"), P())
    return jax.shard_map(
        local, mesh=mesh, in_specs=placed, out_specs=(P(None, "lat", "lon"), P()), check_vma=False
    )
```

```python
import functools
import math

import jax
import jax.numpy as jnp
from jax import lax
from jax.experimental import pallas as pl
from jax.experimental.pallas import tpu as pltpu
from jax.sharding import PartitionSpec as P

K = 4
C = 32
B = 128
RG = 4
R = B // RG
H = 4
RE = R + 2 * H
CE = B + 16
CP = CE + 16
O = 16
F32 = jnp.float32
BF16 = jnp.bfloat16
NT = (((1,), (1,)), ((), ()))


def kernel(
    n_lat, n_lon,
    feat_hbm, cot_hbm, mask_hbm, w_hbm,
    out_v, sum_ref,
    feat_v, cot_v, mask_v, w_v, xf, cf,
    ya, yb, coef, scale, terms, gcat,
    mtx, mrx, sm, vm, snat, wf, wb, sel,
    pack, cpack, lrow, lcol, own, ar1, ar2,
    in_sem, mask_send, mask_recv, halo_send, halo_recv,
    ar1_send, ar1_recv, ar2_send, ar2_recv,
):
    lat = lax.axis_index("lat")
    lon = lax.axis_index("lon")
    north, south = lax.rem(lat + n_lat - 1, n_lat), lax.rem(lat + 1, n_lat)
    west, east = lax.rem(lon + n_lon - 1, n_lon), lax.rem(lon + 1, n_lon)

    feat_in = pltpu.make_async_copy(feat_hbm, feat_v, in_sem.at[0])
    cot_in = pltpu.make_async_copy(cot_hbm, cot_v, in_sem.at[1])
    mask_in = pltpu.make_async_copy(mask_hbm, mask_v, in_sem.at[2])
    w_in = pltpu.make_async_copy(w_hbm, w_v, in_sem.at[3])
    mask_in.start()
    feat_in.start()
    w_in.start()
    cot_in.start()

    barrier = pltpu.get_barrier_semaphore()

    def greet(i, j):
        pl.semaphore_signal(
            barrier, inc=1, device_id=(i, j), device_id_type=pl.DeviceIdType.MESH
        )

    for i in (north, south):
        for j in (west, east):
            greet(i, j)

    def greet_lon(off, _):
        greet(lat, lax.rem(lon + off, n_lon))
        return 0

    def greet_lat(off, _):
        greet(lax.rem(lat + off, n_lat), lon)
        return 0

    lax.fori_loop(1, n_lon, greet_lon, 0)
    lax.fori_loop(1, n_lat, greet_lat, 0)

    row_i = lax.broadcasted_iota(jnp.int32, (B, B), 0)
    col_i = lax.broadcasted_iota(jnp.int32, (B, B), 1)
    sel_r = lax.broadcasted_iota(jnp.int32, (CE, 2 * B), 0)
    sel_c = lax.broadcasted_iota(jnp.int32, (CE, 2 * B), 1)
    inside = (sel_r >= 8) & (sel_r < 8 + B) & (sel_c == sel_r - 8)
    left = (sel_r < 8) & (sel_c == 2 * B - 8 + sel_r)
    right = (sel_r >= 8 + B) & (sel_c == sel_r - 8)
    sel[...] = (inside | left | right).astype(F32).astype(BF16)

    mask_in.wait()
    flags = mask_v[...].astype(F32)
    turned_flags = flags.T
    mtx[0] = flags[B - 8 :]
    mtx[1] = flags[:8]
    mtx[2] = turned_flags[B - 8 :]
    mtx[3] = turned_flags[:8]
    pl.semaphore_wait(barrier, 4 + (n_lon - 1) + (n_lat - 1))

    def remote(src, dst, send, recv, i, j):
        return pltpu.make_async_remote_copy(
            src_ref=src, dst_ref=dst, send_sem=send, recv_sem=recv,
            device_id=(i, j), device_id_type=pl.DeviceIdType.MESH,
        )

    mid = pl.ds(8, B)
    above, below = pl.ds(0, 8), pl.ds(8 + B, 8)
    mask_plan = (
        (2, 0, lat, east),
        (3, 1, lat, west),
        (0, 2, south, lon),
        (1, 3, north, lon),
        (0, 4, south, east),
        (0, 5, south, west),
        (1, 6, north, east),
        (1, 7, north, west),
    )
    mask_copies = [
        remote(mtx.at[src], mrx.at[n], mask_send.at[n], mask_recv.at[n], i, j)
        for src, n, i, j in mask_plan
    ]
    for copy in mask_copies:
        copy.start()

    lane = lax.broadcasted_iota(jnp.int32, (B, B), 1)

    def halo_copies(phase):
        plan = (
            (pack.at[phase, 0], lrow.at[phase, 0, mid], south, lon),
            (pack.at[phase, 1], lrow.at[phase, 1, mid], north, lon),
            (pack.at[phase, 0, pl.ds(B - 8, 8)], lrow.at[phase, 0, above], south, east),
            (pack.at[phase, 0, pl.ds(0, 8)], lrow.at[phase, 0, below], south, west),
            (pack.at[phase, 1, pl.ds(B - 8, 8)], lrow.at[phase, 1, above], north, east),
            (pack.at[phase, 1, pl.ds(0, 8)], lrow.at[phase, 1, below], north, west),
        ) + tuple(
            (cpack.at[phase, side, at], lcol.at[phase, side, at], lat, (east, west)[side])
            for at in (pl.ds(0, 2), pl.ds(14, 2), pl.ds(2, 4), pl.ds(6, 4), pl.ds(10, 4))
            for side in range(2)
        )
        return [
            remote(src, dst, halo_send.at[phase, n], halo_recv.at[phase, n], i, j)
            for n, (src, dst, i, j) in enumerate(plan)
        ]

    def pack_rows(phase, y):
        last, first = None, None
        for i in range(H):
            a = pltpu.roll(y[H + R - H + i, O : O + B, :], (32 * i + 32) % 128, 1)
            b = pltpu.roll(y[H + i, O : O + B, :], (32 * i) % 128, 1)
            here = (lane >= 32 * i) & (lane < 32 * i + 32)
            last = a if last is None else jnp.where(here, a, last)
            first = b if first is None else jnp.where(here, b, first)
        pack[phase, 0] = last
        pack[phase, 1] = first

    half = lax.broadcasted_iota(jnp.int32, (8, B), 0) < 4

    def pack_columns(phase, y, p):
        a, b = y[H + 2 * p, O + B - 8 : O + B, :], y[H + 2 * p + 1, O + B - 8 : O + B, :]
        cpack[phase, 0, p] = jnp.where(half, pltpu.roll(a, 4, 0), b)
        a, b = y[H + 2 * p, O : O + 8, :], y[H + 2 * p + 1, O : O + 8, :]
        cpack[phase, 1, p] = jnp.where(half, a, pltpu.roll(b, 4, 0))

    def send_chunks(phase, y, copies, turn_rows):
        turn_rows(0, H)
        turn_rows(R - H, H)
        for p in (0, 1, 14, 15):
            pack_columns(phase, y, p)
        pack_rows(phase, y)
        for copy in copies[:10]:
            copy.start()
        for n in range(3):
            turn_rows(H + 8 * n, 8)
            for p in range(2 + 4 * n, 6 + 4 * n):
                pack_columns(phase, y, p)
            for copy in copies[10 + 2 * n : 12 + 2 * n]:
                copy.start()

    feat_in.wait()

    def widen(src, dst):
        def body(c, _):
            dst[pl.ds(pl.multiple_of(c * B, B), B), :] = src[c].astype(F32)
            return 0

        lax.fori_loop(0, C, body, 0, unroll=4)

    def rows_of(flat, r):
        return jnp.concatenate(
            [flat[pl.ds(R * g + r, C, stride=B), :] for g in range(RG)], axis=0
        )

    widen(feat_v, xf)

    def turn(r):
        yb[H + r, O : O + B, :] = rows_of(xf, r).T

    def turn_rows(first, count):
        for r in range(first, first + count):
            turn(r)

    first_halo = halo_copies(0)
    send_chunks(0, yb, first_halo, turn_rows)

    w_in.wait()
    block = (row_i // C) == (col_i // C)
    for k in range(K + 1):
        one = w_v[k].astype(F32)
        wide = jnp.concatenate([one] * RG, axis=1)
        full = jnp.where(block, jnp.concatenate([wide] * RG, axis=0), 0.0)
        wb[:, k * B : (k + 1) * B] = full.astype(BF16)
        wf[:, k * B : (k + 1) * B] = full.T.astype(BF16)

    cot_in.wait()
    widen(cot_v, cf)

    for copy in mask_copies:
        copy.wait()
    north_ok = (lat > 0).astype(F32)
    south_ok = (lat < n_lat - 1).astype(F32)
    lane_e = lax.broadcasted_iota(jnp.int32, (CE, B), 1)
    sm[:, 0:8, :] = jnp.zeros((2, 8, B), F32)
    sm[:, 8 + CE :, :] = jnp.zeros((2, 8, B), F32)
    sm[0, 8:16, :] = mrx[2] * north_ok
    sm[0, 16 : 16 + B, :] = mask_v[...].astype(F32)
    sm[0, 16 + B : 24 + B, :] = mrx[3] * south_ok
    low_lanes = lane_e[0:8] < 64
    sm[1, 8:16, :] = jnp.where(low_lanes, mrx[5], mrx[4]) * north_ok
    sm[1, 16 : 16 + B, :] = jnp.concatenate(
        [mrx[1], jnp.zeros((B - 16, B), F32), mrx[0]], axis=0
    ).T
    sm[1, 16 + B : 24 + B, :] = jnp.where(low_lanes, mrx[7], mrx[6]) * south_ok

    def ring(main, side, shift, edge):
        m, s = pltpu.roll(main, shift, 1), pltpu.roll(side, shift, 1)
        at = lane_e == edge
        return jnp.where(at, s, m), jnp.where(at, m, s)

    here = [sm[t, 8 : 8 + CE, :] for t in range(2)]
    up = [sm[t, 7 : 7 + CE, :] for t in range(2)]
    down = [sm[t, 9 : 9 + CE, :] for t in range(2)]
    from_left = ring(here[0] + down[0], here[1] + down[1], 1, 0)
    from_right = ring(here[0] + up[0], here[1] + up[1], B - 1, B - 1)
    for t in range(2):
        degree = from_left[t] + from_right[t] + up[t] + down[t]
        vm[:, t * B : (t + 1) * B] = here[t] * jnp.maximum(degree, 1.0)
        if t == 0:
            snat[...] = jnp.sqrt(jnp.maximum(degree, 1.0)[8 : 8 + B])

    def spread(p, _):
        rows = jnp.concatenate(
            [
                jnp.broadcast_to(vm[pl.ds(8 - H + R * g + 2 * p + j, 1), :], (C, 2 * B))
                for j in range(2)
                for g in range(RG)
            ],
            axis=0,
        )
        v = lax.dot_general(sel[...], rows.astype(BF16), NT, preferred_element_type=F32)
        m = jnp.maximum(v, 1.0)
        rs = lax.rsqrt(m)
        a, s = jnp.where(v > 0.5, -2.0 * rs * rs, 0.0), m * rs
        for j in range(2):
            coef[2 * p + j] = a[:, j * B : (j + 1) * B]
            scale[2 * p + j] = s[:, j * B : (j + 1) * B]
        return 0

    lax.fori_loop(0, RE // 2, spread, 0, unroll=4)

    def assemble(phase, y, ok_north, ok_south):
        for p in range(R // 2):
            a, b = lcol[phase, 0, p], lcol[phase, 1, p]
            y[H + 2 * p, O - 8 : O, :] = pltpu.roll(a, 4, 0)
            y[H + 2 * p + 1, O - 8 : O, :] = a
            y[H + 2 * p, O + B : O + B + 8, :] = b
            y[H + 2 * p + 1, O + B : O + B + 8, :] = pltpu.roll(b, 4, 0)
        for i in range(H):
            own_up = pltpu.roll(y[R + i, O - 8 : O + B + 8, :], 32, 1)
            far_up = pltpu.roll(lrow[phase, 0], (B - 32 * i) % B, 1) * ok_north
            y[i, O - 8 : O + B + 8, :] = jnp.where(lane_e < 32, far_up, own_up)
            own_down = pltpu.roll(y[H + i, O - 8 : O + B + 8, :], B - 32, 1)
            far_down = pltpu.roll(lrow[phase, 1], (96 - 32 * i) % B, 1) * ok_south
            y[H + R + i, O - 8 : O + B + 8, :] = jnp.where(
                lane_e >= 96, far_down, own_down
            )

    def keep(k, r, value):
        terms[pl.ds(pl.multiple_of(r * B, B), B), k * B : (k + 1) * B] = value.astype(BF16)

    def step(src, dst, k, scaled):
        reach = K - k
        first, count = (O - 8, CE) if reach else (O, B)
        size = 48 if reach else 64
        for at in range(0, count, size):
            step_block(src, dst, k, scaled, first + at, size)

    def step_block(src, dst, k, scaled, first, size):
        reach = K - k
        lo, hi = max(first, O), min(first + size, O + B)

        def sums(r):
            mid_ = src[r, first : first + size, :]
            low = src[r, first - 1 : first - 1 + size, :]
            high = src[r, first + 1 : first + 1 + size, :]
            return mid_ + high, low + high, mid_ + low

        def advance(r, carried):
            e0, e1, f1 = carried
            e2, f2, h2 = sums(r + 1)
            a = coef[r, first - O + 8 : first - O + 8 + size, :]
            total = a * (e0 + f1 + h2)
            if k == 1:
                value = 0.5 * total
            else:
                value = total - dst[r, first : first + size, :]
            dst[r, first : first + size, :] = value
            return (e1, e2, f2), value

        def outer(r, carried):
            return advance(r, carried)[0]

        def inner(r, carried):
            carried, value = advance(r, carried)
            value = value[lo - first : hi - first]
            if scaled:
                value = value * scale[r, lo - O + 8 : hi - O + 8, :]
            at = pl.multiple_of((r - H) * B + lo - O, 8)
            terms[pl.ds(at, hi - lo), k * B : (k + 1) * B] = value.astype(BF16)
            return carried

        low = H - reach
        e0 = sums(low - 1)[0]
        e1, f1, _ = sums(low)
        carried = (e0, e1, f1)
        if reach:
            carried = lax.fori_loop(low, H, outer, carried, unroll=reach)
        carried = lax.fori_loop(H, H + R, inner, carried, unroll=8)
        if reach:
            lax.fori_loop(H + R, H + R + reach, outer, carried, unroll=reach)

    for copy in first_halo:
        copy.wait()
    assemble(0, yb, 1.0, 1.0)

    def start_row(r, _):
        x = yb[r, O - 8 : O + B + 8, :]
        ya[r, O - 8 : O + B + 8, :] = (-0.5 * coef[r] * scale[r]) * x
        return 0

    lax.fori_loop(0, RE, start_row, 0, unroll=4)

    def keep_first(r, _):
        keep(0, r, ya[H + r, O : O + B, :] * scale[H + r, 8 : 8 + B, :])
        return 0

    lax.fori_loop(0, R, keep_first, 0, unroll=4)
    step(ya, yb, 1, True)
    step(yb, ya, 2, True)
    step(ya, yb, 3, True)
    step(yb, ya, 4, True)


    def mix(p):
        at = pl.ds(pl.multiple_of(2 * p * B, 2 * B), 2 * B)
        mixed = lax.dot_general(wf[...], terms[at, :], NT, preferred_element_type=F32)
        act = jnp.tanh(mixed)
        cot = jnp.concatenate([rows_of(cf, 2 * p), rows_of(cf, 2 * p + 1)], axis=1)
        gcat[:, at] = (cot * (1.0 - act * act)).astype(BF16)

    def turn_grad(r):
        grad = gcat[:, pl.ds(pl.multiple_of(r * B, B), B)].astype(F32)
        w = -0.5 * coef[H + r, 8 : 8 + B, :] * scale[H + r, 8 : 8 + B, :]
        ya[H + r, O : O + B, :] = w * grad.T

    def grad_rows(first, count):
        for p in range(first // 2, (first + count) // 2):
            mix(p)
        for r in range(first, first + count):
            turn_grad(r)

    second_halo = halo_copies(1)
    send_chunks(1, ya, second_halo, grad_rows)

    chunk = 8 * B
    acc = None
    for n in range(R * B // chunk):
        part = jnp.dot(
            gcat[:, n * chunk : (n + 1) * chunk],
            terms[n * chunk : (n + 1) * chunk, :],
            preferred_element_type=F32,
        )
        acc = part if acc is None else acc + part
    lane_c = lax.broadcasted_iota(jnp.int32, (C, B), 1) // C
    folded = []
    for k in range(K + 1):
        tot = None
        for g in range(RG):
            piece = acc[g * C : (g + 1) * C, k * B : (k + 1) * B]
            tot = piece if tot is None else jnp.where(lane_c == g, piece, tot)
        tot = tot + pltpu.roll(tot, 64, 1)
        tot = tot + pltpu.roll(tot, 32, 1)
        folded.append(tot)
    head = folded[0]
    for k in range(1, K):
        head = jnp.where(lane_c == k, folded[k], head)
    tail = folded[K][0:8]
    for g in range(1, RG):
        tail = jnp.where(lane_c[0:8] == g, folded[K][8 * g : 8 * g + 8], tail)
    grid_cells = n_lat * n_lon * B * B
    own[0, 0:C, :] = head * (1.0 / math.sqrt(grid_cells))
    own[0, C : C + 8, :] = tail * (1.0 / math.sqrt(grid_cells))

    def lon_copy(off):
        return remote(
            own.at[0], ar1.at[lon], ar1_send.at[off], ar1_recv.at[lon],
            lat, lax.rem(lon + off, n_lon),
        )

    def lon_wait(off):
        q = lax.rem(lon + n_lon - off, n_lon)
        return remote(own.at[0], ar1.at[q], ar1_send.at[off], ar1_recv.at[q], lat, q)

    def lat_copy(off):
        return remote(
            own.at[1], ar2.at[lat], ar2_send.at[off], ar2_recv.at[lat],
            lax.rem(lat + off, n_lat), lon,
        )

    def lat_wait(off):
        q = lax.rem(lat + n_lat - off, n_lat)
        return remote(own.at[1], ar2.at[q], ar2_send.at[off], ar2_recv.at[q], q, lon)

    def run(count, act):
        def body(off, _):
            act(off)
            return 0

        lax.fori_loop(1, count, body, 0)

    run(n_lon, lambda off: lon_copy(off).start())
    ar1[lon] = own[0]

    def keep_grad(r, _):
        keep(0, r, ya[H + r, O : O + B, :])
        return 0

    lax.fori_loop(0, R, keep_grad, 0, unroll=4)
    for copy in second_halo:
        copy.wait()
    assemble(1, ya, north_ok, south_ok)

    step(ya, yb, 1, False)

    run(n_lon, lambda off: lon_wait(off).wait())
    total = ar1[0]
    for q in range(1, n_lon):
        total = total + ar1[q]
    own[1] = total
    run(n_lat, lambda off: lat_copy(off).start())
    ar2[lat] = total

    step(yb, ya, 2, False)
    step(ya, yb, 3, False)
    step(yb, ya, 4, False)

    def finish(p, _):
        t = terms[pl.ds(pl.multiple_of(2 * p * B, 2 * B), 2 * B), :]
        res = lax.dot_general(wb[...], t, NT, preferred_element_type=F32)
        for j in range(2):
            for g in range(RG):
                row = R * g + 2 * p + j
                s = jnp.broadcast_to(snat[pl.ds(row, 1), :], (C, B))
                part = res[g * C : (g + 1) * C, j * B : (j + 1) * B]
                xf[pl.ds(row, C, stride=B), :] = part * s
        return 0

    lax.fori_loop(0, R // 2, finish, 0, unroll=4)

    for c in range(C):
        out_v[c] = xf[c * B : (c + 1) * B, :].astype(BF16)

    run(n_lat, lambda off: lat_wait(off).wait())
    total = ar2[0]
    for q in range(1, n_lat):
        total = total + ar2[q]
    sum_ref[...] = total


def close(out_v, sum_ref, out_hbm, wg_ref, out_sem):
    copy = pltpu.make_async_copy(out_v, out_hbm, out_sem)
    copy.start()
    total = sum_ref[...]
    flat = total[0:C].T
    for k in range(K):
        wg_ref[k] = flat[k * C : (k + 1) * C, :]
    last = total[C : C + 8]
    last = jnp.concatenate(
        [last if g == 0 else pltpu.roll(last, B - C * g, 1) for g in range(RG)], axis=0
    )
    wg_ref[K] = last.T[0:C, :]
    copy.wait()


def solution(mesh):
    n_lat, n_lon = mesh.shape["lat"], mesh.shape["lon"]
    hbm = pl.BlockSpec(memory_space=pltpu.HBM)
    sem = pltpu.SemaphoreType.DMA

    def local(features, cotangent, sea_mask, weights):
        vmem = pl.BlockSpec(memory_space=pltpu.VMEM)
        carried = (
            pltpu.VMEM((C, B, B), BF16),
            pltpu.VMEM((C + 8, B), F32),
        )
        carried = pl.pallas_call(
            functools.partial(kernel, n_lat, n_lon),
            out_shape=carried,
            in_specs=[hbm] * 4,
            out_specs=(vmem,) * 2,
            scratch_shapes=[
                pltpu.VMEM((C, B, B), BF16),
                pltpu.VMEM((C, B, B), BF16),
                pltpu.VMEM((B, B), jnp.int32),
                pltpu.VMEM((K + 1, C, C), BF16),
                pltpu.VMEM((C * B, B), F32),
                pltpu.VMEM((C * B, B), F32),
                pltpu.VMEM((RE, CP, B), F32),
                pltpu.VMEM((RE, CP, B), F32),
                pltpu.VMEM((RE, CE, B), F32),
                pltpu.VMEM((RE, CE, B), F32),
                pltpu.VMEM((R * B, (K + 1) * B), BF16),
                pltpu.VMEM((B, R * B), BF16),
                pltpu.VMEM((4, 8, B), F32),
                pltpu.VMEM((8, 8, B), F32),
                pltpu.VMEM((2, CP, B), F32),
                pltpu.VMEM((CE, 2 * B), F32),
                pltpu.VMEM((B, B), F32),
                pltpu.VMEM((B, (K + 1) * B), BF16),
                pltpu.VMEM((B, (K + 1) * B), BF16),
                pltpu.VMEM((CE, 2 * B), BF16),
                pltpu.VMEM((2, 2, B, B), F32),
                pltpu.VMEM((2, 2, R // 2, 8, B), F32),
                pltpu.VMEM((2, 2, CE, B), F32),
                pltpu.VMEM((2, 2, R // 2, 8, B), F32),
                pltpu.VMEM((2, C + 8, B), F32),
                pltpu.VMEM((n_lon, C + 8, B), F32),
                pltpu.VMEM((n_lat, C + 8, B), F32),
                sem((4,)), sem((8,)), sem((8,)), sem((2, 16)), sem((2, 16)),
                sem((n_lon,)), sem((n_lon,)), sem((n_lat,)), sem((n_lat,)),
            ],
            compiler_params=pltpu.CompilerParams(
                collective_id=0, has_side_effects=True, vmem_limit_bytes=62 << 20
            ),
        )(features, cotangent, sea_mask, weights)
        return pl.pallas_call(
            close,
            out_shape=(
                jax.ShapeDtypeStruct((C, B, B), BF16),
                jax.ShapeDtypeStruct((K + 1, C, C), F32),
            ),
            in_specs=[vmem] * 2,
            out_specs=(hbm, vmem),
            scratch_shapes=[sem(())],
            compiler_params=pltpu.CompilerParams(vmem_limit_bytes=4 << 20),
        )(*carried)

    placed = (P(None, "lat", "lon"), P(None, "lat", "lon"), P("lat", "lon"), P())
    return jax.shard_map(
        local, mesh=mesh, in_specs=placed, out_specs=(P(None, "lat", "lon"), P()), check_vma=False
    )
```

```python
import functools
import math

import jax
import jax.numpy as jnp
from jax import lax
from jax.experimental import pallas as pl
from jax.experimental.pallas import tpu as pltpu
from jax.sharding import PartitionSpec as P

K = 4
C = 32
B = 128
RG = 4
R = B // RG
H = 4
RE = R + 2 * H
CE = B + 16
CP = CE + 16
O = 16
F32 = jnp.float32
BF16 = jnp.bfloat16
NT = (((1,), (1,)), ((), ()))


def kernel(
    n_lat, n_lon,
    feat_hbm, cot_hbm, mask_hbm, w_hbm,
    out_v, sum_ref,
    feat_v, cot_v, mask_v, w_v, xf, cf,
    ya, yb, coef, scale, terms, gcat,
    mtx, mrx, sm, vm, snat, wf, wb, sel,
    pack, cpack, lrow, lcol, own, ar1, ar2,
    in_sem, mask_send, mask_recv, halo_send, halo_recv,
    ar1_send, ar1_recv, ar2_send, ar2_recv,
):
    lat = lax.axis_index("lat")
    lon = lax.axis_index("lon")
    north, south = lax.rem(lat + n_lat - 1, n_lat), lax.rem(lat + 1, n_lat)
    west, east = lax.rem(lon + n_lon - 1, n_lon), lax.rem(lon + 1, n_lon)

    feat_in = pltpu.make_async_copy(feat_hbm, feat_v, in_sem.at[0])
    cot_in = pltpu.make_async_copy(cot_hbm, cot_v, in_sem.at[1])
    mask_in = pltpu.make_async_copy(mask_hbm, mask_v, in_sem.at[2])
    w_in = pltpu.make_async_copy(w_hbm, w_v, in_sem.at[3])
    mask_in.start()
    feat_in.start()
    w_in.start()
    cot_in.start()

    barrier = pltpu.get_barrier_semaphore()

    def greet(i, j):
        pl.semaphore_signal(
            barrier, inc=1, device_id=(i, j), device_id_type=pl.DeviceIdType.MESH
        )

    for i in (north, south):
        for j in (west, east):
            greet(i, j)

    def greet_lon(off, _):
        greet(lat, lax.rem(lon + off, n_lon))
        return 0

    def greet_lat(off, _):
        greet(lax.rem(lat + off, n_lat), lon)
        return 0

    lax.fori_loop(1, n_lon, greet_lon, 0)
    lax.fori_loop(1, n_lat, greet_lat, 0)

    row_i = lax.broadcasted_iota(jnp.int32, (B, B), 0)
    col_i = lax.broadcasted_iota(jnp.int32, (B, B), 1)
    sel_r = lax.broadcasted_iota(jnp.int32, (CE, 2 * B), 0)
    sel_c = lax.broadcasted_iota(jnp.int32, (CE, 2 * B), 1)
    inside = (sel_r >= 8) & (sel_r < 8 + B) & (sel_c == sel_r - 8)
    left = (sel_r < 8) & (sel_c == 2 * B - 8 + sel_r)
    right = (sel_r >= 8 + B) & (sel_c == sel_r - 8)
    sel[...] = (inside | left | right).astype(F32).astype(BF16)

    mask_in.wait()
    flags = mask_v[...].astype(F32)
    turned_flags = flags.T
    mtx[0] = flags[B - 8 :]
    mtx[1] = flags[:8]
    mtx[2] = turned_flags[B - 8 :]
    mtx[3] = turned_flags[:8]
    pl.semaphore_wait(barrier, 4 + (n_lon - 1) + (n_lat - 1))

    def remote(src, dst, send, recv, i, j):
        return pltpu.make_async_remote_copy(
            src_ref=src, dst_ref=dst, send_sem=send, recv_sem=recv,
            device_id=(i, j), device_id_type=pl.DeviceIdType.MESH,
        )

    mid = pl.ds(8, B)
    above, below = pl.ds(0, 8), pl.ds(8 + B, 8)
    mask_plan = (
        (2, 0, lat, east),
        (3, 1, lat, west),
        (0, 2, south, lon),
        (1, 3, north, lon),
        (0, 4, south, east),
        (0, 5, south, west),
        (1, 6, north, east),
        (1, 7, north, west),
    )
    mask_copies = [
        remote(mtx.at[src], mrx.at[n], mask_send.at[n], mask_recv.at[n], i, j)
        for src, n, i, j in mask_plan
    ]
    for copy in mask_copies:
        copy.start()

    lane = lax.broadcasted_iota(jnp.int32, (B, B), 1)

    def halo_copies(phase):
        plan = (
            (pack.at[phase, 0], lrow.at[phase, 0, mid], south, lon),
            (pack.at[phase, 1], lrow.at[phase, 1, mid], north, lon),
            (pack.at[phase, 0, pl.ds(B - 8, 8)], lrow.at[phase, 0, above], south, east),
            (pack.at[phase, 0, pl.ds(0, 8)], lrow.at[phase, 0, below], south, west),
            (pack.at[phase, 1, pl.ds(B - 8, 8)], lrow.at[phase, 1, above], north, east),
            (pack.at[phase, 1, pl.ds(0, 8)], lrow.at[phase, 1, below], north, west),
        ) + tuple(
            (cpack.at[phase, side, at], lcol.at[phase, side, at], lat, (east, west)[side])
            for at in (pl.ds(0, 2), pl.ds(14, 2), pl.ds(2, 4), pl.ds(6, 4), pl.ds(10, 4))
            for side in range(2)
        )
        return [
            remote(src, dst, halo_send.at[phase, n], halo_recv.at[phase, n], i, j)
            for n, (src, dst, i, j) in enumerate(plan)
        ]

    def pack_rows(phase, y):
        last, first = None, None
        for i in range(H):
            a = pltpu.roll(y[H + R - H + i, O : O + B, :], (32 * i + 32) % 128, 1)
            b = pltpu.roll(y[H + i, O : O + B, :], (32 * i) % 128, 1)
            here = (lane >= 32 * i) & (lane < 32 * i + 32)
            last = a if last is None else jnp.where(here, a, last)
            first = b if first is None else jnp.where(here, b, first)
        pack[phase, 0] = last
        pack[phase, 1] = first

    half = lax.broadcasted_iota(jnp.int32, (8, B), 0) < 4

    def pack_columns(phase, y, p):
        a, b = y[H + 2 * p, O + B - 8 : O + B, :], y[H + 2 * p + 1, O + B - 8 : O + B, :]
        cpack[phase, 0, p] = jnp.where(half, pltpu.roll(a, 4, 0), b)
        a, b = y[H + 2 * p, O : O + 8, :], y[H + 2 * p + 1, O : O + 8, :]
        cpack[phase, 1, p] = jnp.where(half, a, pltpu.roll(b, 4, 0))

    def send_chunks(phase, y, copies, turn_rows):
        turn_rows(0, H)
        turn_rows(R - H, H)
        for p in (0, 1, 14, 15):
            pack_columns(phase, y, p)
        pack_rows(phase, y)
        for copy in copies[:10]:
            copy.start()
        for n in range(3):
            turn_rows(H + 8 * n, 8)
            for p in range(2 + 4 * n, 6 + 4 * n):
                pack_columns(phase, y, p)
            for copy in copies[10 + 2 * n : 12 + 2 * n]:
                copy.start()

    feat_in.wait()

    def widen(src, dst):
        def body(c, _):
            dst[pl.ds(pl.multiple_of(c * B, B), B), :] = src[c].astype(F32)
            return 0

        lax.fori_loop(0, C, body, 0, unroll=4)

    def rows_of(flat, r):
        return jnp.concatenate(
            [flat[pl.ds(R * g + r, C, stride=B), :] for g in range(RG)], axis=0
        )

    widen(feat_v, xf)

    def turn(r):
        yb[H + r, O : O + B, :] = rows_of(xf, r).T

    def turn_rows(first, count):
        for r in range(first, first + count):
            turn(r)

    first_halo = halo_copies(0)
    send_chunks(0, yb, first_halo, turn_rows)

    w_in.wait()
    block = (row_i // C) == (col_i // C)
    for k in range(K + 1):
        one = w_v[k].astype(F32)
        wide = jnp.concatenate([one] * RG, axis=1)
        full = jnp.where(block, jnp.concatenate([wide] * RG, axis=0), 0.0)
        wb[:, k * B : (k + 1) * B] = full.astype(BF16)
        wf[:, k * B : (k + 1) * B] = full.T.astype(BF16)

    cot_in.wait()
    widen(cot_v, cf)

    for copy in mask_copies:
        copy.wait()
    north_ok = (lat > 0).astype(F32)
    south_ok = (lat < n_lat - 1).astype(F32)
    lane_e = lax.broadcasted_iota(jnp.int32, (CE, B), 1)
    sm[:, 0:8, :] = jnp.zeros((2, 8, B), F32)
    sm[:, 8 + CE :, :] = jnp.zeros((2, 8, B), F32)
    sm[0, 8:16, :] = mrx[2] * north_ok
    sm[0, 16 : 16 + B, :] = mask_v[...].astype(F32)
    sm[0, 16 + B : 24 + B, :] = mrx[3] * south_ok
    low_lanes = lane_e[0:8] < 64
    sm[1, 8:16, :] = jnp.where(low_lanes, mrx[5], mrx[4]) * north_ok
    sm[1, 16 : 16 + B, :] = jnp.concatenate(
        [mrx[1], jnp.zeros((B - 16, B), F32), mrx[0]], axis=0
    ).T
    sm[1, 16 + B : 24 + B, :] = jnp.where(low_lanes, mrx[7], mrx[6]) * south_ok

    def ring(main, side, shift, edge):
        m, s = pltpu.roll(main, shift, 1), pltpu.roll(side, shift, 1)
        at = lane_e == edge
        return jnp.where(at, s, m), jnp.where(at, m, s)

    here = [sm[t, 8 : 8 + CE, :] for t in range(2)]
    up = [sm[t, 7 : 7 + CE, :] for t in range(2)]
    down = [sm[t, 9 : 9 + CE, :] for t in range(2)]
    from_left = ring(here[0] + down[0], here[1] + down[1], 1, 0)
    from_right = ring(here[0] + up[0], here[1] + up[1], B - 1, B - 1)
    for t in range(2):
        degree = from_left[t] + from_right[t] + up[t] + down[t]
        vm[:, t * B : (t + 1) * B] = here[t] * jnp.maximum(degree, 1.0)
        if t == 0:
            snat[...] = jnp.sqrt(jnp.maximum(degree, 1.0)[8 : 8 + B])

    def spread(p, _):
        rows = jnp.concatenate(
            [
                jnp.broadcast_to(vm[pl.ds(8 - H + R * g + 2 * p + j, 1), :], (C, 2 * B))
                for j in range(2)
                for g in range(RG)
            ],
            axis=0,
        )
        v = lax.dot_general(sel[...], rows.astype(BF16), NT, preferred_element_type=F32)
        m = jnp.maximum(v, 1.0)
        rs = lax.rsqrt(m)
        a, s = jnp.where(v > 0.5, -2.0 * rs * rs, 0.0), m * rs
        for j in range(2):
            coef[2 * p + j] = a[:, j * B : (j + 1) * B]
            scale[2 * p + j] = s[:, j * B : (j + 1) * B]
        return 0

    lax.fori_loop(0, RE // 2, spread, 0, unroll=4)

    def groups(y):
        for i in range(H):
            y[i, O : O + B, :] = pltpu.roll(y[R + i, O : O + B, :], C, 1)
            y[H + R + i, O : O + B, :] = pltpu.roll(y[H + i, O : O + B, :], B - C, 1)

    def beside(y, at, row, shift):
        return jnp.concatenate(
            [
                pltpu.roll(y[row, O - 8 : O, :], shift, 1),
                y[at, O : O + B, :],
                pltpu.roll(y[row, O + B : O + B + 8, :], shift, 1),
            ],
            axis=0,
        )

    def assemble(phase, y, ok_north, ok_south):
        for p in range(R // 2):
            a, b = lcol[phase, 0, p], lcol[phase, 1, p]
            y[H + 2 * p, O - 8 : O, :] = pltpu.roll(a, 4, 0)
            y[H + 2 * p + 1, O - 8 : O, :] = a
            y[H + 2 * p, O + B : O + B + 8, :] = b
            y[H + 2 * p + 1, O + B : O + B + 8, :] = pltpu.roll(b, 4, 0)
        for i in range(H):
            own_up = beside(y, i, R + i, C)
            far_up = pltpu.roll(lrow[phase, 0], (B - 32 * i) % B, 1) * ok_north
            y[i, O - 8 : O + B + 8, :] = jnp.where(lane_e < 32, far_up, own_up)
            own_down = beside(y, H + R + i, H + i, B - C)
            far_down = pltpu.roll(lrow[phase, 1], (96 - 32 * i) % B, 1) * ok_south
            y[H + R + i, O - 8 : O + B + 8, :] = jnp.where(
                lane_e >= 96, far_down, own_down
            )

    def keep(k, r, value):
        terms[pl.ds(pl.multiple_of(r * B, B), B), k * B : (k + 1) * B] = value.astype(BF16)

    def step(src, dst, k, scaled):
        reach = K - k
        first, count = (O - 8, CE) if reach else (O, B)
        size = 48 if reach else 64
        for at in range(0, count, size):
            step_block(src, dst, k, scaled, first + at, size)

    def step_block(src, dst, k, scaled, first, size):
        reach = K - k
        lo, hi = max(first, O), min(first + size, O + B)

        def sums(r):
            mid_ = src[r, first : first + size, :]
            low = src[r, first - 1 : first - 1 + size, :]
            high = src[r, first + 1 : first + 1 + size, :]
            return mid_ + high, low + high, mid_ + low

        def advance(r, carried):
            e0, e1, f1 = carried
            e2, f2, h2 = sums(r + 1)
            a = coef[r, first - O + 8 : first - O + 8 + size, :]
            total = a * (e0 + f1 + h2)
            if k == 1:
                value = 0.5 * total
            else:
                value = total - dst[r, first : first + size, :]
            dst[r, first : first + size, :] = value
            return (e1, e2, f2), value

        def outer(r, carried):
            return advance(r, carried)[0]

        def inner(r, carried):
            carried, value = advance(r, carried)
            value = value[lo - first : hi - first]
            if scaled:
                value = value * scale[r, lo - O + 8 : hi - O + 8, :]
            at = pl.multiple_of((r - H) * B + lo - O, 8)
            terms[pl.ds(at, hi - lo), k * B : (k + 1) * B] = value.astype(BF16)
            return carried

        low = H - reach
        e0 = sums(low - 1)[0]
        e1, f1, _ = sums(low)
        carried = (e0, e1, f1)
        if reach:
            carried = lax.fori_loop(low, H, outer, carried, unroll=reach)
        carried = lax.fori_loop(H, H + R, inner, carried, unroll=8)
        if reach:
            lax.fori_loop(H + R, H + R + reach, outer, carried, unroll=reach)

    def cells(src, dst, k, bands, rows, unroll):
        def sums(r, first, size):
            mid_ = src[r, first : first + size, :]
            low = src[r, first - 1 : first - 1 + size, :]
            high = src[r, first + 1 : first + 1 + size, :]
            return mid_ + high, low + high, mid_ + low

        def advance(r, carried, keeps):
            after = []
            for (first, size), (e0, e1, f1) in zip(bands, carried):
                e2, f2, h2 = sums(r + 1, first, size)
                total = coef[r, first - O + 8 : first - O + 8 + size, :] * (e0 + f1 + h2)
                if k == 1:
                    value = 0.5 * total
                else:
                    value = total - dst[r, first : first + size, :]
                dst[r, first : first + size, :] = value
                lo, hi = max(first, O), min(first + size, O + B)
                if keeps:
                    at = (r - H) * B + lo - O
                    if not isinstance(r, int):
                        at = pl.multiple_of(at, 8)
                    terms[pl.ds(at, hi - lo), k * B : (k + 1) * B] = value[
                        lo - first : hi - first
                    ].astype(BF16)
                after.append((e1, e2, f2))
            return tuple(after)

        low, high = rows
        carried = tuple(
            (sums(low - 1, *band)[0],) + sums(low, *band)[:2] for band in bands
        )
        if unroll:
            lax.fori_loop(
                low, high, lambda r, c: advance(r, c, True), carried, unroll=unroll
            )
        else:
            for r in range(low, high):
                carried = advance(r, carried, H <= r < H + R)

    def step_inside(src, dst, k):
        first, last = O + 8 * k, O + B - 8 * k
        size = (last - first) // (1 if k == K else 2)
        for at in range(first, last, size):
            cells(src, dst, k, ((at, size),), (H + k, H + R - k), (0, 6, 7, 13, 8)[k])

    def step_rim(src, dst, k):
        reach = K - k
        first, last = (O - 8, O + B + 8) if reach else (O, O + B)
        size = 48 if reach else 64
        for low in (H - reach, H + R - k):
            for at in range(first, last, size):
                cells(src, dst, k, ((at, size),), (low, low + K), 0)
        width = O + 8 * k - first
        bands = ((first, width), (last - width, width))
        cells(src, dst, k, bands, (H + k, H + R - k), (0, 6, 7, 13, 8)[k])

    for copy in first_halo:
        copy.wait()
    groups(yb)
    assemble(0, yb, 1.0, 1.0)

    def start_row(r, _):
        x = yb[r, O - 8 : O + B + 8, :]
        value = (-0.5 * coef[r] * scale[r]) * x
        ya[r, O - 8 : O + B + 8, :] = value
        return value

    def start_halo(r, _):
        start_row(r, 0)
        return 0

    def start_own(r, _):
        keep(0, r - H, start_row(r, 0)[8 : 8 + B] * scale[r, 8 : 8 + B, :])
        return 0

    lax.fori_loop(0, H, start_halo, 0, unroll=4)
    lax.fori_loop(H, H + R, start_own, 0, unroll=4)
    lax.fori_loop(H + R, RE, start_halo, 0, unroll=4)

    step(ya, yb, 1, True)
    step(yb, ya, 2, True)
    step(ya, yb, 3, True)
    step(yb, ya, 4, True)


    def mix(p):
        at = pl.ds(pl.multiple_of(2 * p * B, 2 * B), 2 * B)
        mixed = lax.dot_general(wf[...], terms[at, :], NT, preferred_element_type=F32)
        act = jnp.tanh(mixed)
        cot = jnp.concatenate([rows_of(cf, 2 * p), rows_of(cf, 2 * p + 1)], axis=1)
        gcat[:, at] = (cot * (1.0 - act * act)).astype(BF16)

    def turn_grad(r):
        grad = gcat[:, pl.ds(pl.multiple_of(r * B, B), B)].astype(F32)
        w = -0.5 * coef[H + r, 8 : 8 + B, :] * scale[H + r, 8 : 8 + B, :]
        ya[H + r, O : O + B, :] = w * grad.T

    def grad_rows(first, count):
        for p in range(first // 2, (first + count) // 2):
            mix(p)
        for r in range(first, first + count):
            turn_grad(r)

    second_halo = halo_copies(1)
    send_chunks(1, ya, second_halo, grad_rows)

    chunk = 8 * B
    acc = None
    for n in range(R * B // chunk):
        part = jnp.dot(
            gcat[:, n * chunk : (n + 1) * chunk],
            terms[n * chunk : (n + 1) * chunk, :],
            preferred_element_type=F32,
        )
        acc = part if acc is None else acc + part
    lane_c = lax.broadcasted_iota(jnp.int32, (C, B), 1) // C
    folded = []
    for k in range(K + 1):
        tot = None
        for g in range(RG):
            piece = acc[g * C : (g + 1) * C, k * B : (k + 1) * B]
            tot = piece if tot is None else jnp.where(lane_c == g, piece, tot)
        tot = tot + pltpu.roll(tot, 64, 1)
        tot = tot + pltpu.roll(tot, 32, 1)
        folded.append(tot)
    head = folded[0]
    for k in range(1, K):
        head = jnp.where(lane_c == k, folded[k], head)
    tail = folded[K][0:8]
    for g in range(1, RG):
        tail = jnp.where(lane_c[0:8] == g, folded[K][8 * g : 8 * g + 8], tail)
    grid_cells = n_lat * n_lon * B * B
    own[0, 0:C, :] = head * (1.0 / math.sqrt(grid_cells))
    own[0, C : C + 8, :] = tail * (1.0 / math.sqrt(grid_cells))

    def lon_copy(off):
        return remote(
            own.at[0], ar1.at[lon], ar1_send.at[off], ar1_recv.at[lon],
            lat, lax.rem(lon + off, n_lon),
        )

    def lon_wait(off):
        q = lax.rem(lon + n_lon - off, n_lon)
        return remote(own.at[0], ar1.at[q], ar1_send.at[off], ar1_recv.at[q], lat, q)

    def lat_copy(off):
        return remote(
            own.at[1], ar2.at[lat], ar2_send.at[off], ar2_recv.at[lat],
            lax.rem(lat + off, n_lat), lon,
        )

    def lat_wait(off):
        q = lax.rem(lat + n_lat - off, n_lat)
        return remote(own.at[1], ar2.at[q], ar2_send.at[off], ar2_recv.at[q], q, lon)

    def run(count, act):
        def body(off, _):
            act(off)
            return 0

        lax.fori_loop(1, count, body, 0)

    run(n_lon, lambda off: lon_copy(off).start())
    ar1[lon] = own[0]

    def keep_grad(r, _):
        keep(0, r, ya[H + r, O : O + B, :])
        return 0

    lax.fori_loop(0, R, keep_grad, 0, unroll=4)
    groups(ya)
    step_inside(ya, yb, 1)
    step_inside(yb, ya, 2)
    step_inside(ya, yb, 3)
    step_inside(yb, ya, 4)
    for copy in second_halo:
        copy.wait()
    assemble(1, ya, north_ok, south_ok)

    step_rim(ya, yb, 1)

    run(n_lon, lambda off: lon_wait(off).wait())
    total = ar1[0]
    for q in range(1, n_lon):
        total = total + ar1[q]
    own[1] = total
    run(n_lat, lambda off: lat_copy(off).start())
    ar2[lat] = total

    step_rim(yb, ya, 2)
    step_rim(ya, yb, 3)
    step_rim(yb, ya, 4)

    def finish(p, _):
        t = terms[pl.ds(pl.multiple_of(2 * p * B, 2 * B), 2 * B), :]
        res = lax.dot_general(wb[...], t, NT, preferred_element_type=F32)
        for j in range(2):
            for g in range(RG):
                row = R * g + 2 * p + j
                s = jnp.broadcast_to(snat[pl.ds(row, 1), :], (C, B))
                part = res[g * C : (g + 1) * C, j * B : (j + 1) * B]
                xf[pl.ds(row, C, stride=B), :] = part * s
        return 0

    lax.fori_loop(0, R // 2, finish, 0, unroll=4)

    for c in range(C):
        out_v[c] = xf[c * B : (c + 1) * B, :].astype(BF16)

    run(n_lat, lambda off: lat_wait(off).wait())
    total = ar2[0]
    for q in range(1, n_lat):
        total = total + ar2[q]
    sum_ref[...] = total


def close(out_v, sum_ref, out_hbm, wg_ref, out_sem):
    copy = pltpu.make_async_copy(out_v, out_hbm, out_sem)
    copy.start()
    total = sum_ref[...]
    flat = total[0:C].T
    for k in range(K):
        wg_ref[k] = flat[k * C : (k + 1) * C, :]
    last = total[C : C + 8]
    last = jnp.concatenate(
        [last if g == 0 else pltpu.roll(last, B - C * g, 1) for g in range(RG)], axis=0
    )
    wg_ref[K] = last.T[0:C, :]
    copy.wait()


def solution(mesh):
    n_lat, n_lon = mesh.shape["lat"], mesh.shape["lon"]
    hbm = pl.BlockSpec(memory_space=pltpu.HBM)
    sem = pltpu.SemaphoreType.DMA

    def local(features, cotangent, sea_mask, weights):
        vmem = pl.BlockSpec(memory_space=pltpu.VMEM)
        carried = (
            pltpu.VMEM((C, B, B), BF16),
            pltpu.VMEM((C + 8, B), F32),
        )
        carried = pl.pallas_call(
            functools.partial(kernel, n_lat, n_lon),
            out_shape=carried,
            in_specs=[hbm] * 4,
            out_specs=(vmem,) * 2,
            scratch_shapes=[
                pltpu.VMEM((C, B, B), BF16),
                pltpu.VMEM((C, B, B), BF16),
                pltpu.VMEM((B, B), jnp.int32),
                pltpu.VMEM((K + 1, C, C), BF16),
                pltpu.VMEM((C * B, B), F32),
                pltpu.VMEM((C * B, B), F32),
                pltpu.VMEM((RE, CP, B), F32),
                pltpu.VMEM((RE, CP, B), F32),
                pltpu.VMEM((RE, CE, B), F32),
                pltpu.VMEM((RE, CE, B), F32),
                pltpu.VMEM((R * B, (K + 1) * B), BF16),
                pltpu.VMEM((B, R * B), BF16),
                pltpu.VMEM((4, 8, B), F32),
                pltpu.VMEM((8, 8, B), F32),
                pltpu.VMEM((2, CP, B), F32),
                pltpu.VMEM((CE, 2 * B), F32),
                pltpu.VMEM((B, B), F32),
                pltpu.VMEM((B, (K + 1) * B), BF16),
                pltpu.VMEM((B, (K + 1) * B), BF16),
                pltpu.VMEM((CE, 2 * B), BF16),
                pltpu.VMEM((2, 2, B, B), F32),
                pltpu.VMEM((2, 2, R // 2, 8, B), F32),
                pltpu.VMEM((2, 2, CE, B), F32),
                pltpu.VMEM((2, 2, R // 2, 8, B), F32),
                pltpu.VMEM((2, C + 8, B), F32),
                pltpu.VMEM((n_lon, C + 8, B), F32),
                pltpu.VMEM((n_lat, C + 8, B), F32),
                sem((4,)), sem((8,)), sem((8,)), sem((2, 16)), sem((2, 16)),
                sem((n_lon,)), sem((n_lon,)), sem((n_lat,)), sem((n_lat,)),
            ],
            compiler_params=pltpu.CompilerParams(
                collective_id=0, has_side_effects=True, vmem_limit_bytes=62 << 20
            ),
        )(features, cotangent, sea_mask, weights)
        return pl.pallas_call(
            close,
            out_shape=(
                jax.ShapeDtypeStruct((C, B, B), BF16),
                jax.ShapeDtypeStruct((K + 1, C, C), F32),
            ),
            in_specs=[vmem] * 2,
            out_specs=(hbm, vmem),
            scratch_shapes=[sem(())],
            compiler_params=pltpu.CompilerParams(vmem_limit_bytes=4 << 20),
        )(*carried)

    placed = (P(None, "lat", "lon"), P(None, "lat", "lon"), P("lat", "lon"), P())
    return jax.shard_map(
        local, mesh=mesh, in_specs=placed, out_specs=(P(None, "lat", "lon"), P()), check_vma=False
    )
```

```python
import functools
import math

import jax
import jax.numpy as jnp
from jax import lax
from jax.experimental import pallas as pl
from jax.experimental.pallas import tpu as pltpu
from jax.sharding import PartitionSpec as P

K = 4
C = 32
B = 128
RG = 4
R = B // RG
H = 4
RE = R + 2 * H
CE = B + 16
CP = CE + 16
O = 16
F32 = jnp.float32
BF16 = jnp.bfloat16
NT = (((1,), (1,)), ((), ()))


def kernel(
    n_lat, n_lon,
    feat_hbm, cot_hbm, mask_hbm, w_hbm,
    out_v, sum_ref,
    feat_v, cot_v, mask_v, w_v, xf, cf,
    ya, yb, coef, scale, terms, gcat,
    mtx, mrx, sm, vm, snat, wf, wb, sel,
    pack, cpack, lrow, lcol, own, ar1, ar2,
    in_sem, mask_send, mask_recv, halo_send, halo_recv,
    ar1_send, ar1_recv, ar2_send, ar2_recv,
):
    lat = lax.axis_index("lat")
    lon = lax.axis_index("lon")
    north, south = lax.rem(lat + n_lat - 1, n_lat), lax.rem(lat + 1, n_lat)
    west, east = lax.rem(lon + n_lon - 1, n_lon), lax.rem(lon + 1, n_lon)

    feat_in = pltpu.make_async_copy(feat_hbm, feat_v, in_sem.at[0])
    cot_in = pltpu.make_async_copy(cot_hbm, cot_v, in_sem.at[1])
    mask_in = pltpu.make_async_copy(mask_hbm, mask_v, in_sem.at[2])
    w_in = pltpu.make_async_copy(w_hbm, w_v, in_sem.at[3])
    mask_in.start()
    feat_in.start()
    w_in.start()
    cot_in.start()

    barrier = pltpu.get_barrier_semaphore()

    def greet(i, j):
        pl.semaphore_signal(
            barrier, inc=1, device_id=(i, j), device_id_type=pl.DeviceIdType.MESH
        )

    for i in (north, south):
        for j in (west, east):
            greet(i, j)

    def greet_lon(off, _):
        greet(lat, lax.rem(lon + off, n_lon))
        return 0

    def greet_lat(off, _):
        greet(lax.rem(lat + off, n_lat), lon)
        return 0

    lax.fori_loop(1, n_lon, greet_lon, 0)
    lax.fori_loop(1, n_lat, greet_lat, 0)

    row_i = lax.broadcasted_iota(jnp.int32, (B, B), 0)
    col_i = lax.broadcasted_iota(jnp.int32, (B, B), 1)
    sel_r = lax.broadcasted_iota(jnp.int32, (CE, 2 * B), 0)
    sel_c = lax.broadcasted_iota(jnp.int32, (CE, 2 * B), 1)
    inside = (sel_r >= 8) & (sel_r < 8 + B) & (sel_c == sel_r - 8)
    left = (sel_r < 8) & (sel_c == 2 * B - 8 + sel_r)
    right = (sel_r >= 8 + B) & (sel_c == sel_r - 8)
    sel[...] = (inside | left | right).astype(F32).astype(BF16)

    mask_in.wait()
    flags = mask_v[...].astype(F32)
    turned_flags = flags.T
    mtx[0] = flags[B - 8 :]
    mtx[1] = flags[:8]
    mtx[2] = turned_flags[B - 8 :]
    mtx[3] = turned_flags[:8]
    pl.semaphore_wait(barrier, 4 + (n_lon - 1) + (n_lat - 1))

    def remote(src, dst, send, recv, i, j):
        return pltpu.make_async_remote_copy(
            src_ref=src, dst_ref=dst, send_sem=send, recv_sem=recv,
            device_id=(i, j), device_id_type=pl.DeviceIdType.MESH,
        )

    mid = pl.ds(8, B)
    above, below = pl.ds(0, 8), pl.ds(8 + B, 8)
    mask_plan = (
        (2, 0, lat, east),
        (3, 1, lat, west),
        (0, 2, south, lon),
        (1, 3, north, lon),
        (0, 4, south, east),
        (0, 5, south, west),
        (1, 6, north, east),
        (1, 7, north, west),
    )
    mask_copies = [
        remote(mtx.at[src], mrx.at[n], mask_send.at[n], mask_recv.at[n], i, j)
        for src, n, i, j in mask_plan
    ]
    for copy in mask_copies:
        copy.start()

    lane = lax.broadcasted_iota(jnp.int32, (B, B), 1)

    def halo_copies(phase):
        plan = (
            (pack.at[phase, 0], lrow.at[phase, 0, mid], south, lon),
            (pack.at[phase, 1], lrow.at[phase, 1, mid], north, lon),
            (pack.at[phase, 0, pl.ds(B - 8, 8)], lrow.at[phase, 0, above], south, east),
            (pack.at[phase, 0, pl.ds(0, 8)], lrow.at[phase, 0, below], south, west),
            (pack.at[phase, 1, pl.ds(B - 8, 8)], lrow.at[phase, 1, above], north, east),
            (pack.at[phase, 1, pl.ds(0, 8)], lrow.at[phase, 1, below], north, west),
        ) + tuple(
            (cpack.at[phase, side, at], lcol.at[phase, side, at], lat, (east, west)[side])
            for at in (pl.ds(0, 2), pl.ds(14, 2), pl.ds(2, 4), pl.ds(6, 4), pl.ds(10, 4))
            for side in range(2)
        )
        return [
            remote(src, dst, halo_send.at[phase, n], halo_recv.at[phase, n], i, j)
            for n, (src, dst, i, j) in enumerate(plan)
        ]

    def pack_rows(phase, y):
        last, first = None, None
        for i in range(H):
            a = pltpu.roll(y[H + R - H + i, O : O + B, :], (32 * i + 32) % 128, 1)
            b = pltpu.roll(y[H + i, O : O + B, :], (32 * i) % 128, 1)
            here = (lane >= 32 * i) & (lane < 32 * i + 32)
            last = a if last is None else jnp.where(here, a, last)
            first = b if first is None else jnp.where(here, b, first)
        pack[phase, 0] = last
        pack[phase, 1] = first

    half = lax.broadcasted_iota(jnp.int32, (8, B), 0) < 4

    def pack_columns(phase, y, p):
        a, b = y[H + 2 * p, O + B - 8 : O + B, :], y[H + 2 * p + 1, O + B - 8 : O + B, :]
        cpack[phase, 0, p] = jnp.where(half, pltpu.roll(a, 4, 0), b)
        a, b = y[H + 2 * p, O : O + 8, :], y[H + 2 * p + 1, O : O + 8, :]
        cpack[phase, 1, p] = jnp.where(half, a, pltpu.roll(b, 4, 0))

    def send_chunks(phase, y, copies, turn_rows):
        turn_rows(0, H)
        turn_rows(R - H, H)
        for p in (0, 1, 14, 15):
            pack_columns(phase, y, p)
        pack_rows(phase, y)
        for copy in copies[:10]:
            copy.start()
        for n in range(3):
            turn_rows(H + 8 * n, 8)
            for p in range(2 + 4 * n, 6 + 4 * n):
                pack_columns(phase, y, p)
            for copy in copies[10 + 2 * n : 12 + 2 * n]:
                copy.start()

    feat_in.wait()

    def widen(src, dst):
        def body(c, _):
            dst[pl.ds(pl.multiple_of(c * B, B), B), :] = src[c].astype(F32)
            return 0

        lax.fori_loop(0, C, body, 0, unroll=4)

    def rows_of(flat, r):
        return jnp.concatenate(
            [flat[pl.ds(R * g + r, C, stride=B), :] for g in range(RG)], axis=0
        )

    widen(feat_v, xf)

    def turn(r):
        yb[H + r, O : O + B, :] = rows_of(xf, r).T

    def turn_rows(first, count):
        for r in range(first, first + count):
            turn(r)

    first_halo = halo_copies(0)
    send_chunks(0, yb, first_halo, turn_rows)

    w_in.wait()
    block = (row_i // C) == (col_i // C)
    for k in range(K + 1):
        one = w_v[k].astype(F32)
        wide = jnp.concatenate([one] * RG, axis=1)
        full = jnp.where(block, jnp.concatenate([wide] * RG, axis=0), 0.0)
        wb[:, k * B : (k + 1) * B] = full.astype(BF16)
        wf[:, k * B : (k + 1) * B] = full.T.astype(BF16)

    cot_in.wait()
    widen(cot_v, cf)

    lane_e = lax.broadcasted_iota(jnp.int32, (CE, B), 1)
    sm[...] = jnp.zeros_like(sm)
    sm[0, 16 : 16 + B, :] = mask_v[...].astype(F32)

    def ring(main, side, shift, edge):
        m, s = pltpu.roll(main, shift, 1), pltpu.roll(side, shift, 1)
        at = lane_e == edge
        return jnp.where(at, s, m), jnp.where(at, m, s)

    def degrees():
        here = [sm[t, 8 : 8 + CE, :] for t in range(2)]
        up = [sm[t, 7 : 7 + CE, :] for t in range(2)]
        down = [sm[t, 9 : 9 + CE, :] for t in range(2)]
        from_left = ring(here[0] + down[0], here[1] + down[1], 1, 0)
        from_right = ring(here[0] + up[0], here[1] + up[1], B - 1, B - 1)
        for t in range(2):
            degree = from_left[t] + from_right[t] + up[t] + down[t]
            vm[:, t * B : (t + 1) * B] = here[t] * jnp.maximum(degree, 1.0)
            if t == 0:
                snat[...] = jnp.sqrt(jnp.maximum(degree, 1.0)[8 : 8 + B])

    def values(p, pick):
        rows = jnp.concatenate(
            [
                jnp.broadcast_to(vm[pl.ds(8 - H + R * g + 2 * p + j, 1), :], (C, 2 * B))
                for j in range(2)
                for g in range(RG)
            ],
            axis=0,
        )
        v = lax.dot_general(pick, rows.astype(BF16), NT, preferred_element_type=F32)
        m = jnp.maximum(v, 1.0)
        rs = lax.rsqrt(m)
        return jnp.where(v > 0.5, -2.0 * rs * rs, 0.0), m * rs

    def spread(p, _):
        a, s = values(p, sel[...])
        for j in range(2):
            coef[2 * p + j] = a[:, j * B : (j + 1) * B]
            scale[2 * p + j] = s[:, j * B : (j + 1) * B]
        return 0

    def spread_sides(p, _):
        a, s = values(p, jnp.concatenate([sel[0:16, :], sel[CE - 16 :, :]], axis=0))
        for j in range(2):
            for ref, part in ((coef, a), (scale, s)):
                ref[2 * p + j, 0:16, :] = part[0:16, j * B : (j + 1) * B]
                ref[2 * p + j, CE - 16 :, :] = part[16:32, j * B : (j + 1) * B]
        return 0

    degrees()
    lax.fori_loop(3, RE // 2 - 3, spread, 0, unroll=7)

    def groups(y):
        for i in range(H):
            y[i, O : O + B, :] = pltpu.roll(y[R + i, O : O + B, :], C, 1)
            y[H + R + i, O : O + B, :] = pltpu.roll(y[H + i, O : O + B, :], B - C, 1)

    def beside(y, at, row, shift):
        return jnp.concatenate(
            [
                pltpu.roll(y[row, O - 8 : O, :], shift, 1),
                y[at, O : O + B, :],
                pltpu.roll(y[row, O + B : O + B + 8, :], shift, 1),
            ],
            axis=0,
        )

    def assemble(phase, y, ok_north, ok_south):
        for p in range(R // 2):
            a, b = lcol[phase, 0, p], lcol[phase, 1, p]
            y[H + 2 * p, O - 8 : O, :] = pltpu.roll(a, 4, 0)
            y[H + 2 * p + 1, O - 8 : O, :] = a
            y[H + 2 * p, O + B : O + B + 8, :] = b
            y[H + 2 * p + 1, O + B : O + B + 8, :] = pltpu.roll(b, 4, 0)
        for i in range(H):
            own_up = beside(y, i, R + i, C)
            far_up = pltpu.roll(lrow[phase, 0], (B - 32 * i) % B, 1) * ok_north
            y[i, O - 8 : O + B + 8, :] = jnp.where(lane_e < 32, far_up, own_up)
            own_down = beside(y, H + R + i, H + i, B - C)
            far_down = pltpu.roll(lrow[phase, 1], (96 - 32 * i) % B, 1) * ok_south
            y[H + R + i, O - 8 : O + B + 8, :] = jnp.where(
                lane_e >= 96, far_down, own_down
            )

    def keep(k, r, value):
        terms[pl.ds(pl.multiple_of(r * B, B), B), k * B : (k + 1) * B] = value.astype(BF16)

    def cells(src, dst, k, scaled, bands, rows, unroll):
        def sums(r, first, size):
            mid_ = src[r, first : first + size, :]
            low = src[r, first - 1 : first - 1 + size, :]
            high = src[r, first + 1 : first + 1 + size, :]
            return mid_ + high, low + high, mid_ + low

        def advance(r, carried, keeps):
            after = []
            for (first, size), (e0, e1, f1) in zip(bands, carried):
                e2, f2, h2 = sums(r + 1, first, size)
                total = coef[r, first - O + 8 : first - O + 8 + size, :] * (e0 + f1 + h2)
                if k == 1:
                    value = 0.5 * total
                else:
                    value = total - dst[r, first : first + size, :]
                dst[r, first : first + size, :] = value
                lo, hi = max(first, O), min(first + size, O + B)
                if keeps:
                    at = (r - H) * B + lo - O
                    if not isinstance(r, int):
                        at = pl.multiple_of(at, 8)
                    kept = value[lo - first : hi - first]
                    if scaled:
                        kept = kept * scale[r, lo - O + 8 : hi - O + 8, :]
                    terms[pl.ds(at, hi - lo), k * B : (k + 1) * B] = kept.astype(BF16)
                after.append((e1, e2, f2))
            return tuple(after)

        low, high = rows
        carried = tuple(
            (sums(low - 1, *band)[0],) + sums(low, *band)[:2] for band in bands
        )
        if unroll:
            lax.fori_loop(
                low, high, lambda r, c: advance(r, c, True), carried, unroll=unroll
            )
        else:
            for r in range(low, high):
                carried = advance(r, carried, H <= r < H + R)

    def inner_rows(k, less):
        low, high = H + k + less, H + R - k - less
        return (low, high), {30: 6, 28: 7, 26: 13, 24: 8, 22: 11, 20: 10}[high - low]

    def step_inside(src, dst, k, scaled, less):
        first, last = O + 8 * k, O + B - 8 * k
        size = (last - first) // (1 if k == K else 2)
        for at in range(first, last, size):
            cells(src, dst, k, scaled, ((at, size),), *inner_rows(k, less))

    def step_rim(src, dst, k, scaled, less):
        reach = K - k
        first, last = (O - 8, O + B + 8) if reach else (O, O + B)
        size = 48 if reach else 64
        for low in (H - reach, H + R - k - less):
            for at in range(first, last, size):
                cells(src, dst, k, scaled, ((at, size),), (low, low + K + less), 0)
        width = O + 8 * k - first
        bands = ((first, width), (last - width, width))
        cells(src, dst, k, scaled, bands, *inner_rows(k, less))

    def start_row(r, first, last):
        at = slice(first - O + 8, last - O + 8)
        value = (-0.5 * coef[r, at, :] * scale[r, at, :]) * yb[r, first:last, :]
        ya[r, first:last, :] = value
        return value * scale[r, at, :]

    def start_inner(r, _):
        keep(0, r - H, start_row(r, O, O + B))
        return 0

    groups(yb)
    lax.fori_loop(6, RE - 6, start_inner, 0, unroll=7)
    step_inside(ya, yb, 1, True, 2)
    step_inside(yb, ya, 2, True, 2)
    step_inside(ya, yb, 3, True, 2)
    step_inside(yb, ya, 4, True, 2)

    for copy in mask_copies:
        copy.wait()
    north_ok = (lat > 0).astype(F32)
    south_ok = (lat < n_lat - 1).astype(F32)
    low_lanes = lane_e[0:8] < 64
    sm[0, 8:16, :] = mrx[2] * north_ok
    sm[0, 16 + B : 24 + B, :] = mrx[3] * south_ok
    sm[1, 8:16, :] = jnp.where(low_lanes, mrx[5], mrx[4]) * north_ok
    sm[1, 16 : 16 + B, :] = jnp.concatenate(
        [mrx[1], jnp.zeros((B - 16, B), F32), mrx[0]], axis=0
    ).T
    sm[1, 16 + B : 24 + B, :] = jnp.where(low_lanes, mrx[7], mrx[6]) * south_ok
    degrees()
    for p in (0, 1, 2, 17, 18, 19):
        spread(p, 0)
    lax.fori_loop(3, RE // 2 - 3, spread_sides, 0, unroll=7)

    for copy in first_halo:
        copy.wait()
    assemble(0, yb, 1.0, 1.0)
    for r in tuple(range(6)) + tuple(range(RE - 6, RE)):
        value = start_row(r, O - 8, O + B + 8)
        if H <= r < H + R:
            keep(0, r - H, value[8 : 8 + B])

    def start_sides(r, _):
        left = start_row(r, O - 8, O + 8)
        right = start_row(r, O + B - 8, O + B + 8)
        at = pl.multiple_of((r - H) * B, B)
        terms[pl.ds(at, 8), 0:B] = left[8:16].astype(BF16)
        terms[pl.ds(at + B - 8, 8), 0:B] = right[0:8].astype(BF16)
        return 0

    lax.fori_loop(6, RE - 6, start_sides, 0, unroll=7)
    step_rim(ya, yb, 1, True, 2)
    step_rim(yb, ya, 2, True, 2)
    step_rim(ya, yb, 3, True, 2)
    step_rim(yb, ya, 4, True, 2)


    def mix(p):
        at = pl.ds(pl.multiple_of(2 * p * B, 2 * B), 2 * B)
        mixed = lax.dot_general(wf[...], terms[at, :], NT, preferred_element_type=F32)
        act = jnp.tanh(mixed)
        cot = jnp.concatenate([rows_of(cf, 2 * p), rows_of(cf, 2 * p + 1)], axis=1)
        gcat[:, at] = (cot * (1.0 - act * act)).astype(BF16)

    def turn_grad(r):
        grad = gcat[:, pl.ds(pl.multiple_of(r * B, B), B)].astype(F32)
        w = -0.5 * coef[H + r, 8 : 8 + B, :] * scale[H + r, 8 : 8 + B, :]
        ya[H + r, O : O + B, :] = w * grad.T

    def grad_rows(first, count):
        for p in range(first // 2, (first + count) // 2):
            mix(p)
        for r in range(first, first + count):
            turn_grad(r)

    second_halo = halo_copies(1)
    send_chunks(1, ya, second_halo, grad_rows)

    chunk = 8 * B
    acc = None
    for n in range(R * B // chunk):
        part = jnp.dot(
            gcat[:, n * chunk : (n + 1) * chunk],
            terms[n * chunk : (n + 1) * chunk, :],
            preferred_element_type=F32,
        )
        acc = part if acc is None else acc + part
    lane_c = lax.broadcasted_iota(jnp.int32, (C, B), 1) // C
    folded = []
    for k in range(K + 1):
        tot = None
        for g in range(RG):
            piece = acc[g * C : (g + 1) * C, k * B : (k + 1) * B]
            tot = piece if tot is None else jnp.where(lane_c == g, piece, tot)
        tot = tot + pltpu.roll(tot, 64, 1)
        tot = tot + pltpu.roll(tot, 32, 1)
        folded.append(tot)
    head = folded[0]
    for k in range(1, K):
        head = jnp.where(lane_c == k, folded[k], head)
    tail = folded[K][0:8]
    for g in range(1, RG):
        tail = jnp.where(lane_c[0:8] == g, folded[K][8 * g : 8 * g + 8], tail)
    grid_cells = n_lat * n_lon * B * B
    own[0, 0:C, :] = head * (1.0 / math.sqrt(grid_cells))
    own[0, C : C + 8, :] = tail * (1.0 / math.sqrt(grid_cells))

    def lon_copy(off):
        return remote(
            own.at[0], ar1.at[lon], ar1_send.at[off], ar1_recv.at[lon],
            lat, lax.rem(lon + off, n_lon),
        )

    def lon_wait(off):
        q = lax.rem(lon + n_lon - off, n_lon)
        return remote(own.at[0], ar1.at[q], ar1_send.at[off], ar1_recv.at[q], lat, q)

    def lat_copy(off):
        return remote(
            own.at[1], ar2.at[lat], ar2_send.at[off], ar2_recv.at[lat],
            lax.rem(lat + off, n_lat), lon,
        )

    def lat_wait(off):
        q = lax.rem(lat + n_lat - off, n_lat)
        return remote(own.at[1], ar2.at[q], ar2_send.at[off], ar2_recv.at[q], q, lon)

    def run(count, act):
        def body(off, _):
            act(off)
            return 0

        lax.fori_loop(1, count, body, 0)

    run(n_lon, lambda off: lon_copy(off).start())
    ar1[lon] = own[0]

    def keep_grad(r, _):
        keep(0, r, ya[H + r, O : O + B, :])
        return 0

    lax.fori_loop(0, R, keep_grad, 0, unroll=4)
    groups(ya)
    step_inside(ya, yb, 1, False, 0)
    step_inside(yb, ya, 2, False, 0)
    step_inside(ya, yb, 3, False, 0)
    step_inside(yb, ya, 4, False, 0)
    for copy in second_halo:
        copy.wait()
    assemble(1, ya, north_ok, south_ok)

    step_rim(ya, yb, 1, False, 0)

    run(n_lon, lambda off: lon_wait(off).wait())
    total = ar1[0]
    for q in range(1, n_lon):
        total = total + ar1[q]
    own[1] = total
    run(n_lat, lambda off: lat_copy(off).start())
    ar2[lat] = total

    step_rim(yb, ya, 2, False, 0)
    step_rim(ya, yb, 3, False, 0)
    step_rim(yb, ya, 4, False, 0)

    def finish(p, _):
        t = terms[pl.ds(pl.multiple_of(2 * p * B, 2 * B), 2 * B), :]
        res = lax.dot_general(wb[...], t, NT, preferred_element_type=F32)
        for j in range(2):
            for g in range(RG):
                row = R * g + 2 * p + j
                s = jnp.broadcast_to(snat[pl.ds(row, 1), :], (C, B))
                part = res[g * C : (g + 1) * C, j * B : (j + 1) * B]
                xf[pl.ds(row, C, stride=B), :] = part * s
        return 0

    lax.fori_loop(0, R // 2, finish, 0, unroll=4)

    for c in range(C):
        out_v[c] = xf[c * B : (c + 1) * B, :].astype(BF16)

    run(n_lat, lambda off: lat_wait(off).wait())
    total = ar2[0]
    for q in range(1, n_lat):
        total = total + ar2[q]
    sum_ref[...] = total


def close(out_v, sum_ref, out_hbm, wg_ref, out_sem):
    copy = pltpu.make_async_copy(out_v, out_hbm, out_sem)
    copy.start()
    total = sum_ref[...]
    flat = total[0:C].T
    for k in range(K):
        wg_ref[k] = flat[k * C : (k + 1) * C, :]
    last = total[C : C + 8]
    last = jnp.concatenate(
        [last if g == 0 else pltpu.roll(last, B - C * g, 1) for g in range(RG)], axis=0
    )
    wg_ref[K] = last.T[0:C, :]
    copy.wait()


def solution(mesh):
    n_lat, n_lon = mesh.shape["lat"], mesh.shape["lon"]
    hbm = pl.BlockSpec(memory_space=pltpu.HBM)
    sem = pltpu.SemaphoreType.DMA

    def local(features, cotangent, sea_mask, weights):
        vmem = pl.BlockSpec(memory_space=pltpu.VMEM)
        carried = (
            pltpu.VMEM((C, B, B), BF16),
            pltpu.VMEM((C + 8, B), F32),
        )
        carried = pl.pallas_call(
            functools.partial(kernel, n_lat, n_lon),
            out_shape=carried,
            in_specs=[hbm] * 4,
            out_specs=(vmem,) * 2,
            scratch_shapes=[
                pltpu.VMEM((C, B, B), BF16),
                pltpu.VMEM((C, B, B), BF16),
                pltpu.VMEM((B, B), jnp.int32),
                pltpu.VMEM((K + 1, C, C), BF16),
                pltpu.VMEM((C * B, B), F32),
                pltpu.VMEM((C * B, B), F32),
                pltpu.VMEM((RE, CP, B), F32),
                pltpu.VMEM((RE, CP, B), F32),
                pltpu.VMEM((RE, CE, B), F32),
                pltpu.VMEM((RE, CE, B), F32),
                pltpu.VMEM((R * B, (K + 1) * B), BF16),
                pltpu.VMEM((B, R * B), BF16),
                pltpu.VMEM((4, 8, B), F32),
                pltpu.VMEM((8, 8, B), F32),
                pltpu.VMEM((2, CP, B), F32),
                pltpu.VMEM((CE, 2 * B), F32),
                pltpu.VMEM((B, B), F32),
                pltpu.VMEM((B, (K + 1) * B), BF16),
                pltpu.VMEM((B, (K + 1) * B), BF16),
                pltpu.VMEM((CE, 2 * B), BF16),
                pltpu.VMEM((2, 2, B, B), F32),
                pltpu.VMEM((2, 2, R // 2, 8, B), F32),
                pltpu.VMEM((2, 2, CE, B), F32),
                pltpu.VMEM((2, 2, R // 2, 8, B), F32),
                pltpu.VMEM((2, C + 8, B), F32),
                pltpu.VMEM((n_lon, C + 8, B), F32),
                pltpu.VMEM((n_lat, C + 8, B), F32),
                sem((4,)), sem((8,)), sem((8,)), sem((2, 16)), sem((2, 16)),
                sem((n_lon,)), sem((n_lon,)), sem((n_lat,)), sem((n_lat,)),
            ],
            compiler_params=pltpu.CompilerParams(
                collective_id=0, has_side_effects=True, vmem_limit_bytes=62 << 20
            ),
        )(features, cotangent, sea_mask, weights)
        return pl.pallas_call(
            close,
            out_shape=(
                jax.ShapeDtypeStruct((C, B, B), BF16),
                jax.ShapeDtypeStruct((K + 1, C, C), F32),
            ),
            in_specs=[vmem] * 2,
            out_specs=(hbm, vmem),
            scratch_shapes=[sem(())],
            compiler_params=pltpu.CompilerParams(vmem_limit_bytes=4 << 20),
        )(*carried)

    placed = (P(None, "lat", "lon"), P(None, "lat", "lon"), P("lat", "lon"), P())
    return jax.shard_map(
        local, mesh=mesh, in_specs=placed, out_specs=(P(None, "lat", "lon"), P()), check_vma=False
    )
```

```python
import functools
import math

import jax
import jax.numpy as jnp
from jax import lax
from jax.experimental import pallas as pl
from jax.experimental.pallas import tpu as pltpu
from jax.sharding import PartitionSpec as P

K = 4
C = 32
B = 128
RG = 4
R = B // RG
H = 4
RE = R + 2 * H
CE = B + 16
CP = CE + 16
O = 16
F32 = jnp.float32
BF16 = jnp.bfloat16
NT = (((1,), (1,)), ((), ()))


def kernel(
    n_lat, n_lon,
    feat_hbm, cot_hbm, mask_hbm, w_hbm,
    out_v, sum_ref,
    feat_v, cot_v, mask_v, w_v, xf, cf,
    ya, yb, coef, scale, terms, gcat,
    mtx, mrx, sm, vm, snat, wf, wb, sel,
    pack, cpack, lrow, lcol, own, ar1, ar2,
    in_sem, mask_send, mask_recv, halo_send, halo_recv,
    ar1_send, ar1_recv, ar2_send, ar2_recv,
):
    lat = lax.axis_index("lat")
    lon = lax.axis_index("lon")
    north, south = lax.rem(lat + n_lat - 1, n_lat), lax.rem(lat + 1, n_lat)
    west, east = lax.rem(lon + n_lon - 1, n_lon), lax.rem(lon + 1, n_lon)

    part = C // 4
    feat_in = [
        pltpu.make_async_copy(
            feat_hbm.at[pl.ds(n * part, part)], feat_v.at[pl.ds(n * part, part)], in_sem.at[4 + n]
        )
        for n in range(4)
    ]
    cot_in = pltpu.make_async_copy(cot_hbm, cot_v, in_sem.at[1])
    mask_in = pltpu.make_async_copy(mask_hbm, mask_v, in_sem.at[2])
    w_in = pltpu.make_async_copy(w_hbm, w_v, in_sem.at[3])
    mask_in.start()
    for copy in feat_in:
        copy.start()
    w_in.start()
    cot_in.start()

    barrier = pltpu.get_barrier_semaphore()

    def greet(i, j):
        pl.semaphore_signal(
            barrier, inc=1, device_id=(i, j), device_id_type=pl.DeviceIdType.MESH
        )

    for i in (north, south):
        for j in (west, east):
            greet(i, j)

    def greet_lon(off, _):
        greet(lat, lax.rem(lon + off, n_lon))
        return 0

    def greet_lat(off, _):
        greet(lax.rem(lat + off, n_lat), lon)
        return 0

    lax.fori_loop(1, n_lon, greet_lon, 0)
    lax.fori_loop(1, n_lat, greet_lat, 0)

    row_i = lax.broadcasted_iota(jnp.int32, (B, B), 0)
    col_i = lax.broadcasted_iota(jnp.int32, (B, B), 1)
    sel_r = lax.broadcasted_iota(jnp.int32, (CE, 2 * B), 0)
    sel_c = lax.broadcasted_iota(jnp.int32, (CE, 2 * B), 1)
    inside = (sel_r >= 8) & (sel_r < 8 + B) & (sel_c == sel_r - 8)
    left = (sel_r < 8) & (sel_c == 2 * B - 8 + sel_r)
    right = (sel_r >= 8 + B) & (sel_c == sel_r - 8)
    sel[...] = (inside | left | right).astype(F32).astype(BF16)

    mask_in.wait()
    flags = mask_v[...].astype(F32)
    turned_flags = flags.T
    mtx[0] = flags[B - 8 :]
    mtx[1] = flags[:8]
    mtx[2] = turned_flags[B - 8 :]
    mtx[3] = turned_flags[:8]
    pl.semaphore_wait(barrier, 4 + (n_lon - 1) + (n_lat - 1))

    def remote(src, dst, send, recv, i, j):
        return pltpu.make_async_remote_copy(
            src_ref=src, dst_ref=dst, send_sem=send, recv_sem=recv,
            device_id=(i, j), device_id_type=pl.DeviceIdType.MESH,
        )

    mid = pl.ds(8, B)
    above, below = pl.ds(0, 8), pl.ds(8 + B, 8)
    mask_plan = (
        (2, 0, lat, east),
        (3, 1, lat, west),
        (0, 2, south, lon),
        (1, 3, north, lon),
        (0, 4, south, east),
        (0, 5, south, west),
        (1, 6, north, east),
        (1, 7, north, west),
    )
    mask_copies = [
        remote(mtx.at[src], mrx.at[n], mask_send.at[n], mask_recv.at[n], i, j)
        for src, n, i, j in mask_plan
    ]
    for copy in mask_copies:
        copy.start()

    lane = lax.broadcasted_iota(jnp.int32, (B, B), 1)

    def halo_copies(phase):
        plan = (
            (pack.at[phase, 0], lrow.at[phase, 0, mid], south, lon),
            (pack.at[phase, 1], lrow.at[phase, 1, mid], north, lon),
            (pack.at[phase, 0, pl.ds(B - 8, 8)], lrow.at[phase, 0, above], south, east),
            (pack.at[phase, 0, pl.ds(0, 8)], lrow.at[phase, 0, below], south, west),
            (pack.at[phase, 1, pl.ds(B - 8, 8)], lrow.at[phase, 1, above], north, east),
            (pack.at[phase, 1, pl.ds(0, 8)], lrow.at[phase, 1, below], north, west),
        ) + tuple(
            (cpack.at[phase, side, at], lcol.at[phase, side, at], lat, (east, west)[side])
            for at in (pl.ds(0, 2), pl.ds(14, 2), pl.ds(2, 4), pl.ds(6, 4), pl.ds(10, 4))
            for side in range(2)
        )
        return [
            remote(src, dst, halo_send.at[phase, n], halo_recv.at[phase, n], i, j)
            for n, (src, dst, i, j) in enumerate(plan)
        ]

    def pack_rows(phase, y):
        last, first = None, None
        for i in range(H):
            a = pltpu.roll(y[H + R - H + i, O : O + B, :], (32 * i + 32) % 128, 1)
            b = pltpu.roll(y[H + i, O : O + B, :], (32 * i) % 128, 1)
            here = (lane >= 32 * i) & (lane < 32 * i + 32)
            last = a if last is None else jnp.where(here, a, last)
            first = b if first is None else jnp.where(here, b, first)
        pack[phase, 0] = last
        pack[phase, 1] = first

    half = lax.broadcasted_iota(jnp.int32, (8, B), 0) < 4

    def pack_columns(phase, y, p):
        a, b = y[H + 2 * p, O + B - 8 : O + B, :], y[H + 2 * p + 1, O + B - 8 : O + B, :]
        cpack[phase, 0, p] = jnp.where(half, pltpu.roll(a, 4, 0), b)
        a, b = y[H + 2 * p, O : O + 8, :], y[H + 2 * p + 1, O : O + 8, :]
        cpack[phase, 1, p] = jnp.where(half, a, pltpu.roll(b, 4, 0))

    def send_chunks(phase, y, copies, turn_rows):
        turn_rows(0, H)
        turn_rows(R - H, H)
        for p in (0, 1, 14, 15):
            pack_columns(phase, y, p)
        pack_rows(phase, y)
        for copy in copies[:10]:
            copy.start()
        for n in range(3):
            turn_rows(H + 8 * n, 8)
            for p in range(2 + 4 * n, 6 + 4 * n):
                pack_columns(phase, y, p)
            for copy in copies[10 + 2 * n : 12 + 2 * n]:
                copy.start()


    def widen(src, dst, first, last):
        def body(c, _):
            dst[pl.ds(pl.multiple_of(c * B, B), B), :] = src[c].astype(F32)
            return 0

        lax.fori_loop(first, last, body, 0, unroll=4)

    def rows_of(flat, r):
        return jnp.concatenate(
            [flat[pl.ds(R * g + r, C, stride=B), :] for g in range(RG)], axis=0
        )

    for n in range(4):
        feat_in[n].wait()
        widen(feat_v, xf, n * part, (n + 1) * part)

    def turn(r):
        yb[H + r, O : O + B, :] = rows_of(xf, r).T

    def turn_rows(first, count):
        for r in range(first, first + count):
            turn(r)

    first_halo = halo_copies(0)
    send_chunks(0, yb, first_halo, turn_rows)

    w_in.wait()
    block = (row_i // C) == (col_i // C)
    for k in range(K + 1):
        one = w_v[k].astype(F32)
        wide = jnp.concatenate([one] * RG, axis=1)
        full = jnp.where(block, jnp.concatenate([wide] * RG, axis=0), 0.0)
        wb[:, k * B : (k + 1) * B] = full.astype(BF16)
        wf[:, k * B : (k + 1) * B] = full.T.astype(BF16)

    cot_in.wait()
    widen(cot_v, cf, 0, C)

    lane_e = lax.broadcasted_iota(jnp.int32, (CE, B), 1)
    sm[...] = jnp.zeros_like(sm)
    sm[0, 16 : 16 + B, :] = mask_v[...].astype(F32)

    def ring(main, side, shift, edge):
        m, s = pltpu.roll(main, shift, 1), pltpu.roll(side, shift, 1)
        at = lane_e == edge
        return jnp.where(at, s, m), jnp.where(at, m, s)

    def degrees():
        here = [sm[t, 8 : 8 + CE, :] for t in range(2)]
        up = [sm[t, 7 : 7 + CE, :] for t in range(2)]
        down = [sm[t, 9 : 9 + CE, :] for t in range(2)]
        from_left = ring(here[0] + down[0], here[1] + down[1], 1, 0)
        from_right = ring(here[0] + up[0], here[1] + up[1], B - 1, B - 1)
        for t in range(2):
            degree = from_left[t] + from_right[t] + up[t] + down[t]
            vm[:, t * B : (t + 1) * B] = here[t] * jnp.maximum(degree, 1.0)
            if t == 0:
                snat[...] = jnp.sqrt(jnp.maximum(degree, 1.0)[8 : 8 + B])

    def values(p, pick):
        rows = jnp.concatenate(
            [
                jnp.broadcast_to(vm[pl.ds(8 - H + R * g + 2 * p + j, 1), :], (C, 2 * B))
                for j in range(2)
                for g in range(RG)
            ],
            axis=0,
        )
        v = lax.dot_general(pick, rows.astype(BF16), NT, preferred_element_type=F32)
        m = jnp.maximum(v, 1.0)
        rs = lax.rsqrt(m)
        return jnp.where(v > 0.5, -2.0 * rs * rs, 0.0), m * rs

    def spread(p, _):
        a, s = values(p, sel[...])
        for j in range(2):
            coef[2 * p + j] = a[:, j * B : (j + 1) * B]
            scale[2 * p + j] = s[:, j * B : (j + 1) * B]
        return 0

    def spread_sides(p, _):
        a, s = values(p, jnp.concatenate([sel[0:16, :], sel[CE - 16 :, :]], axis=0))
        for j in range(2):
            for ref, part in ((coef, a), (scale, s)):
                ref[2 * p + j, 0:16, :] = part[0:16, j * B : (j + 1) * B]
                ref[2 * p + j, CE - 16 :, :] = part[16:32, j * B : (j + 1) * B]
        return 0

    degrees()
    lax.fori_loop(3, RE // 2 - 3, spread, 0, unroll=7)

    def groups(y):
        for i in range(H):
            y[i, O : O + B, :] = pltpu.roll(y[R + i, O : O + B, :], C, 1)
            y[H + R + i, O : O + B, :] = pltpu.roll(y[H + i, O : O + B, :], B - C, 1)

    def beside(y, at, row, shift):
        return jnp.concatenate(
            [
                pltpu.roll(y[row, O - 8 : O, :], shift, 1),
                y[at, O : O + B, :],
                pltpu.roll(y[row, O + B : O + B + 8, :], shift, 1),
            ],
            axis=0,
        )

    def assemble(phase, y, ok_north, ok_south):
        for p in range(R // 2):
            a, b = lcol[phase, 0, p], lcol[phase, 1, p]
            y[H + 2 * p, O - 8 : O, :] = pltpu.roll(a, 4, 0)
            y[H + 2 * p + 1, O - 8 : O, :] = a
            y[H + 2 * p, O + B : O + B + 8, :] = b
            y[H + 2 * p + 1, O + B : O + B + 8, :] = pltpu.roll(b, 4, 0)
        for i in range(H):
            own_up = beside(y, i, R + i, C)
            far_up = pltpu.roll(lrow[phase, 0], (B - 32 * i) % B, 1) * ok_north
            y[i, O - 8 : O + B + 8, :] = jnp.where(lane_e < 32, far_up, own_up)
            own_down = beside(y, H + R + i, H + i, B - C)
            far_down = pltpu.roll(lrow[phase, 1], (96 - 32 * i) % B, 1) * ok_south
            y[H + R + i, O - 8 : O + B + 8, :] = jnp.where(
                lane_e >= 96, far_down, own_down
            )

    def keep(k, r, value):
        terms[pl.ds(pl.multiple_of(r * B, B), B), k * B : (k + 1) * B] = value.astype(BF16)

    def cells(src, dst, k, scaled, bands, rows, unroll):
        def sums(r, first, size):
            mid_ = src[r, first : first + size, :]
            low = src[r, first - 1 : first - 1 + size, :]
            high = src[r, first + 1 : first + 1 + size, :]
            return mid_ + high, low + high, mid_ + low

        def advance(r, carried, keeps):
            after = []
            for (first, size), (e0, e1, f1) in zip(bands, carried):
                e2, f2, h2 = sums(r + 1, first, size)
                total = coef[r, first - O + 8 : first - O + 8 + size, :] * (e0 + f1 + h2)
                if k == 1:
                    value = 0.5 * total
                else:
                    value = total - dst[r, first : first + size, :]
                dst[r, first : first + size, :] = value
                lo, hi = max(first, O), min(first + size, O + B)
                if keeps:
                    at = (r - H) * B + lo - O
                    if not isinstance(r, int):
                        at = pl.multiple_of(at, 8)
                    kept = value[lo - first : hi - first]
                    if scaled:
                        kept = kept * scale[r, lo - O + 8 : hi - O + 8, :]
                    terms[pl.ds(at, hi - lo), k * B : (k + 1) * B] = kept.astype(BF16)
                after.append((e1, e2, f2))
            return tuple(after)

        low, high = rows
        carried = tuple(
            (sums(low - 1, *band)[0],) + sums(low, *band)[:2] for band in bands
        )
        if unroll:
            lax.fori_loop(
                low, high, lambda r, c: advance(r, c, True), carried, unroll=unroll
            )
        else:
            for r in range(low, high):
                carried = advance(r, carried, H <= r < H + R)

    def inner_rows(k, less):
        low, high = H + k + less, H + R - k - less
        return (low, high), {30: 6, 28: 7, 26: 13, 24: 8, 22: 11, 20: 10}[high - low]

    def step_inside(src, dst, k, scaled, less):
        first, last = O + 8 * k, O + B - 8 * k
        size = (last - first) // (1 if k == K else 2)
        for at in range(first, last, size):
            cells(src, dst, k, scaled, ((at, size),), *inner_rows(k, less))

    def step_rim(src, dst, k, scaled, less):
        reach = K - k
        first, last = (O - 8, O + B + 8) if reach else (O, O + B)
        size = 48 if reach else 64
        for low in (H - reach, H + R - k - less):
            for at in range(first, last, size):
                cells(src, dst, k, scaled, ((at, size),), (low, low + K + less), 0)
        width = O + 8 * k - first
        bands = ((first, width), (last - width, width))
        cells(src, dst, k, scaled, bands, *inner_rows(k, less))

    def start_row(r, first, last):
        at = slice(first - O + 8, last - O + 8)
        value = (-0.5 * coef[r, at, :] * scale[r, at, :]) * yb[r, first:last, :]
        ya[r, first:last, :] = value
        return value * scale[r, at, :]

    def start_inner(r, _):
        keep(0, r - H, start_row(r, O, O + B))
        return 0

    groups(yb)
    lax.fori_loop(6, RE - 6, start_inner, 0, unroll=7)
    step_inside(ya, yb, 1, True, 2)
    step_inside(yb, ya, 2, True, 2)
    step_inside(ya, yb, 3, True, 2)
    step_inside(yb, ya, 4, True, 2)

    for copy in mask_copies:
        copy.wait()
    north_ok = (lat > 0).astype(F32)
    south_ok = (lat < n_lat - 1).astype(F32)
    low_lanes = lane_e[0:8] < 64
    sm[0, 8:16, :] = mrx[2] * north_ok
    sm[0, 16 + B : 24 + B, :] = mrx[3] * south_ok
    sm[1, 8:16, :] = jnp.where(low_lanes, mrx[5], mrx[4]) * north_ok
    sm[1, 16 : 16 + B, :] = jnp.concatenate(
        [mrx[1], jnp.zeros((B - 16, B), F32), mrx[0]], axis=0
    ).T
    sm[1, 16 + B : 24 + B, :] = jnp.where(low_lanes, mrx[7], mrx[6]) * south_ok
    degrees()
    for p in (0, 1, 2, 17, 18, 19):
        spread(p, 0)
    lax.fori_loop(3, RE // 2 - 3, spread_sides, 0, unroll=7)

    for copy in first_halo:
        copy.wait()
    assemble(0, yb, 1.0, 1.0)
    for r in tuple(range(6)) + tuple(range(RE - 6, RE)):
        value = start_row(r, O - 8, O + B + 8)
        if H <= r < H + R:
            keep(0, r - H, value[8 : 8 + B])

    def start_sides(r, _):
        left = start_row(r, O - 8, O + 8)
        right = start_row(r, O + B - 8, O + B + 8)
        at = pl.multiple_of((r - H) * B, B)
        terms[pl.ds(at, 8), 0:B] = left[8:16].astype(BF16)
        terms[pl.ds(at + B - 8, 8), 0:B] = right[0:8].astype(BF16)
        return 0

    lax.fori_loop(6, RE - 6, start_sides, 0, unroll=7)
    step_rim(ya, yb, 1, True, 2)
    step_rim(yb, ya, 2, True, 2)
    step_rim(ya, yb, 3, True, 2)
    step_rim(yb, ya, 4, True, 2)


    def mix(p):
        at = pl.ds(pl.multiple_of(2 * p * B, 2 * B), 2 * B)
        mixed = lax.dot_general(wf[...], terms[at, :], NT, preferred_element_type=F32)
        act = jnp.tanh(mixed)
        cot = jnp.concatenate([rows_of(cf, 2 * p), rows_of(cf, 2 * p + 1)], axis=1)
        gcat[:, at] = (cot * (1.0 - act * act)).astype(BF16)

    def turn_grad(r):
        grad = gcat[:, pl.ds(pl.multiple_of(r * B, B), B)].astype(F32)
        w = -0.5 * coef[H + r, 8 : 8 + B, :] * scale[H + r, 8 : 8 + B, :]
        ya[H + r, O : O + B, :] = w * grad.T

    def grad_rows(first, count):
        for p in range(first // 2, (first + count) // 2):
            mix(p)
        for r in range(first, first + count):
            turn_grad(r)

    second_halo = halo_copies(1)
    send_chunks(1, ya, second_halo, grad_rows)

    chunk = 8 * B
    acc = None
    for n in range(R * B // chunk):
        part = jnp.dot(
            gcat[:, n * chunk : (n + 1) * chunk],
            terms[n * chunk : (n + 1) * chunk, :],
            preferred_element_type=F32,
        )
        acc = part if acc is None else acc + part
    lane_c = lax.broadcasted_iota(jnp.int32, (C, B), 1) // C
    folded = []
    for k in range(K + 1):
        tot = None
        for g in range(RG):
            piece = acc[g * C : (g + 1) * C, k * B : (k + 1) * B]
            tot = piece if tot is None else jnp.where(lane_c == g, piece, tot)
        tot = tot + pltpu.roll(tot, 64, 1)
        tot = tot + pltpu.roll(tot, 32, 1)
        folded.append(tot)
    head = folded[0]
    for k in range(1, K):
        head = jnp.where(lane_c == k, folded[k], head)
    tail = folded[K][0:8]
    for g in range(1, RG):
        tail = jnp.where(lane_c[0:8] == g, folded[K][8 * g : 8 * g + 8], tail)
    grid_cells = n_lat * n_lon * B * B
    own[0, 0:C, :] = head * (1.0 / math.sqrt(grid_cells))
    own[0, C : C + 8, :] = tail * (1.0 / math.sqrt(grid_cells))

    def lon_copy(off):
        return remote(
            own.at[0], ar1.at[lon], ar1_send.at[off], ar1_recv.at[lon],
            lat, lax.rem(lon + off, n_lon),
        )

    def lon_wait(off):
        q = lax.rem(lon + n_lon - off, n_lon)
        return remote(own.at[0], ar1.at[q], ar1_send.at[off], ar1_recv.at[q], lat, q)

    def lat_copy(off):
        return remote(
            own.at[1], ar2.at[lat], ar2_send.at[off], ar2_recv.at[lat],
            lax.rem(lat + off, n_lat), lon,
        )

    def lat_wait(off):
        q = lax.rem(lat + n_lat - off, n_lat)
        return remote(own.at[1], ar2.at[q], ar2_send.at[off], ar2_recv.at[q], q, lon)

    def run(count, act):
        def body(off, _):
            act(off)
            return 0

        lax.fori_loop(1, count, body, 0)

    run(n_lon, lambda off: lon_copy(off).start())
    ar1[lon] = own[0]

    def keep_grad(r, _):
        keep(0, r, ya[H + r, O : O + B, :])
        return 0

    lax.fori_loop(0, R, keep_grad, 0, unroll=4)
    groups(ya)
    step_inside(ya, yb, 1, False, 0)
    step_inside(yb, ya, 2, False, 0)
    step_inside(ya, yb, 3, False, 0)
    step_inside(yb, ya, 4, False, 0)
    for copy in second_halo:
        copy.wait()
    assemble(1, ya, north_ok, south_ok)

    step_rim(ya, yb, 1, False, 0)

    run(n_lon, lambda off: lon_wait(off).wait())
    total = ar1[0]
    for q in range(1, n_lon):
        total = total + ar1[q]
    own[1] = total
    run(n_lat, lambda off: lat_copy(off).start())
    ar2[lat] = total

    step_rim(yb, ya, 2, False, 0)
    step_rim(ya, yb, 3, False, 0)
    step_rim(yb, ya, 4, False, 0)

    def finish(p, _):
        t = terms[pl.ds(pl.multiple_of(2 * p * B, 2 * B), 2 * B), :]
        res = lax.dot_general(wb[...], t, NT, preferred_element_type=F32)
        for j in range(2):
            for g in range(RG):
                row = R * g + 2 * p + j
                s = jnp.broadcast_to(snat[pl.ds(row, 1), :], (C, B))
                part = res[g * C : (g + 1) * C, j * B : (j + 1) * B]
                xf[pl.ds(row, C, stride=B), :] = part * s
        return 0

    lax.fori_loop(0, R // 2, finish, 0, unroll=4)

    for c in range(C):
        out_v[c] = xf[c * B : (c + 1) * B, :].astype(BF16)

    run(n_lat, lambda off: lat_wait(off).wait())
    total = ar2[0]
    for q in range(1, n_lat):
        total = total + ar2[q]
    sum_ref[...] = total


def close(out_v, sum_ref, out_hbm, wg_ref, out_sem):
    part = C // 4
    copies = [
        pltpu.make_async_copy(
            out_v.at[pl.ds(n * part, part)], out_hbm.at[pl.ds(n * part, part)], out_sem.at[n]
        )
        for n in range(4)
    ]
    for copy in copies:
        copy.start()
    total = sum_ref[...]
    flat = total[0:C].T
    for k in range(K):
        wg_ref[k] = flat[k * C : (k + 1) * C, :]
    last = total[C : C + 8]
    last = jnp.concatenate(
        [last if g == 0 else pltpu.roll(last, B - C * g, 1) for g in range(RG)], axis=0
    )
    wg_ref[K] = last.T[0:C, :]
    for copy in copies:
        copy.wait()


def solution(mesh):
    n_lat, n_lon = mesh.shape["lat"], mesh.shape["lon"]
    hbm = pl.BlockSpec(memory_space=pltpu.HBM)
    sem = pltpu.SemaphoreType.DMA

    def local(features, cotangent, sea_mask, weights):
        vmem = pl.BlockSpec(memory_space=pltpu.VMEM)
        carried = (
            pltpu.VMEM((C, B, B), BF16),
            pltpu.VMEM((C + 8, B), F32),
        )
        carried = pl.pallas_call(
            functools.partial(kernel, n_lat, n_lon),
            out_shape=carried,
            in_specs=[hbm] * 4,
            out_specs=(vmem,) * 2,
            scratch_shapes=[
                pltpu.VMEM((C, B, B), BF16),
                pltpu.VMEM((C, B, B), BF16),
                pltpu.VMEM((B, B), jnp.int32),
                pltpu.VMEM((K + 1, C, C), BF16),
                pltpu.VMEM((C * B, B), F32),
                pltpu.VMEM((C * B, B), F32),
                pltpu.VMEM((RE, CP, B), F32),
                pltpu.VMEM((RE, CP, B), F32),
                pltpu.VMEM((RE, CE, B), F32),
                pltpu.VMEM((RE, CE, B), F32),
                pltpu.VMEM((R * B, (K + 1) * B), BF16),
                pltpu.VMEM((B, R * B), BF16),
                pltpu.VMEM((4, 8, B), F32),
                pltpu.VMEM((8, 8, B), F32),
                pltpu.VMEM((2, CP, B), F32),
                pltpu.VMEM((CE, 2 * B), F32),
                pltpu.VMEM((B, B), F32),
                pltpu.VMEM((B, (K + 1) * B), BF16),
                pltpu.VMEM((B, (K + 1) * B), BF16),
                pltpu.VMEM((CE, 2 * B), BF16),
                pltpu.VMEM((2, 2, B, B), F32),
                pltpu.VMEM((2, 2, R // 2, 8, B), F32),
                pltpu.VMEM((2, 2, CE, B), F32),
                pltpu.VMEM((2, 2, R // 2, 8, B), F32),
                pltpu.VMEM((2, C + 8, B), F32),
                pltpu.VMEM((n_lon, C + 8, B), F32),
                pltpu.VMEM((n_lat, C + 8, B), F32),
                sem((8,)), sem((8,)), sem((8,)), sem((2, 16)), sem((2, 16)),
                sem((n_lon,)), sem((n_lon,)), sem((n_lat,)), sem((n_lat,)),
            ],
            compiler_params=pltpu.CompilerParams(
                collective_id=0, has_side_effects=True, vmem_limit_bytes=62 << 20
            ),
        )(features, cotangent, sea_mask, weights)
        return pl.pallas_call(
            close,
            out_shape=(
                jax.ShapeDtypeStruct((C, B, B), BF16),
                jax.ShapeDtypeStruct((K + 1, C, C), F32),
            ),
            in_specs=[vmem] * 2,
            out_specs=(hbm, vmem),
            scratch_shapes=[sem((4,))],
            compiler_params=pltpu.CompilerParams(vmem_limit_bytes=4 << 20),
        )(*carried)

    placed = (P(None, "lat", "lon"), P(None, "lat", "lon"), P("lat", "lon"), P())
    return jax.shard_map(
        local, mesh=mesh, in_specs=placed, out_specs=(P(None, "lat", "lon"), P()), check_vma=False
    )
```

```python
import functools
import math

import jax
import jax.numpy as jnp
from jax import lax
from jax.experimental import pallas as pl
from jax.experimental.pallas import tpu as pltpu
from jax.sharding import PartitionSpec as P

K = 4
C = 32
B = 128
RG = 4
R = B // RG
H = 4
RE = R + 2 * H
CE = B + 16
CP = CE + 16
O = 16
F32 = jnp.float32
BF16 = jnp.bfloat16
NT = (((1,), (1,)), ((), ()))


def kernel(
    n_lat, n_lon,
    feat_hbm, cot_hbm, mask_hbm, w_hbm,
    out_v, sum_ref,
    feat_v, cot_v, mask_v, w_v, xf, cf,
    ya, yb, coef, scale, terms, gcat,
    mtx, mrx, sm, vm, snat, wf, wb, sel,
    pack, cpack, lrow, lcol, own, ar1, ar2,
    in_sem, mask_send, mask_recv, halo_send, halo_recv,
    ar1_send, ar1_recv, ar2_send, ar2_recv,
):
    lat = lax.axis_index("lat")
    lon = lax.axis_index("lon")
    north, south = lax.rem(lat + n_lat - 1, n_lat), lax.rem(lat + 1, n_lat)
    west, east = lax.rem(lon + n_lon - 1, n_lon), lax.rem(lon + 1, n_lon)

    feat_in = pltpu.make_async_copy(feat_hbm, feat_v, in_sem.at[0])
    cot_in = pltpu.make_async_copy(cot_hbm, cot_v, in_sem.at[1])
    mask_in = pltpu.make_async_copy(mask_hbm, mask_v, in_sem.at[2])
    w_in = pltpu.make_async_copy(w_hbm, w_v, in_sem.at[3])
    mask_in.start()
    feat_in.start()
    w_in.start()
    cot_in.start()

    barrier = pltpu.get_barrier_semaphore()

    def greet(i, j):
        pl.semaphore_signal(
            barrier, inc=1, device_id=(i, j), device_id_type=pl.DeviceIdType.MESH
        )

    for i in (north, south):
        for j in (west, east):
            greet(i, j)

    def greet_lon(off, _):
        greet(lat, lax.rem(lon + off, n_lon))
        return 0

    def greet_lat(off, _):
        greet(lax.rem(lat + off, n_lat), lon)
        return 0

    lax.fori_loop(1, n_lon, greet_lon, 0)
    lax.fori_loop(1, n_lat, greet_lat, 0)

    row_i = lax.broadcasted_iota(jnp.int32, (B, B), 0)
    col_i = lax.broadcasted_iota(jnp.int32, (B, B), 1)
    sel_r = lax.broadcasted_iota(jnp.int32, (CE, 2 * B), 0)
    sel_c = lax.broadcasted_iota(jnp.int32, (CE, 2 * B), 1)
    inside = (sel_r >= 8) & (sel_r < 8 + B) & (sel_c == sel_r - 8)
    left = (sel_r < 8) & (sel_c == 2 * B - 8 + sel_r)
    right = (sel_r >= 8 + B) & (sel_c == sel_r - 8)
    sel[...] = (inside | left | right).astype(F32).astype(BF16)

    mask_in.wait()
    flags = mask_v[...].astype(F32)
    turned_flags = flags.T
    mtx[0] = flags[B - 8 :]
    mtx[1] = flags[:8]
    mtx[2] = turned_flags[B - 8 :]
    mtx[3] = turned_flags[:8]

    def remote(src, dst, send, recv, i, j):
        return pltpu.make_async_remote_copy(
            src_ref=src, dst_ref=dst, send_sem=send, recv_sem=recv,
            device_id=(i, j), device_id_type=pl.DeviceIdType.MESH,
        )

    mid = pl.ds(8, B)
    above, below = pl.ds(0, 8), pl.ds(8 + B, 8)
    mask_plan = (
        (2, 0, lat, east),
        (3, 1, lat, west),
        (0, 2, south, lon),
        (1, 3, north, lon),
        (0, 4, south, east),
        (0, 5, south, west),
        (1, 6, north, east),
        (1, 7, north, west),
    )
    mask_copies = [
        remote(mtx.at[src], mrx.at[n], mask_send.at[n], mask_recv.at[n], i, j)
        for src, n, i, j in mask_plan
    ]

    lane = lax.broadcasted_iota(jnp.int32, (B, B), 1)

    def halo_copies(phase):
        plan = (
            (pack.at[phase, 0], lrow.at[phase, 0, mid], south, lon),
            (pack.at[phase, 1], lrow.at[phase, 1, mid], north, lon),
            (pack.at[phase, 0, pl.ds(B - 8, 8)], lrow.at[phase, 0, above], south, east),
            (pack.at[phase, 0, pl.ds(0, 8)], lrow.at[phase, 0, below], south, west),
            (pack.at[phase, 1, pl.ds(B - 8, 8)], lrow.at[phase, 1, above], north, east),
            (pack.at[phase, 1, pl.ds(0, 8)], lrow.at[phase, 1, below], north, west),
        ) + tuple(
            (cpack.at[phase, side, at], lcol.at[phase, side, at], lat, (east, west)[side])
            for at in (pl.ds(0, 2), pl.ds(14, 2), pl.ds(2, 4), pl.ds(6, 4), pl.ds(10, 4))
            for side in range(2)
        )
        return [
            remote(src, dst, halo_send.at[phase, n], halo_recv.at[phase, n], i, j)
            for n, (src, dst, i, j) in enumerate(plan)
        ]

    def pack_rows(phase, y):
        last, first = None, None
        for i in range(H):
            a = pltpu.roll(y[H + R - H + i, O : O + B, :], (32 * i + 32) % 128, 1)
            b = pltpu.roll(y[H + i, O : O + B, :], (32 * i) % 128, 1)
            here = (lane >= 32 * i) & (lane < 32 * i + 32)
            last = a if last is None else jnp.where(here, a, last)
            first = b if first is None else jnp.where(here, b, first)
        pack[phase, 0] = last
        pack[phase, 1] = first

    half = lax.broadcasted_iota(jnp.int32, (8, B), 0) < 4

    def pack_columns(phase, y, p):
        a, b = y[H + 2 * p, O + B - 8 : O + B, :], y[H + 2 * p + 1, O + B - 8 : O + B, :]
        cpack[phase, 0, p] = jnp.where(half, pltpu.roll(a, 4, 0), b)
        a, b = y[H + 2 * p, O : O + 8, :], y[H + 2 * p + 1, O : O + 8, :]
        cpack[phase, 1, p] = jnp.where(half, a, pltpu.roll(b, 4, 0))

    def send_chunks(phase, y, copies, turn_rows):
        turn_rows(0, H)
        turn_rows(R - H, H)
        for p in (0, 1, 14, 15):
            pack_columns(phase, y, p)
        pack_rows(phase, y)
        for copy in copies[:10]:
            copy.start()
        for n in range(3):
            turn_rows(H + 8 * n, 8)
            for p in range(2 + 4 * n, 6 + 4 * n):
                pack_columns(phase, y, p)
            for copy in copies[10 + 2 * n : 12 + 2 * n]:
                copy.start()

    feat_in.wait()

    def widen(src, dst):
        def body(c, _):
            dst[pl.ds(pl.multiple_of(c * B, B), B), :] = src[c].astype(F32)
            return 0

        lax.fori_loop(0, C, body, 0, unroll=4)

    def rows_of(flat, r):
        return jnp.concatenate(
            [flat[pl.ds(R * g + r, C, stride=B), :] for g in range(RG)], axis=0
        )

    widen(feat_v, xf)

    def turn(r):
        yb[H + r, O : O + B, :] = rows_of(xf, r).T

    def turn_rows(first, count):
        for r in range(first, first + count):
            turn(r)

    turn_rows(0, R)
    for p in range(R // 2):
        pack_columns(0, yb, p)
    pack_rows(0, yb)
    pl.semaphore_wait(barrier, 4 + (n_lon - 1) + (n_lat - 1))
    for copy in mask_copies:
        copy.start()
    first_halo = halo_copies(0)
    for copy in first_halo:
        copy.start()

    w_in.wait()
    block = (row_i // C) == (col_i // C)
    for k in range(K + 1):
        one = w_v[k].astype(F32)
        wide = jnp.concatenate([one] * RG, axis=1)
        full = jnp.where(block, jnp.concatenate([wide] * RG, axis=0), 0.0)
        wb[:, k * B : (k + 1) * B] = full.astype(BF16)
        wf[:, k * B : (k + 1) * B] = full.T.astype(BF16)

    cot_in.wait()
    widen(cot_v, cf)

    lane_e = lax.broadcasted_iota(jnp.int32, (CE, B), 1)
    sm[...] = jnp.zeros_like(sm)
    sm[0, 16 : 16 + B, :] = mask_v[...].astype(F32)

    def ring(main, side, shift, edge):
        m, s = pltpu.roll(main, shift, 1), pltpu.roll(side, shift, 1)
        at = lane_e == edge
        return jnp.where(at, s, m), jnp.where(at, m, s)

    def degrees():
        here = [sm[t, 8 : 8 + CE, :] for t in range(2)]
        up = [sm[t, 7 : 7 + CE, :] for t in range(2)]
        down = [sm[t, 9 : 9 + CE, :] for t in range(2)]
        from_left = ring(here[0] + down[0], here[1] + down[1], 1, 0)
        from_right = ring(here[0] + up[0], here[1] + up[1], B - 1, B - 1)
        for t in range(2):
            degree = from_left[t] + from_right[t] + up[t] + down[t]
            vm[:, t * B : (t + 1) * B] = here[t] * jnp.maximum(degree, 1.0)
            if t == 0:
                snat[...] = jnp.sqrt(jnp.maximum(degree, 1.0)[8 : 8 + B])

    def values(p, pick):
        rows = jnp.concatenate(
            [
                jnp.broadcast_to(vm[pl.ds(8 - H + R * g + 2 * p + j, 1), :], (C, 2 * B))
                for j in range(2)
                for g in range(RG)
            ],
            axis=0,
        )
        v = lax.dot_general(pick, rows.astype(BF16), NT, preferred_element_type=F32)
        m = jnp.maximum(v, 1.0)
        rs = lax.rsqrt(m)
        return jnp.where(v > 0.5, -2.0 * rs * rs, 0.0), m * rs

    def spread(p, _):
        a, s = values(p, sel[...])
        for j in range(2):
            coef[2 * p + j] = a[:, j * B : (j + 1) * B]
            scale[2 * p + j] = s[:, j * B : (j + 1) * B]
        return 0

    def spread_sides(p, _):
        a, s = values(p, jnp.concatenate([sel[0:16, :], sel[CE - 16 :, :]], axis=0))
        for j in range(2):
            for ref, part in ((coef, a), (scale, s)):
                ref[2 * p + j, 0:16, :] = part[0:16, j * B : (j + 1) * B]
                ref[2 * p + j, CE - 16 :, :] = part[16:32, j * B : (j + 1) * B]
        return 0

    degrees()
    lax.fori_loop(3, RE // 2 - 3, spread, 0, unroll=7)

    def groups(y):
        for i in range(H):
            y[i, O : O + B, :] = pltpu.roll(y[R + i, O : O + B, :], C, 1)
            y[H + R + i, O : O + B, :] = pltpu.roll(y[H + i, O : O + B, :], B - C, 1)

    def beside(y, at, row, shift):
        return jnp.concatenate(
            [
                pltpu.roll(y[row, O - 8 : O, :], shift, 1),
                y[at, O : O + B, :],
                pltpu.roll(y[row, O + B : O + B + 8, :], shift, 1),
            ],
            axis=0,
        )

    def assemble(phase, y, ok_north, ok_south):
        for p in range(R // 2):
            a, b = lcol[phase, 0, p], lcol[phase, 1, p]
            y[H + 2 * p, O - 8 : O, :] = pltpu.roll(a, 4, 0)
            y[H + 2 * p + 1, O - 8 : O, :] = a
            y[H + 2 * p, O + B : O + B + 8, :] = b
            y[H + 2 * p + 1, O + B : O + B + 8, :] = pltpu.roll(b, 4, 0)
        for i in range(H):
            own_up = beside(y, i, R + i, C)
            far_up = pltpu.roll(lrow[phase, 0], (B - 32 * i) % B, 1) * ok_north
            y[i, O - 8 : O + B + 8, :] = jnp.where(lane_e < 32, far_up, own_up)
            own_down = beside(y, H + R + i, H + i, B - C)
            far_down = pltpu.roll(lrow[phase, 1], (96 - 32 * i) % B, 1) * ok_south
            y[H + R + i, O - 8 : O + B + 8, :] = jnp.where(
                lane_e >= 96, far_down, own_down
            )

    def keep(k, r, value):
        terms[pl.ds(pl.multiple_of(r * B, B), B), k * B : (k + 1) * B] = value.astype(BF16)

    def cells(src, dst, k, scaled, bands, rows, unroll):
        def sums(r, first, size):
            mid_ = src[r, first : first + size, :]
            low = src[r, first - 1 : first - 1 + size, :]
            high = src[r, first + 1 : first + 1 + size, :]
            return mid_ + high, low + high, mid_ + low

        def advance(r, carried, keeps):
            after = []
            for (first, size), (e0, e1, f1) in zip(bands, carried):
                e2, f2, h2 = sums(r + 1, first, size)
                total = coef[r, first - O + 8 : first - O + 8 + size, :] * (e0 + f1 + h2)
                if k == 1:
                    value = 0.5 * total
                else:
                    value = total - dst[r, first : first + size, :]
                dst[r, first : first + size, :] = value
                lo, hi = max(first, O), min(first + size, O + B)
                if keeps:
                    at = (r - H) * B + lo - O
                    if not isinstance(r, int):
                        at = pl.multiple_of(at, 8)
                    kept = value[lo - first : hi - first]
                    if scaled:
                        kept = kept * scale[r, lo - O + 8 : hi - O + 8, :]
                    terms[pl.ds(at, hi - lo), k * B : (k + 1) * B] = kept.astype(BF16)
                after.append((e1, e2, f2))
            return tuple(after)

        low, high = rows
        carried = tuple(
            (sums(low - 1, *band)[0],) + sums(low, *band)[:2] for band in bands
        )
        if unroll:
            lax.fori_loop(
                low, high, lambda r, c: advance(r, c, True), carried, unroll=unroll
            )
        else:
            for r in range(low, high):
                carried = advance(r, carried, H <= r < H + R)

    def inner_rows(k, less):
        low, high = H + k + less, H + R - k - less
        return (low, high), {30: 6, 28: 7, 26: 13, 24: 8, 22: 11, 20: 10}[high - low]

    def step_inside(src, dst, k, scaled, less):
        first, last = O + 8 * k, O + B - 8 * k
        size = (last - first) // (1 if k == K else 2)
        for at in range(first, last, size):
            cells(src, dst, k, scaled, ((at, size),), *inner_rows(k, less))

    def step_rim(src, dst, k, scaled, less):
        reach = K - k
        first, last = (O - 8, O + B + 8) if reach else (O, O + B)
        size = 48 if reach else 64
        for low in (H - reach, H + R - k - less):
            for at in range(first, last, size):
                cells(src, dst, k, scaled, ((at, size),), (low, low + K + less), 0)
        width = O + 8 * k - first
        bands = ((first, width), (last - width, width))
        cells(src, dst, k, scaled, bands, *inner_rows(k, less))

    def start_row(r, first, last):
        at = slice(first - O + 8, last - O + 8)
        value = (-0.5 * coef[r, at, :] * scale[r, at, :]) * yb[r, first:last, :]
        ya[r, first:last, :] = value
        return value * scale[r, at, :]

    def start_inner(r, _):
        keep(0, r - H, start_row(r, O, O + B))
        return 0

    groups(yb)
    lax.fori_loop(6, RE - 6, start_inner, 0, unroll=7)
    step_inside(ya, yb, 1, True, 2)
    step_inside(yb, ya, 2, True, 2)
    step_inside(ya, yb, 3, True, 2)
    step_inside(yb, ya, 4, True, 2)

    for copy in mask_copies:
        copy.wait()
    north_ok = (lat > 0).astype(F32)
    south_ok = (lat < n_lat - 1).astype(F32)
    low_lanes = lane_e[0:8] < 64
    sm[0, 8:16, :] = mrx[2] * north_ok
    sm[0, 16 + B : 24 + B, :] = mrx[3] * south_ok
    sm[1, 8:16, :] = jnp.where(low_lanes, mrx[5], mrx[4]) * north_ok
    sm[1, 16 : 16 + B, :] = jnp.concatenate(
        [mrx[1], jnp.zeros((B - 16, B), F32), mrx[0]], axis=0
    ).T
    sm[1, 16 + B : 24 + B, :] = jnp.where(low_lanes, mrx[7], mrx[6]) * south_ok
    degrees()
    for p in (0, 1, 2, 17, 18, 19):
        spread(p, 0)
    lax.fori_loop(3, RE // 2 - 3, spread_sides, 0, unroll=7)

    for copy in first_halo:
        copy.wait()
    assemble(0, yb, 1.0, 1.0)
    for r in tuple(range(6)) + tuple(range(RE - 6, RE)):
        value = start_row(r, O - 8, O + B + 8)
        if H <= r < H + R:
            keep(0, r - H, value[8 : 8 + B])

    def start_sides(r, _):
        left = start_row(r, O - 8, O + 8)
        right = start_row(r, O + B - 8, O + B + 8)
        at = pl.multiple_of((r - H) * B, B)
        terms[pl.ds(at, 8), 0:B] = left[8:16].astype(BF16)
        terms[pl.ds(at + B - 8, 8), 0:B] = right[0:8].astype(BF16)
        return 0

    lax.fori_loop(6, RE - 6, start_sides, 0, unroll=7)
    step_rim(ya, yb, 1, True, 2)
    step_rim(yb, ya, 2, True, 2)
    step_rim(ya, yb, 3, True, 2)
    step_rim(yb, ya, 4, True, 2)


    def mix(p):
        at = pl.ds(pl.multiple_of(2 * p * B, 2 * B), 2 * B)
        mixed = lax.dot_general(wf[...], terms[at, :], NT, preferred_element_type=F32)
        act = jnp.tanh(mixed)
        cot = jnp.concatenate([rows_of(cf, 2 * p), rows_of(cf, 2 * p + 1)], axis=1)
        gcat[:, at] = (cot * (1.0 - act * act)).astype(BF16)

    def turn_grad(r):
        grad = gcat[:, pl.ds(pl.multiple_of(r * B, B), B)].astype(F32)
        w = -0.5 * coef[H + r, 8 : 8 + B, :] * scale[H + r, 8 : 8 + B, :]
        ya[H + r, O : O + B, :] = w * grad.T

    def grad_rows(first, count):
        for p in range(first // 2, (first + count) // 2):
            mix(p)
        for r in range(first, first + count):
            turn_grad(r)

    second_halo = halo_copies(1)
    send_chunks(1, ya, second_halo, grad_rows)

    chunk = 8 * B
    acc = None
    for n in range(R * B // chunk):
        part = jnp.dot(
            gcat[:, n * chunk : (n + 1) * chunk],
            terms[n * chunk : (n + 1) * chunk, :],
            preferred_element_type=F32,
        )
        acc = part if acc is None else acc + part
    lane_c = lax.broadcasted_iota(jnp.int32, (C, B), 1) // C
    folded = []
    for k in range(K + 1):
        tot = None
        for g in range(RG):
            piece = acc[g * C : (g + 1) * C, k * B : (k + 1) * B]
            tot = piece if tot is None else jnp.where(lane_c == g, piece, tot)
        tot = tot + pltpu.roll(tot, 64, 1)
        tot = tot + pltpu.roll(tot, 32, 1)
        folded.append(tot)
    head = folded[0]
    for k in range(1, K):
        head = jnp.where(lane_c == k, folded[k], head)
    tail = folded[K][0:8]
    for g in range(1, RG):
        tail = jnp.where(lane_c[0:8] == g, folded[K][8 * g : 8 * g + 8], tail)
    grid_cells = n_lat * n_lon * B * B
    own[0, 0:C, :] = head * (1.0 / math.sqrt(grid_cells))
    own[0, C : C + 8, :] = tail * (1.0 / math.sqrt(grid_cells))

    def lon_copy(off):
        return remote(
            own.at[0], ar1.at[lon], ar1_send.at[off], ar1_recv.at[lon],
            lat, lax.rem(lon + off, n_lon),
        )

    def lon_wait(off):
        q = lax.rem(lon + n_lon - off, n_lon)
        return remote(own.at[0], ar1.at[q], ar1_send.at[off], ar1_recv.at[q], lat, q)

    def lat_copy(off):
        return remote(
            own.at[1], ar2.at[lat], ar2_send.at[off], ar2_recv.at[lat],
            lax.rem(lat + off, n_lat), lon,
        )

    def lat_wait(off):
        q = lax.rem(lat + n_lat - off, n_lat)
        return remote(own.at[1], ar2.at[q], ar2_send.at[off], ar2_recv.at[q], q, lon)

    def run(count, act):
        def body(off, _):
            act(off)
            return 0

        lax.fori_loop(1, count, body, 0)

    run(n_lon, lambda off: lon_copy(off).start())
    ar1[lon] = own[0]

    def keep_grad(r, _):
        keep(0, r, ya[H + r, O : O + B, :])
        return 0

    lax.fori_loop(0, R, keep_grad, 0, unroll=4)
    groups(ya)
    step_inside(ya, yb, 1, False, 0)
    step_inside(yb, ya, 2, False, 0)
    step_inside(ya, yb, 3, False, 0)
    step_inside(yb, ya, 4, False, 0)
    for copy in second_halo:
        copy.wait()
    assemble(1, ya, north_ok, south_ok)

    step_rim(ya, yb, 1, False, 0)

    run(n_lon, lambda off: lon_wait(off).wait())
    total = ar1[0]
    for q in range(1, n_lon):
        total = total + ar1[q]
    own[1] = total
    run(n_lat, lambda off: lat_copy(off).start())
    ar2[lat] = total

    step_rim(yb, ya, 2, False, 0)
    step_rim(ya, yb, 3, False, 0)
    step_rim(yb, ya, 4, False, 0)

    def finish(p, _):
        t = terms[pl.ds(pl.multiple_of(2 * p * B, 2 * B), 2 * B), :]
        res = lax.dot_general(wb[...], t, NT, preferred_element_type=F32)
        for j in range(2):
            for g in range(RG):
                row = R * g + 2 * p + j
                s = jnp.broadcast_to(snat[pl.ds(row, 1), :], (C, B))
                part = res[g * C : (g + 1) * C, j * B : (j + 1) * B]
                xf[pl.ds(row, C, stride=B), :] = part * s
        return 0

    lax.fori_loop(0, R // 2, finish, 0, unroll=4)

    for c in range(C):
        out_v[c] = xf[c * B : (c + 1) * B, :].astype(BF16)

    run(n_lat, lambda off: lat_wait(off).wait())
    total = ar2[0]
    for q in range(1, n_lat):
        total = total + ar2[q]
    sum_ref[...] = total


def close(out_v, sum_ref, out_hbm, wg_ref, out_sem):
    copy = pltpu.make_async_copy(out_v, out_hbm, out_sem)
    copy.start()
    total = sum_ref[...]
    flat = total[0:C].T
    for k in range(K):
        wg_ref[k] = flat[k * C : (k + 1) * C, :]
    last = total[C : C + 8]
    last = jnp.concatenate(
        [last if g == 0 else pltpu.roll(last, B - C * g, 1) for g in range(RG)], axis=0
    )
    wg_ref[K] = last.T[0:C, :]
    copy.wait()


def solution(mesh):
    n_lat, n_lon = mesh.shape["lat"], mesh.shape["lon"]
    hbm = pl.BlockSpec(memory_space=pltpu.HBM)
    sem = pltpu.SemaphoreType.DMA

    def local(features, cotangent, sea_mask, weights):
        vmem = pl.BlockSpec(memory_space=pltpu.VMEM)
        carried = (
            pltpu.VMEM((C, B, B), BF16),
            pltpu.VMEM((C + 8, B), F32),
        )
        carried = pl.pallas_call(
            functools.partial(kernel, n_lat, n_lon),
            out_shape=carried,
            in_specs=[hbm] * 4,
            out_specs=(vmem,) * 2,
            scratch_shapes=[
                pltpu.VMEM((C, B, B), BF16),
                pltpu.VMEM((C, B, B), BF16),
                pltpu.VMEM((B, B), jnp.int32),
                pltpu.VMEM((K + 1, C, C), BF16),
                pltpu.VMEM((C * B, B), F32),
                pltpu.VMEM((C * B, B), F32),
                pltpu.VMEM((RE, CP, B), F32),
                pltpu.VMEM((RE, CP, B), F32),
                pltpu.VMEM((RE, CE, B), F32),
                pltpu.VMEM((RE, CE, B), F32),
                pltpu.VMEM((R * B, (K + 1) * B), BF16),
                pltpu.VMEM((B, R * B), BF16),
                pltpu.VMEM((4, 8, B), F32),
                pltpu.VMEM((8, 8, B), F32),
                pltpu.VMEM((2, CP, B), F32),
                pltpu.VMEM((CE, 2 * B), F32),
                pltpu.VMEM((B, B), F32),
                pltpu.VMEM((B, (K + 1) * B), BF16),
                pltpu.VMEM((B, (K + 1) * B), BF16),
                pltpu.VMEM((CE, 2 * B), BF16),
                pltpu.VMEM((2, 2, B, B), F32),
                pltpu.VMEM((2, 2, R // 2, 8, B), F32),
                pltpu.VMEM((2, 2, CE, B), F32),
                pltpu.VMEM((2, 2, R // 2, 8, B), F32),
                pltpu.VMEM((2, C + 8, B), F32),
                pltpu.VMEM((n_lon, C + 8, B), F32),
                pltpu.VMEM((n_lat, C + 8, B), F32),
                sem((4,)), sem((8,)), sem((8,)), sem((2, 16)), sem((2, 16)),
                sem((n_lon,)), sem((n_lon,)), sem((n_lat,)), sem((n_lat,)),
            ],
            compiler_params=pltpu.CompilerParams(
                collective_id=0, has_side_effects=True, vmem_limit_bytes=62 << 20
            ),
        )(features, cotangent, sea_mask, weights)
        return pl.pallas_call(
            close,
            out_shape=(
                jax.ShapeDtypeStruct((C, B, B), BF16),
                jax.ShapeDtypeStruct((K + 1, C, C), F32),
            ),
            in_specs=[vmem] * 2,
            out_specs=(hbm, vmem),
            scratch_shapes=[sem(())],
            compiler_params=pltpu.CompilerParams(vmem_limit_bytes=4 << 20),
        )(*carried)

    placed = (P(None, "lat", "lon"), P(None, "lat", "lon"), P("lat", "lon"), P())
    return jax.shard_map(
        local, mesh=mesh, in_specs=placed, out_specs=(P(None, "lat", "lon"), P()), check_vma=False
    )
```

```python
import functools
import math

import jax
import jax.numpy as jnp
from jax import lax
from jax.experimental import pallas as pl
from jax.experimental.pallas import tpu as pltpu
from jax.sharding import PartitionSpec as P

K = 4
C = 32
B = 128
RG = 4
R = B // RG
H = 4
RE = R + 2 * H
CE = B + 16
CP = CE + 16
O = 16
F32 = jnp.float32
BF16 = jnp.bfloat16
NT = (((1,), (1,)), ((), ()))


def kernel(
    n_lat, n_lon,
    feat_hbm, cot_hbm, mask_hbm, w_hbm,
    out_v, sum_ref,
    feat_v, cot_v, mask_v, w_v, xf, cf,
    ya, yb, coef, scale, terms, gcat,
    mtx, mrx, sm, vm, snat, wf, wb, sel,
    pack, cpack, lrow, lcol, own, ar1, ar2,
    in_sem, mask_send, mask_recv, halo_send, halo_recv,
    ar1_send, ar1_recv, ar2_send, ar2_recv,
):
    lat = lax.axis_index("lat")
    lon = lax.axis_index("lon")
    north, south = lax.rem(lat + n_lat - 1, n_lat), lax.rem(lat + 1, n_lat)
    west, east = lax.rem(lon + n_lon - 1, n_lon), lax.rem(lon + 1, n_lon)

    feat_in = pltpu.make_async_copy(feat_hbm, feat_v, in_sem.at[0])
    cot_in = pltpu.make_async_copy(cot_hbm, cot_v, in_sem.at[1])
    mask_in = pltpu.make_async_copy(mask_hbm, mask_v, in_sem.at[2])
    w_in = pltpu.make_async_copy(w_hbm, w_v, in_sem.at[3])
    mask_in.start()
    feat_in.start()
    w_in.start()
    cot_in.start()

    barrier = pltpu.get_barrier_semaphore()

    def greet(i, j):
        pl.semaphore_signal(
            barrier, inc=1, device_id=(i, j), device_id_type=pl.DeviceIdType.MESH
        )

    for i in (north, south):
        for j in (west, east):
            greet(i, j)

    def greet_lon(off, _):
        greet(lat, lax.rem(lon + off, n_lon))
        return 0

    def greet_lat(off, _):
        greet(lax.rem(lat + off, n_lat), lon)
        return 0

    lax.fori_loop(1, n_lon, greet_lon, 0)
    lax.fori_loop(1, n_lat, greet_lat, 0)

    row_i = lax.broadcasted_iota(jnp.int32, (B, B), 0)
    col_i = lax.broadcasted_iota(jnp.int32, (B, B), 1)
    sel_r = lax.broadcasted_iota(jnp.int32, (CE, 2 * B), 0)
    sel_c = lax.broadcasted_iota(jnp.int32, (CE, 2 * B), 1)
    inside = (sel_r >= 8) & (sel_r < 8 + B) & (sel_c == sel_r - 8)
    left = (sel_r < 8) & (sel_c == 2 * B - 8 + sel_r)
    right = (sel_r >= 8 + B) & (sel_c == sel_r - 8)
    sel[...] = (inside | left | right).astype(F32).astype(BF16)

    mask_in.wait()
    flags = mask_v[...].astype(F32)
    turned_flags = flags.T
    mtx[0] = flags[B - 8 :]
    mtx[1] = flags[:8]
    mtx[2] = turned_flags[B - 8 :]
    mtx[3] = turned_flags[:8]

    def remote(src, dst, send, recv, i, j):
        return pltpu.make_async_remote_copy(
            src_ref=src, dst_ref=dst, send_sem=send, recv_sem=recv,
            device_id=(i, j), device_id_type=pl.DeviceIdType.MESH,
        )

    mid = pl.ds(8, B)
    above, below = pl.ds(0, 8), pl.ds(8 + B, 8)
    mask_plan = (
        (2, 0, lat, east),
        (3, 1, lat, west),
        (0, 2, south, lon),
        (1, 3, north, lon),
        (0, 4, south, east),
        (0, 5, south, west),
        (1, 6, north, east),
        (1, 7, north, west),
    )
    mask_copies = [
        remote(mtx.at[src], mrx.at[n], mask_send.at[n], mask_recv.at[n], i, j)
        for src, n, i, j in mask_plan
    ]

    lane = lax.broadcasted_iota(jnp.int32, (B, B), 1)

    def halo_copies(phase):
        plan = (
            (pack.at[phase, 0], lrow.at[phase, 0, mid], south, lon),
            (pack.at[phase, 1], lrow.at[phase, 1, mid], north, lon),
            (pack.at[phase, 0, pl.ds(B - 8, 8)], lrow.at[phase, 0, above], south, east),
            (pack.at[phase, 0, pl.ds(0, 8)], lrow.at[phase, 0, below], south, west),
            (pack.at[phase, 1, pl.ds(B - 8, 8)], lrow.at[phase, 1, above], north, east),
            (pack.at[phase, 1, pl.ds(0, 8)], lrow.at[phase, 1, below], north, west),
        ) + tuple(
            (cpack.at[phase, side, at], lcol.at[phase, side, at], lat, (east, west)[side])
            for at in (pl.ds(0, 2), pl.ds(14, 2), pl.ds(2, 4), pl.ds(6, 4), pl.ds(10, 4))
            for side in range(2)
        )
        return [
            remote(src, dst, halo_send.at[phase, n], halo_recv.at[phase, n], i, j)
            for n, (src, dst, i, j) in enumerate(plan)
        ]

    def pack_rows(phase, y):
        last, first = None, None
        for i in range(H):
            a = pltpu.roll(y[H + R - H + i, O : O + B, :], (32 * i + 32) % 128, 1)
            b = pltpu.roll(y[H + i, O : O + B, :], (32 * i) % 128, 1)
            here = (lane >= 32 * i) & (lane < 32 * i + 32)
            last = a if last is None else jnp.where(here, a, last)
            first = b if first is None else jnp.where(here, b, first)
        pack[phase, 0] = last
        pack[phase, 1] = first

    half = lax.broadcasted_iota(jnp.int32, (8, B), 0) < 4

    def pack_columns(phase, y, p):
        a, b = y[H + 2 * p, O + B - 8 : O + B, :], y[H + 2 * p + 1, O + B - 8 : O + B, :]
        cpack[phase, 0, p] = jnp.where(half, pltpu.roll(a, 4, 0), b)
        a, b = y[H + 2 * p, O : O + 8, :], y[H + 2 * p + 1, O : O + 8, :]
        cpack[phase, 1, p] = jnp.where(half, a, pltpu.roll(b, 4, 0))

    def send_chunks(phase, y, copies, turn_rows):
        turn_rows(0, H)
        turn_rows(R - H, H)
        for p in (0, 1, 14, 15):
            pack_columns(phase, y, p)
        pack_rows(phase, y)
        for copy in copies[:10]:
            copy.start()
        for n in range(3):
            turn_rows(H + 8 * n, 8)
            for p in range(2 + 4 * n, 6 + 4 * n):
                pack_columns(phase, y, p)
            for copy in copies[10 + 2 * n : 12 + 2 * n]:
                copy.start()

    feat_in.wait()

    def widen(src, dst):
        def body(c, _):
            dst[pl.ds(pl.multiple_of(c * B, B), B), :] = src[c].astype(F32)
            return 0

        lax.fori_loop(0, C, body, 0, unroll=4)

    def rows_of(flat, r):
        return jnp.concatenate(
            [flat[pl.ds(R * g + r, C, stride=B), :] for g in range(RG)], axis=0
        )

    widen(feat_v, xf)

    def turn(r):
        yb[H + r, O : O + B, :] = rows_of(xf, r).T

    def turn_rows(first, count):
        for r in range(first, first + count):
            turn(r)

    w_in.wait()
    block = (row_i // C) == (col_i // C)
    for k in range(K + 1):
        one = w_v[k].astype(F32)
        wide = jnp.concatenate([one] * RG, axis=1)
        full = jnp.where(block, jnp.concatenate([wide] * RG, axis=0), 0.0)
        wb[:, k * B : (k + 1) * B] = full.astype(BF16)
        wf[:, k * B : (k + 1) * B] = full.T.astype(BF16)

    turn_rows(0, R)
    for p in range(R // 2):
        pack_columns(0, yb, p)
    pack_rows(0, yb)
    pl.semaphore_wait(barrier, 4 + (n_lon - 1) + (n_lat - 1))
    for copy in mask_copies:
        copy.start()
    first_halo = halo_copies(0)
    for copy in first_halo:
        copy.start()

    cot_in.wait()
    widen(cot_v, cf)

    lane_e = lax.broadcasted_iota(jnp.int32, (CE, B), 1)
    sm[...] = jnp.zeros_like(sm)
    sm[0, 16 : 16 + B, :] = mask_v[...].astype(F32)

    def ring(main, side, shift, edge):
        m, s = pltpu.roll(main, shift, 1), pltpu.roll(side, shift, 1)
        at = lane_e == edge
        return jnp.where(at, s, m), jnp.where(at, m, s)

    def degrees():
        here = [sm[t, 8 : 8 + CE, :] for t in range(2)]
        up = [sm[t, 7 : 7 + CE, :] for t in range(2)]
        down = [sm[t, 9 : 9 + CE, :] for t in range(2)]
        from_left = ring(here[0] + down[0], here[1] + down[1], 1, 0)
        from_right = ring(here[0] + up[0], here[1] + up[1], B - 1, B - 1)
        for t in range(2):
            degree = from_left[t] + from_right[t] + up[t] + down[t]
            vm[:, t * B : (t + 1) * B] = here[t] * jnp.maximum(degree, 1.0)
            if t == 0:
                snat[...] = jnp.sqrt(jnp.maximum(degree, 1.0)[8 : 8 + B])

    def values(p, pick):
        rows = jnp.concatenate(
            [
                jnp.broadcast_to(vm[pl.ds(8 - H + R * g + 2 * p + j, 1), :], (C, 2 * B))
                for j in range(2)
                for g in range(RG)
            ],
            axis=0,
        )
        v = lax.dot_general(pick, rows.astype(BF16), NT, preferred_element_type=F32)
        m = jnp.maximum(v, 1.0)
        rs = lax.rsqrt(m)
        return jnp.where(v > 0.5, -2.0 * rs * rs, 0.0), m * rs

    def spread(p, _):
        a, s = values(p, sel[...])
        for j in range(2):
            coef[2 * p + j] = a[:, j * B : (j + 1) * B]
            scale[2 * p + j] = s[:, j * B : (j + 1) * B]
        return 0

    def spread_sides(p, _):
        a, s = values(p, jnp.concatenate([sel[0:16, :], sel[CE - 16 :, :]], axis=0))
        for j in range(2):
            for ref, part in ((coef, a), (scale, s)):
                ref[2 * p + j, 0:16, :] = part[0:16, j * B : (j + 1) * B]
                ref[2 * p + j, CE - 16 :, :] = part[16:32, j * B : (j + 1) * B]
        return 0

    degrees()
    lax.fori_loop(3, RE // 2 - 3, spread, 0, unroll=7)

    def groups(y):
        for i in range(H):
            y[i, O : O + B, :] = pltpu.roll(y[R + i, O : O + B, :], C, 1)
            y[H + R + i, O : O + B, :] = pltpu.roll(y[H + i, O : O + B, :], B - C, 1)

    def beside(y, at, row, shift):
        return jnp.concatenate(
            [
                pltpu.roll(y[row, O - 8 : O, :], shift, 1),
                y[at, O : O + B, :],
                pltpu.roll(y[row, O + B : O + B + 8, :], shift, 1),
            ],
            axis=0,
        )

    def assemble(phase, y, ok_north, ok_south):
        for p in range(R // 2):
            a, b = lcol[phase, 0, p], lcol[phase, 1, p]
            y[H + 2 * p, O - 8 : O, :] = pltpu.roll(a, 4, 0)
            y[H + 2 * p + 1, O - 8 : O, :] = a
            y[H + 2 * p, O + B : O + B + 8, :] = b
            y[H + 2 * p + 1, O + B : O + B + 8, :] = pltpu.roll(b, 4, 0)
        for i in range(H):
            own_up = beside(y, i, R + i, C)
            far_up = pltpu.roll(lrow[phase, 0], (B - 32 * i) % B, 1) * ok_north
            y[i, O - 8 : O + B + 8, :] = jnp.where(lane_e < 32, far_up, own_up)
            own_down = beside(y, H + R + i, H + i, B - C)
            far_down = pltpu.roll(lrow[phase, 1], (96 - 32 * i) % B, 1) * ok_south
            y[H + R + i, O - 8 : O + B + 8, :] = jnp.where(
                lane_e >= 96, far_down, own_down
            )

    def keep(k, r, value):
        terms[pl.ds(pl.multiple_of(r * B, B), B), k * B : (k + 1) * B] = value.astype(BF16)

    def cells(src, dst, k, scaled, bands, rows, unroll):
        def sums(r, first, size):
            mid_ = src[r, first : first + size, :]
            low = src[r, first - 1 : first - 1 + size, :]
            high = src[r, first + 1 : first + 1 + size, :]
            return mid_ + high, low + high, mid_ + low

        def advance(r, carried, keeps):
            after = []
            for (first, size), (e0, e1, f1) in zip(bands, carried):
                e2, f2, h2 = sums(r + 1, first, size)
                total = coef[r, first - O + 8 : first - O + 8 + size, :] * (e0 + f1 + h2)
                if k == 1:
                    value = 0.5 * total
                else:
                    value = total - dst[r, first : first + size, :]
                dst[r, first : first + size, :] = value
                lo, hi = max(first, O), min(first + size, O + B)
                if keeps:
                    at = (r - H) * B + lo - O
                    if not isinstance(r, int):
                        at = pl.multiple_of(at, 8)
                    kept = value[lo - first : hi - first]
                    if scaled:
                        kept = kept * scale[r, lo - O + 8 : hi - O + 8, :]
                    terms[pl.ds(at, hi - lo), k * B : (k + 1) * B] = kept.astype(BF16)
                after.append((e1, e2, f2))
            return tuple(after)

        low, high = rows
        carried = tuple(
            (sums(low - 1, *band)[0],) + sums(low, *band)[:2] for band in bands
        )
        if unroll:
            lax.fori_loop(
                low, high, lambda r, c: advance(r, c, True), carried, unroll=unroll
            )
        else:
            for r in range(low, high):
                carried = advance(r, carried, H <= r < H + R)

    def inner_rows(k, less):
        low, high = H + k + less, H + R - k - less
        return (low, high), {30: 6, 28: 7, 26: 13, 24: 8, 22: 11, 20: 10}[high - low]

    def step_inside(src, dst, k, scaled, less):
        first, last = O + 8 * k, O + B - 8 * k
        size = (last - first) // (1 if k == K else 2)
        for at in range(first, last, size):
            cells(src, dst, k, scaled, ((at, size),), *inner_rows(k, less))

    def step_rim(src, dst, k, scaled, less):
        reach = K - k
        first, last = (O - 8, O + B + 8) if reach else (O, O + B)
        size = 48 if reach else 64
        for low in (H - reach, H + R - k - less):
            for at in range(first, last, size):
                cells(src, dst, k, scaled, ((at, size),), (low, low + K + less), 0)
        width = O + 8 * k - first
        bands = ((first, width), (last - width, width))
        cells(src, dst, k, scaled, bands, *inner_rows(k, less))

    def start_row(r, first, last):
        at = slice(first - O + 8, last - O + 8)
        value = (-0.5 * coef[r, at, :] * scale[r, at, :]) * yb[r, first:last, :]
        ya[r, first:last, :] = value
        return value * scale[r, at, :]

    def start_inner(r, _):
        keep(0, r - H, start_row(r, O, O + B))
        return 0

    groups(yb)
    lax.fori_loop(6, RE - 6, start_inner, 0, unroll=7)
    step_inside(ya, yb, 1, True, 2)
    step_inside(yb, ya, 2, True, 2)
    step_inside(ya, yb, 3, True, 2)
    step_inside(yb, ya, 4, True, 2)

    for copy in mask_copies:
        copy.wait()
    north_ok = (lat > 0).astype(F32)
    south_ok = (lat < n_lat - 1).astype(F32)
    low_lanes = lane_e[0:8] < 64
    sm[0, 8:16, :] = mrx[2] * north_ok
    sm[0, 16 + B : 24 + B, :] = mrx[3] * south_ok
    sm[1, 8:16, :] = jnp.where(low_lanes, mrx[5], mrx[4]) * north_ok
    sm[1, 16 : 16 + B, :] = jnp.concatenate(
        [mrx[1], jnp.zeros((B - 16, B), F32), mrx[0]], axis=0
    ).T
    sm[1, 16 + B : 24 + B, :] = jnp.where(low_lanes, mrx[7], mrx[6]) * south_ok
    degrees()
    for p in (0, 1, 2, 17, 18, 19):
        spread(p, 0)
    lax.fori_loop(3, RE // 2 - 3, spread_sides, 0, unroll=7)

    for copy in first_halo:
        copy.wait()
    assemble(0, yb, 1.0, 1.0)
    for r in tuple(range(6)) + tuple(range(RE - 6, RE)):
        value = start_row(r, O - 8, O + B + 8)
        if H <= r < H + R:
            keep(0, r - H, value[8 : 8 + B])

    def start_sides(r, _):
        left = start_row(r, O - 8, O + 8)
        right = start_row(r, O + B - 8, O + B + 8)
        at = pl.multiple_of((r - H) * B, B)
        terms[pl.ds(at, 8), 0:B] = left[8:16].astype(BF16)
        terms[pl.ds(at + B - 8, 8), 0:B] = right[0:8].astype(BF16)
        return 0

    lax.fori_loop(6, RE - 6, start_sides, 0, unroll=7)
    step_rim(ya, yb, 1, True, 2)
    step_rim(yb, ya, 2, True, 2)
    step_rim(ya, yb, 3, True, 2)
    step_rim(yb, ya, 4, True, 2)


    def mix(p):
        at = pl.ds(pl.multiple_of(2 * p * B, 2 * B), 2 * B)
        mixed = lax.dot_general(wf[...], terms[at, :], NT, preferred_element_type=F32)
        act = jnp.tanh(mixed)
        cot = jnp.concatenate([rows_of(cf, 2 * p), rows_of(cf, 2 * p + 1)], axis=1)
        gcat[:, at] = (cot * (1.0 - act * act)).astype(BF16)

    def turn_grad(r):
        grad = gcat[:, pl.ds(pl.multiple_of(r * B, B), B)].astype(F32)
        w = -0.5 * coef[H + r, 8 : 8 + B, :] * scale[H + r, 8 : 8 + B, :]
        ya[H + r, O : O + B, :] = w * grad.T

    def grad_rows(first, count):
        for p in range(first // 2, (first + count) // 2):
            mix(p)
        for r in range(first, first + count):
            turn_grad(r)

    second_halo = halo_copies(1)
    send_chunks(1, ya, second_halo, grad_rows)

    chunk = 8 * B
    acc = None
    for n in range(R * B // chunk):
        part = jnp.dot(
            gcat[:, n * chunk : (n + 1) * chunk],
            terms[n * chunk : (n + 1) * chunk, :],
            preferred_element_type=F32,
        )
        acc = part if acc is None else acc + part
    lane_c = lax.broadcasted_iota(jnp.int32, (C, B), 1) // C
    folded = []
    for k in range(K + 1):
        tot = None
        for g in range(RG):
            piece = acc[g * C : (g + 1) * C, k * B : (k + 1) * B]
            tot = piece if tot is None else jnp.where(lane_c == g, piece, tot)
        tot = tot + pltpu.roll(tot, 64, 1)
        tot = tot + pltpu.roll(tot, 32, 1)
        folded.append(tot)
    head = folded[0]
    for k in range(1, K):
        head = jnp.where(lane_c == k, folded[k], head)
    tail = folded[K][0:8]
    for g in range(1, RG):
        tail = jnp.where(lane_c[0:8] == g, folded[K][8 * g : 8 * g + 8], tail)
    grid_cells = n_lat * n_lon * B * B
    own[0, 0:C, :] = head * (1.0 / math.sqrt(grid_cells))
    own[0, C : C + 8, :] = tail * (1.0 / math.sqrt(grid_cells))

    def lon_copy(off):
        return remote(
            own.at[0], ar1.at[lon], ar1_send.at[off], ar1_recv.at[lon],
            lat, lax.rem(lon + off, n_lon),
        )

    def lon_wait(off):
        q = lax.rem(lon + n_lon - off, n_lon)
        return remote(own.at[0], ar1.at[q], ar1_send.at[off], ar1_recv.at[q], lat, q)

    def lat_copy(off):
        return remote(
            own.at[1], ar2.at[lat], ar2_send.at[off], ar2_recv.at[lat],
            lax.rem(lat + off, n_lat), lon,
        )

    def lat_wait(off):
        q = lax.rem(lat + n_lat - off, n_lat)
        return remote(own.at[1], ar2.at[q], ar2_send.at[off], ar2_recv.at[q], q, lon)

    def run(count, act):
        def body(off, _):
            act(off)
            return 0

        lax.fori_loop(1, count, body, 0)

    run(n_lon, lambda off: lon_copy(off).start())
    ar1[lon] = own[0]

    def keep_grad(r, _):
        keep(0, r, ya[H + r, O : O + B, :])
        return 0

    lax.fori_loop(0, R, keep_grad, 0, unroll=4)
    groups(ya)
    step_inside(ya, yb, 1, False, 0)
    step_inside(yb, ya, 2, False, 0)
    step_inside(ya, yb, 3, False, 0)
    step_inside(yb, ya, 4, False, 0)
    for copy in second_halo:
        copy.wait()
    assemble(1, ya, north_ok, south_ok)

    step_rim(ya, yb, 1, False, 0)

    run(n_lon, lambda off: lon_wait(off).wait())
    total = ar1[0]
    for q in range(1, n_lon):
        total = total + ar1[q]
    own[1] = total
    run(n_lat, lambda off: lat_copy(off).start())
    ar2[lat] = total

    step_rim(yb, ya, 2, False, 0)
    step_rim(ya, yb, 3, False, 0)
    step_rim(yb, ya, 4, False, 0)

    def finish(p, _):
        t = terms[pl.ds(pl.multiple_of(2 * p * B, 2 * B), 2 * B), :]
        res = lax.dot_general(wb[...], t, NT, preferred_element_type=F32)
        for j in range(2):
            for g in range(RG):
                row = R * g + 2 * p + j
                s = jnp.broadcast_to(snat[pl.ds(row, 1), :], (C, B))
                part = res[g * C : (g + 1) * C, j * B : (j + 1) * B]
                xf[pl.ds(row, C, stride=B), :] = part * s
        return 0

    lax.fori_loop(0, R // 2, finish, 0, unroll=4)

    for c in range(C):
        out_v[c] = xf[c * B : (c + 1) * B, :].astype(BF16)

    run(n_lat, lambda off: lat_wait(off).wait())
    total = ar2[0]
    for q in range(1, n_lat):
        total = total + ar2[q]
    sum_ref[...] = total


def close(out_v, sum_ref, out_hbm, wg_ref, out_sem):
    copy = pltpu.make_async_copy(out_v, out_hbm, out_sem)
    copy.start()
    total = sum_ref[...]
    flat = total[0:C].T
    for k in range(K):
        wg_ref[k] = flat[k * C : (k + 1) * C, :]
    last = total[C : C + 8]
    last = jnp.concatenate(
        [last if g == 0 else pltpu.roll(last, B - C * g, 1) for g in range(RG)], axis=0
    )
    wg_ref[K] = last.T[0:C, :]
    copy.wait()


def solution(mesh):
    n_lat, n_lon = mesh.shape["lat"], mesh.shape["lon"]
    hbm = pl.BlockSpec(memory_space=pltpu.HBM)
    sem = pltpu.SemaphoreType.DMA

    def local(features, cotangent, sea_mask, weights):
        vmem = pl.BlockSpec(memory_space=pltpu.VMEM)
        carried = (
            pltpu.VMEM((C, B, B), BF16),
            pltpu.VMEM((C + 8, B), F32),
        )
        carried = pl.pallas_call(
            functools.partial(kernel, n_lat, n_lon),
            out_shape=carried,
            in_specs=[hbm] * 4,
            out_specs=(vmem,) * 2,
            scratch_shapes=[
                pltpu.VMEM((C, B, B), BF16),
                pltpu.VMEM((C, B, B), BF16),
                pltpu.VMEM((B, B), jnp.int32),
                pltpu.VMEM((K + 1, C, C), BF16),
                pltpu.VMEM((C * B, B), F32),
                pltpu.VMEM((C * B, B), F32),
                pltpu.VMEM((RE, CP, B), F32),
                pltpu.VMEM((RE, CP, B), F32),
                pltpu.VMEM((RE, CE, B), F32),
                pltpu.VMEM((RE, CE, B), F32),
                pltpu.VMEM((R * B, (K + 1) * B), BF16),
                pltpu.VMEM((B, R * B), BF16),
                pltpu.VMEM((4, 8, B), F32),
                pltpu.VMEM((8, 8, B), F32),
                pltpu.VMEM((2, CP, B), F32),
                pltpu.VMEM((CE, 2 * B), F32),
                pltpu.VMEM((B, B), F32),
                pltpu.VMEM((B, (K + 1) * B), BF16),
                pltpu.VMEM((B, (K + 1) * B), BF16),
                pltpu.VMEM((CE, 2 * B), BF16),
                pltpu.VMEM((2, 2, B, B), F32),
                pltpu.VMEM((2, 2, R // 2, 8, B), F32),
                pltpu.VMEM((2, 2, CE, B), F32),
                pltpu.VMEM((2, 2, R // 2, 8, B), F32),
                pltpu.VMEM((2, C + 8, B), F32),
                pltpu.VMEM((n_lon, C + 8, B), F32),
                pltpu.VMEM((n_lat, C + 8, B), F32),
                sem((4,)), sem((8,)), sem((8,)), sem((2, 16)), sem((2, 16)),
                sem((n_lon,)), sem((n_lon,)), sem((n_lat,)), sem((n_lat,)),
            ],
            compiler_params=pltpu.CompilerParams(
                collective_id=0, has_side_effects=True, vmem_limit_bytes=62 << 20
            ),
        )(features, cotangent, sea_mask, weights)
        return pl.pallas_call(
            close,
            out_shape=(
                jax.ShapeDtypeStruct((C, B, B), BF16),
                jax.ShapeDtypeStruct((K + 1, C, C), F32),
            ),
            in_specs=[vmem] * 2,
            out_specs=(hbm, vmem),
            scratch_shapes=[sem(())],
            compiler_params=pltpu.CompilerParams(vmem_limit_bytes=4 << 20),
        )(*carried)

    placed = (P(None, "lat", "lon"), P(None, "lat", "lon"), P("lat", "lon"), P())
    return jax.shard_map(
        local, mesh=mesh, in_specs=placed, out_specs=(P(None, "lat", "lon"), P()), check_vma=False
    )
```
